32 devices in a mesh: row: 8 (over z, y), col: 4 (over x, core).
Axes of the slice: x: 2, y: 2, z: 4, core: 2. Of those that a mesh axis runs over, the one named last changes fastest.
Arguments:
- anc_inverse: float32 [20480, 20480], P('row', 'col'), may hold values from -6 to 6
- l_store: float32 [4, 20480, 256], P('col', 'row'), may hold values from -0.0546875 to 0.0546875
- diag_inv: float32 [4, 256, 256], P('col'), may hold values from -6 to 6
- block_lists: int32 [4, 96], replicated, may hold values from 0 to 159, as said below
- block_counts: int32 [4], replicated, may hold values from 48 to 96, as said below
- sibling_columns: int32 [4], replicated, may hold values from 0 to 3, as said below
Outputs:
- upper_out: float32 [4, 256, 20480], P(None, 'row', 'col')
- lower_out: float32 [4, 20480, 256], P('col', 'row')
- diag_out: float32 [4, 256, 256], P('col')
The draws below stay inside these ranges and needn't reach their ends.
Inputs may be any that keep to these rules, and one draw needn't show every extreme that they name: `block_lists`: in each sibling's row the entries are distinct block indices; entries at positions from block_counts onward are ignored. `block_counts`: some sibling uses all 96 entries. `sibling_columns`: distinct columns for distinct siblings.
All inputs are finite; a program needn't handle non-finite values.
Results may differ from the reference program's by a relative error of at most 0.00011.
Values sent between devices are 32-bit elements; how exact they have to be, the bound alone decides.
A program may use at most 128 MiB of HBM per device.

```python
import jax
import jax.numpy as jnp
from jax import lax

BLK = 128
NBLK = 160
W = 256
SIB = 4
KMAX = 96
S = 20480
N_COL = 4


def draw_block_lists(key, part):
    sib_keys = jax.random.split(jax.random.fold_in(key, 3), SIB)
    picked = jax.vmap(lambda one_key: jax.random.permutation(one_key, NBLK)[:KMAX])(sib_keys)
    return picked.astype(jnp.int32)


def draw_block_counts(key, part):
    counts = jax.random.randint(jax.random.fold_in(key, 7), (SIB,), KMAX // 2, KMAX + 1)
    pick_one = jax.random.randint(jax.random.fold_in(key, 8), (), 0, SIB)
    counts = jnp.where(jnp.arange(SIB) == pick_one, KMAX, counts)
    return counts.astype(jnp.int32)


def draw_sibling_columns(key, part):
    column_order = jax.random.permutation(jax.random.fold_in(key, 11), N_COL)
    return column_order[:SIB].astype(jnp.int32)


def block_levels(key, dims, cuts, smallest, high):
    def one(axis_at, parts):
        draws = jax.random.uniform(jax.random.fold_in(jax.random.fold_in(key, 6), axis_at), (parts,), jnp.float32, smallest / len(cuts), high / len(cuts))
        return jnp.repeat(jnp.exp(draws), dims[axis_at] // parts).reshape((-1,) + (1,) * (len(dims) - axis_at - 1))

    level = one(*cuts[0])
    for cut in cuts[1:]:
        level = level * one(*cut)
    return level


def gaussian(own_key, extent, scale, limit, cuts=(), kind=jnp.bfloat16):
    result = scale * jax.random.normal(own_key, extent, jnp.float32)
    if cuts:
        result = result * block_levels(own_key, extent, cuts, -0.22, 0.18)
    return jnp.clip(result, -limit, limit).astype(kind)


def setup_inputs(seed: int = 0) -> dict:
    streams_of = jax.random.split(jax.random.key(seed), 7)
    anc_inverse = gaussian(streams_of[0], (S, S), 1.0, 6.0, ((0, 8), (1, 4)), jnp.float32)
    l_store = gaussian(streams_of[1], (N_COL, S, W), (KMAX * BLK) ** -0.5, 0.0546875, ((0, 4), (1, 8)), jnp.float32)
    diag_inv = gaussian(streams_of[2], (N_COL, W, W), 1.0, 6.0, ((0, 4),), jnp.float32)
    block_lists = draw_block_lists(jax.random.fold_in(streams_of[6], 71), 0)
    block_counts = draw_block_counts(jax.random.fold_in(streams_of[6], 71), 0)
    sibling_columns = draw_sibling_columns(jax.random.fold_in(streams_of[6], 71), 0)
    return dict(anc_inverse=anc_inverse, l_store=l_store, diag_inv=diag_inv, block_lists=block_lists, block_counts=block_counts, sibling_columns=sibling_columns)


def member_mask(block_lists, block_counts):
    block_ids = jnp.arange(NBLK, dtype=jnp.int32)
    valid_entry = jnp.arange(KMAX, dtype=jnp.int32)[None, :] < block_counts[:, None]
    entry_hits = (block_lists[:, :, None] == block_ids[None, None, :]) & valid_entry[:, :, None]
    return jnp.repeat(jnp.any(entry_hits, axis=1).astype(jnp.float32), BLK, axis=1)


def reference(anc_inverse, l_store, diag_inv, block_lists, block_counts, sibling_columns):
    listed = member_mask(block_lists, block_counts)
    panels = l_store[sibling_columns.astype(jnp.int32)] * listed[:, :, None]
    upper_out = -jnp.einsum("jsw,st->jwt", panels, anc_inverse, precision=lax.Precision.HIGHEST, preferred_element_type=jnp.float32) * listed[:, None, :]
    inner_sum = jnp.einsum("jws,jsv->jwv", upper_out, panels, precision=lax.Precision.HIGHEST, preferred_element_type=jnp.float32)
    chosen = (sibling_columns[:, None] == jnp.arange(N_COL, dtype=jnp.int32)[None, :]).astype(jnp.float32)
    present = jnp.sum(chosen, axis=0)
    lower_out = jnp.einsum("jc,jws->csw", chosen, upper_out, precision=lax.Precision.HIGHEST, preferred_element_type=jnp.float32)
    diag_out = present[:, None, None] * diag_inv - jnp.einsum("jc,jwv->cwv", chosen, inner_sum, precision=lax.Precision.HIGHEST, preferred_element_type=jnp.float32)
    return upper_out, lower_out, diag_out
```

```python
import functools

import jax
import jax.numpy as jnp
from jax import lax
from jax.experimental import pallas as pl
from jax.experimental.pallas import tpu as pltpu
from jax.sharding import PartitionSpec as P

BLK = 128
MESH = pl.DeviceIdType.MESH


def listed_table(block_lists, block_counts, block_total):
    block_ids = jnp.arange(block_total, dtype=jnp.int32)
    valid_entry = jnp.arange(block_lists.shape[1], dtype=jnp.int32)[None, :] < block_counts[:, None]
    entry_hits = (block_lists[:, :, None] == block_ids[None, None, :]) & valid_entry[:, :, None]
    return jnp.any(entry_hits, axis=1)


def product_kernel(siblings, tile_blocks, col_blocks, row_blocks,
                   slot_ref, rows_ref, count_ref, column_ref,
                   a_ref, panels_ref, out_ref, a_high, a_low, p_high, p_low, acc):
    stripe = pl.program_id(0)
    width = out_ref.shape[0]

    @pl.when(stripe == 0)
    def _():
        for sibling in range(siblings):
            column = column_ref[sibling]

            @pl.loop(0, row_blocks)
            def _(block):
                lanes = pl.ds(pl.multiple_of(block * BLK, BLK), BLK)
                value = panels_ref[pl.ds(pl.multiple_of(column * width, width), width), lanes]
                high = value.astype(jnp.bfloat16)
                p_high[sibling, block] = high
                p_low[sibling, block] = (value - high.astype(jnp.float32)).astype(jnp.bfloat16)

            p_high[sibling, row_blocks] = jnp.zeros(p_high.shape[2:], jnp.bfloat16)
            p_low[sibling, row_blocks] = jnp.zeros(p_low.shape[2:], jnp.bfloat16)

    @pl.loop(0, row_blocks)
    def _(block):
        rows = pl.ds(pl.multiple_of(block * BLK, BLK), BLK)
        value = a_ref[rows, :]
        high = value.astype(jnp.bfloat16)
        a_high[block] = high
        a_low[block] = (value - high.astype(jnp.float32)).astype(jnp.bfloat16)

    for sibling in range(siblings):
        acc[...] = jnp.zeros_like(acc)
        base = sibling * (row_blocks + 1)

        @pl.loop(0, (count_ref[sibling] + 1) // 2)
        def _(pair):
            first = rows_ref[base + 2 * pair]
            second = rows_ref[base + 2 * pair + 1]
            second_a = jnp.minimum(second, row_blocks - 1)
            ph = [p_high[sibling, first], p_high[sibling, second]]
            plo = [p_low[sibling, first], p_low[sibling, second]]
            ah = [a_high[first], a_high[second_a]]
            al = [a_low[first], a_low[second_a]]
            left = jnp.concatenate(ph + ph + plo, axis=1)
            right = jnp.concatenate(ah + al + ah, axis=0)
            acc[...] += jnp.dot(left, right, preferred_element_type=jnp.float32)

        for block in range(tile_blocks):
            slot = slot_ref[sibling * col_blocks + stripe * tile_blocks + block]

            @pl.when(slot >= 0)
            def _():
                out_ref[:, pl.ds(pl.multiple_of(slot * BLK, BLK), BLK)] = (
                    -acc[:, block * BLK:(block + 1) * BLK]
                )


def product(slot, rows, counts, columns, anc, panels, width, cap):
    siblings = counts.shape[0]
    depth, cells = anc.shape
    row_blocks, col_blocks = depth // BLK, cells // BLK
    tile_blocks = next(n for n in (4, 2, 1) if col_blocks % n == 0)
    tile = tile_blocks * BLK
    return pl.pallas_call(
        functools.partial(product_kernel, siblings, tile_blocks, col_blocks, row_blocks),
        out_shape=jax.ShapeDtypeStruct((width, cap * BLK), jnp.float32),
        grid_spec=pltpu.PrefetchScalarGridSpec(
            num_scalar_prefetch=4,
            grid=(col_blocks // tile_blocks,),
            in_specs=[
                pl.BlockSpec((depth, tile), lambda i, *_: (0, i)),
                pl.BlockSpec(panels.shape, lambda i, *_: (0, 0), pipeline_mode=pl.Buffered(1)),
            ],
            out_specs=pl.BlockSpec((width, cap * BLK), lambda i, *_: (0, 0), pipeline_mode=pl.Buffered(1)),
            scratch_shapes=[
                pltpu.VMEM((row_blocks, BLK, tile), jnp.bfloat16),
                pltpu.VMEM((row_blocks, BLK, tile), jnp.bfloat16),
                pltpu.VMEM((siblings, row_blocks + 1, width, BLK), jnp.bfloat16),
                pltpu.VMEM((siblings, row_blocks + 1, width, BLK), jnp.bfloat16),
                pltpu.VMEM((width, tile), jnp.float32),
            ],
        ),
        compiler_params=pltpu.CompilerParams(
            dimension_semantics=("arbitrary",), vmem_limit_bytes=63 * 1024 * 1000
        ),
    )(slot, rows, counts, columns, anc, panels)


def flip_kernel(value_ref, out_ref):
    out_ref[...] = value_ref[...].T


def flipped(value):
    depth, width = value.shape
    step = next(n for n in (512, 256, 128) if depth % n == 0)
    return pl.pallas_call(
        flip_kernel,
        out_shape=jax.ShapeDtypeStruct((width, depth), value.dtype),
        grid=(depth // step,),
        in_specs=[pl.BlockSpec((step, width), lambda i: (i, 0))],
        out_specs=pl.BlockSpec((width, step), lambda i: (0, i)),
    )(value)


def expand_kernel(siblings, col_count, col_blocks, slot_ref, owner_ref, compact_ref, upper_ref, slots_ref):
    @pl.loop(0, col_blocks)
    def _(block):
        lanes = pl.ds(pl.multiple_of(block * BLK, BLK), BLK)
        for sibling in range(siblings):
            slot = slot_ref[sibling * col_blocks + block]
            at = pl.ds(pl.multiple_of(jnp.maximum(slot, 0) * BLK, BLK), BLK)
            value = compact_ref[:, at]
            upper_ref[sibling, :, lanes] = jnp.where(slot >= 0, value, jnp.zeros_like(value))

    for column in range(col_count):
        sibling = owner_ref[column]
        value = upper_ref[jnp.maximum(sibling, 0)]
        slots_ref[column] = jnp.where(sibling >= 0, value, jnp.zeros_like(value))


def expand(slot, owner, compact, siblings, col_blocks):
    col_count = owner.shape[0]
    rows = compact.shape[0]
    return pl.pallas_call(
        functools.partial(expand_kernel, siblings, col_count, col_blocks),
        out_shape=(
            jax.ShapeDtypeStruct((siblings, rows, col_blocks * BLK), jnp.float32),
            jax.ShapeDtypeStruct((col_count, rows, col_blocks * BLK), jnp.float32),
        ),
        in_specs=[pl.BlockSpec(memory_space=pltpu.SMEM)] * 2 + [pl.BlockSpec(memory_space=pltpu.VMEM)],
        out_specs=(pl.BlockSpec(memory_space=pltpu.VMEM),) * 2,
    )(slot, owner, compact)


def reduce_kernel(line, flat_first, chunks,
                  partial_ref, out_ref,
                  pair_buf, up_buf, down_buf, flat_up, flat_down, flat_sum, flat_pair,
                  pair_send, pair_recv, up_send, up_recv, down_send, down_recv, flat_send, flat_recv):
    r, c = lax.axis_index("row"), lax.axis_index("col")
    z, y = r // 2, lax.rem(r, 2)
    other = 1 - y
    width = out_ref.shape[1] // chunks
    last = line - 1
    late = chunks - flat_first

    def lanes(chunk):
        return pl.ds(pl.multiple_of(chunk * width, width), width)

    barrier = pltpu.get_barrier_semaphore()
    pl.semaphore_signal(barrier, inc=1, device_id=(z * 2 + other, c), device_id_type=MESH)

    @pl.when(z > 0)
    def _():
        pl.semaphore_signal(barrier, inc=1, device_id=(r - 2, c), device_id_type=MESH)

    @pl.when(z < last)
    def _():
        pl.semaphore_signal(barrier, inc=1, device_id=(r + 2, c), device_id_type=MESH)

    pl.semaphore_wait(barrier, 1 + (z > 0).astype(jnp.int32) + (z < last).astype(jnp.int32))

    def pair_copy(k):
        return pltpu.make_async_remote_copy(
            src_ref=partial_ref.at[:, other, :, lanes(k + flat_first)],
            dst_ref=pair_buf.at[k],
            send_sem=pair_send.at[k],
            recv_sem=pair_recv.at[k],
            device_id=(z * 2 + other, c),
            device_id_type=MESH,
        )

    def flat_copy(k):
        return pltpu.make_async_remote_copy(
            src_ref=flat_sum.at[k, other],
            dst_ref=flat_pair.at[k],
            send_sem=flat_send.at[k],
            recv_sem=flat_recv.at[k],
            device_id=(z * 2 + other, c),
            device_id_type=MESH,
        )

    def up_copy(buf, k, slot, at):
        return pltpu.make_async_remote_copy(
            src_ref=buf.at[k, pl.ds(at, last - at)],
            dst_ref=buf.at[k, pl.ds(at, last - at)],
            send_sem=up_send.at[slot],
            recv_sem=up_recv.at[slot],
            device_id=(r + 2, c),
            device_id_type=MESH,
        )

    def down_copy(buf, k, slot, at):
        return pltpu.make_async_remote_copy(
            src_ref=buf.at[k, pl.ds(0, at)],
            dst_ref=buf.at[k, pl.ds(0, at)],
            send_sem=down_send.at[slot],
            recv_sem=down_recv.at[slot],
            device_id=(r - 2, c),
            device_id_type=MESH,
        )

    def pass_up(buf, k, slot, own):
        for at in range(line):
            @pl.when(z == at)
            def _():
                if at > 0:
                    up_copy(buf, k, slot, at - 1).wait_recv()
                for place in range(at + 1, line):
                    if at > 0:
                        buf[k, place - 1] = buf[k, place - 1] + own(place)
                    else:
                        buf[k, place - 1] = own(place)
                if at < last:
                    up_copy(buf, k, slot, at).start()

    def pass_down(up, down, k, slot, own, finish):
        for at in range(line):
            @pl.when(z == at)
            def _():
                if at < last:
                    down_copy(down, k, slot, at + 1).wait_recv()
                for place in range(at):
                    if at < last:
                        down[k, place] = down[k, place] + own(place)
                    else:
                        down[k, place] = own(place)
                if at > 0:
                    down_copy(down, k, slot, at).start()
                value = own(at)
                if at > 0:
                    value = value + up[k, at - 1]
                if at < last:
                    value = value + down[k, at]
                finish(value)

    def flat_own(k):
        return lambda place: partial_ref[place, :, :, lanes(k)]

    def pair_own(k):
        return lambda place: pair_buf[k, place]

    def flat_up_step(k):
        pass_up(flat_up, k, k, flat_own(k))

    def flat_down_step(k):
        def keep(value):
            flat_sum[k] = value

        pass_down(flat_up, flat_down, k, k, flat_own(k), keep)
        flat_copy(k).start()

    def pair_up_step(k):
        pair_copy(k).wait_recv()
        for place in range(line):
            pair_buf[k, place] = pair_buf[k, place] + partial_ref[place, y, :, lanes(k + flat_first)]
        pass_up(up_buf, k, k + flat_first, pair_own(k))

    def pair_down_step(k):
        def keep(value):
            out_ref[:, lanes(k + flat_first)] = value

        pass_down(up_buf, down_buf, k, k + flat_first, pair_own(k), keep)

    @pl.loop(0, late)
    def _(k):
        pair_copy(k).start()

    @pl.loop(0, flat_first)
    def _(k):
        flat_up_step(k)

    @pl.loop(0, flat_first)
    def _(k):
        pair_up_step(k)
        flat_down_step(k)

    @pl.loop(flat_first, late)
    def _(k):
        pair_up_step(k)
        pair_down_step(k - flat_first)

    @pl.loop(late - flat_first, late)
    def _(k):
        pair_down_step(k)

    @pl.loop(0, flat_first)
    def _(k):
        flat_copy(k).wait_recv()
        out_ref[:, lanes(k)] = flat_sum[k, y] + flat_pair[k]

    @pl.loop(0, late)
    def _(k):
        pair_copy(k).wait_send()

    @pl.loop(0, flat_first)
    def _(k):
        flat_copy(k).wait_send()

    for at in range(line):
        @pl.when(z == at)
        def _():
            for buf, start, stop, shift in ((flat_up, 0, flat_first, 0), (up_buf, 0, late, flat_first)):
                if at < last:
                    @pl.loop(start, stop)
                    def _(k):
                        up_copy(buf, k, k + shift, at).wait_send()
            for buf, start, stop, shift in ((flat_down, 0, flat_first, 0), (down_buf, 0, late, flat_first)):
                if at > 0:
                    @pl.loop(start, stop)
                    def _(k):
                        down_copy(buf, k, k + shift, at).wait_send()


def reduce_rows(value, row_count, chunks, collective):
    width, columns = value.shape
    line, slice_rows = row_count // 2, width // row_count
    lanes = columns // chunks
    flat_first = (chunks + 3) // 6
    late = chunks - flat_first
    vmem = pl.BlockSpec(memory_space=pltpu.VMEM)
    dma = pltpu.SemaphoreType.DMA
    return pl.pallas_call(
        functools.partial(reduce_kernel, line, flat_first, chunks),
        out_shape=jax.ShapeDtypeStruct((slice_rows, columns), jnp.float32),
        in_specs=[vmem],
        out_specs=vmem,
        scratch_shapes=[
            pltpu.VMEM((late, line, slice_rows, lanes), jnp.float32),
            pltpu.VMEM((late, line - 1, slice_rows, lanes), jnp.float32),
            pltpu.VMEM((late, line - 1, slice_rows, lanes), jnp.float32),
            pltpu.VMEM((flat_first, line - 1, 2, slice_rows, lanes), jnp.float32),
            pltpu.VMEM((flat_first, line - 1, 2, slice_rows, lanes), jnp.float32),
            pltpu.VMEM((flat_first, 2, slice_rows, lanes), jnp.float32),
            pltpu.VMEM((flat_first, slice_rows, lanes), jnp.float32),
            dma((late,)),
            dma((late,)),
            dma((chunks,)),
            dma((chunks,)),
            dma((chunks,)),
            dma((chunks,)),
            dma((flat_first,)),
            dma((flat_first,)),
        ],
        compiler_params=pltpu.CompilerParams(
            collective_id=collective, has_side_effects=True, vmem_limit_bytes=63 * 1024 * 1000
        ),
    )(value.reshape(line, 2, slice_rows, columns))


def finish_kernel(row_count, col_count,
                  slots_ref, own_ref, base_ref, lower_ref, diag_ref,
                  stage, picked, inner, part, reduced, total,
                  stage_send, stage_recv, send_sem, recv_sem, part_send, part_recv, total_send, total_recv):
    r, c = lax.axis_index("row"), lax.axis_index("col")
    ratio = row_count // col_count
    slice_rows, cells = picked.shape[1], picked.shape[2]

    barrier = pltpu.get_barrier_semaphore()
    for peer in range(row_count):
        @pl.when(peer != r)
        def _():
            pl.semaphore_signal(barrier, inc=1, device_id=(peer, c), device_id_type=MESH)
    for peer in range(col_count):
        @pl.when(peer != c)
        def _():
            pl.semaphore_signal(barrier, inc=1, device_id=(r, peer), device_id_type=MESH)
    pl.semaphore_wait(barrier, row_count + col_count - 2)

    def near(offset):
        pair = lax.rem(c // 2 + offset // 2, col_count // 2)
        return pair * 2 + lax.rem(lax.rem(c, 2) + offset % 2, 2)

    def column_copy(target):
        return pltpu.make_async_remote_copy(
            src_ref=slots_ref.at[target],
            dst_ref=stage.at[c],
            send_sem=stage_send.at[target],
            recv_sem=stage_recv.at[c],
            device_id=(r, target),
            device_id_type=MESH,
        )

    def column_arrived(source):
        return pltpu.make_async_remote_copy(
            src_ref=slots_ref.at[source],
            dst_ref=stage.at[source],
            send_sem=stage_send.at[source],
            recv_sem=stage_recv.at[source],
            device_id=(r, source),
            device_id_type=MESH,
        )

    def row_copy(held, source, k):
        target = source * ratio + k
        return pltpu.make_async_remote_copy(
            src_ref=held.at[source, :, pl.ds(k * cells, cells)],
            dst_ref=picked.at[r],
            send_sem=send_sem.at[target],
            recv_sem=recv_sem.at[r],
            device_id=(target, c),
            device_id_type=MESH,
        )

    def row_local(held, source, k):
        return pltpu.make_async_copy(
            held.at[source, :, pl.ds(k * cells, cells)], picked.at[r], recv_sem.at[r]
        )

    def row_arrived(source):
        return pltpu.make_async_remote_copy(
            src_ref=picked.at[source],
            dst_ref=picked.at[source],
            send_sem=send_sem.at[source],
            recv_sem=recv_sem.at[source],
            device_id=(source, c),
            device_id_type=MESH,
        )

    for offset in range(2, col_count):
        column_copy(near(offset)).start()
    column_copy(near(1)).start()
    for offset in range(col_count):
        source = near(offset)
        held = stage if offset else slots_ref
        if offset:
            column_arrived(source).wait_recv()
        for k in range(ratio):
            @pl.when(source * ratio + k == r)
            def _():
                row_local(held, source, k).start()

            @pl.when(source * ratio + k != r)
            def _():
                row_copy(held, source, k).start()

    for offset in range(col_count):
        source = near(offset)
        held = stage if offset else slots_ref
        for k in range(ratio):
            @pl.when(source * ratio + k == r)
            def _():
                row_local(held, source, k).wait()
    for source in range(row_count):
        @pl.when(source != r)
        def _():
            row_arrived(source).wait_recv()

    step = 256 if cells % 256 == 0 else BLK
    inner[...] = jnp.zeros_like(inner)

    @pl.loop(0, cells // step)
    def _(i):
        at = pl.ds(pl.multiple_of(i * step, step), step)
        block = picked[:, :, at].reshape(row_count * slice_rows, step)
        inner[...] += jnp.dot(
            block, own_ref[at, :], precision=lax.Precision.HIGHEST, preferred_element_type=jnp.float32
        )

    def part_copy(peer):
        return pltpu.make_async_remote_copy(
            src_ref=inner.at[pl.ds(peer * slice_rows, slice_rows), :],
            dst_ref=part.at[r],
            send_sem=part_send.at[peer],
            recv_sem=part_recv.at[r],
            device_id=(peer, c),
            device_id_type=MESH,
        )

    def part_arrived(peer):
        return pltpu.make_async_remote_copy(
            src_ref=inner.at[pl.ds(0, slice_rows), :],
            dst_ref=part.at[peer],
            send_sem=part_send.at[peer],
            recv_sem=part_recv.at[peer],
            device_id=(peer, c),
            device_id_type=MESH,
        )

    def total_copy(peer):
        return pltpu.make_async_remote_copy(
            src_ref=reduced,
            dst_ref=total.at[r],
            send_sem=total_send.at[peer],
            recv_sem=total_recv.at[r],
            device_id=(peer, c),
            device_id_type=MESH,
        )

    def total_arrived(peer):
        return pltpu.make_async_remote_copy(
            src_ref=reduced,
            dst_ref=total.at[peer],
            send_sem=total_send.at[peer],
            recv_sem=total_recv.at[peer],
            device_id=(peer, c),
            device_id_type=MESH,
        )

    def peers(action):
        for peer in range(row_count):
            @pl.when(peer != r)
            def _():
                action(peer)

    peers(lambda peer: part_copy(peer).start())
    peers(lambda peer: part_arrived(peer).wait_recv())
    mine = inner[pl.ds(pl.multiple_of(r * slice_rows, slice_rows), slice_rows), :]
    for peer in range(row_count):
        @pl.when(peer == r)
        def _():
            part[peer] = mine
    value = part[0]
    for peer in range(1, row_count):
        value = value + part[peer]
    reduced[...] = value
    peers(lambda peer: total_copy(peer).start())

    @pl.loop(0, cells // step)
    def _(i):
        at = pl.ds(pl.multiple_of(i * step, step), step)
        block = picked[:, :, at].reshape(row_count * slice_rows, step)
        lower_ref[at, :] = block.T

    peers(lambda peer: total_arrived(peer).wait_recv())
    for peer in range(row_count):
        @pl.when(peer == r)
        def _():
            total[peer] = reduced[...]
    diag_ref[...] = base_ref[...] - total[...].reshape(diag_ref.shape)

    for offset in range(col_count):
        source = near(offset)
        held = stage if offset else slots_ref
        if offset:
            column_copy(source).wait_send()
        for k in range(ratio):
            @pl.when(source * ratio + k != r)
            def _():
                row_copy(held, source, k).wait_send()
    peers(lambda peer: part_copy(peer).wait_send())
    peers(lambda peer: total_copy(peer).wait_send())


def finish(slots, own, base, row_count):
    col_count, slice_rows, _ = slots.shape
    cells, width = own.shape
    vmem = pl.BlockSpec(memory_space=pltpu.VMEM)
    dma = pltpu.SemaphoreType.DMA
    return pl.pallas_call(
        functools.partial(finish_kernel, row_count, col_count),
        out_shape=(
            jax.ShapeDtypeStruct((cells, width), jnp.float32),
            jax.ShapeDtypeStruct((width, width), jnp.float32),
        ),
        in_specs=[vmem] * 3,
        out_specs=(vmem, vmem),
        scratch_shapes=[
            pltpu.VMEM(slots.shape, jnp.float32),
            pltpu.VMEM((row_count, slice_rows, cells), jnp.float32),
            pltpu.VMEM((width, width), jnp.float32),
            pltpu.VMEM((row_count, slice_rows, width), jnp.float32),
            pltpu.VMEM((slice_rows, width), jnp.float32),
            pltpu.VMEM((row_count, slice_rows, width), jnp.float32),
            dma((col_count,)),
            dma((col_count,)),
            dma((row_count,)),
            dma((row_count,)),
            dma((row_count,)),
            dma((row_count,)),
            dma((row_count,)),
            dma((row_count,)),
        ],
        compiler_params=pltpu.CompilerParams(collective_id=0, has_side_effects=True),
    )(slots, own, base)


def per_device(anc_inverse, l_store, diag_inv, block_lists, block_counts, sibling_columns):
    siblings = block_lists.shape[0]
    row_count, col_count = lax.axis_size("row"), lax.axis_size("col")
    r, c = lax.axis_index("row"), lax.axis_index("col")
    row_blocks, col_blocks = anc_inverse.shape[0] // BLK, anc_inverse.shape[1] // BLK
    panels = lax.all_gather(flipped(l_store[0]), "col", tiled=True)

    table = listed_table(block_lists, block_counts, row_blocks * row_count)
    row_listed = lax.dynamic_slice_in_dim(table, r * row_blocks, row_blocks, axis=1)
    col_listed = lax.dynamic_slice_in_dim(table, c * col_blocks, col_blocks, axis=1)
    row_ints = row_listed.astype(jnp.int32)
    counts = jnp.sum(row_ints, axis=1)
    place = jnp.cumsum(row_ints, axis=1) - 1
    ids = jnp.arange(row_blocks, dtype=jnp.int32)
    entry = jnp.arange(row_blocks + 1, dtype=jnp.int32)
    hits = row_listed[:, :, None] & (place[:, :, None] == entry[None, None, :])
    rows = jnp.sum(jnp.where(hits, ids[None, :, None], 0), axis=1)
    rows = jnp.where(entry[None, :] < counts[:, None], rows, row_blocks).astype(jnp.int32).reshape(-1)

    flat = col_listed.reshape(-1)
    slot = jnp.where(flat, jnp.cumsum(flat.astype(jnp.int32)) - 1, -1).astype(jnp.int32)
    per_column = jnp.sum(table.reshape(siblings, col_count, col_blocks).astype(jnp.int32), axis=(0, 2))
    needed = jnp.max(per_column)
    slots_all = siblings * col_blocks
    grain = -(-slots_all // 40)
    caps = [grain * n for n in (19, 21, 23, 25, 28, 32, 40)]
    level = jnp.sum((needed > jnp.array(caps[:-1], jnp.int32)).astype(jnp.int32))

    match = sibling_columns[:, None] == jnp.arange(col_count, dtype=jnp.int32)[None, :]
    owner = jnp.max(
        jnp.where(match, jnp.arange(siblings, dtype=jnp.int32)[:, None], -1), axis=0
    ).astype(jnp.int32)
    mine = sibling_columns == c
    own_listed = jnp.any(row_listed & mine[:, None], axis=0)
    own = l_store[0] * jnp.repeat(own_listed.astype(jnp.float32), BLK)[:, None]
    base = jnp.sum(mine.astype(jnp.float32)) * diag_inv[0]

    def branch(place, cap):
        def run(anc, panels):
            partial_value = product(slot, rows, counts, sibling_columns, anc, panels, l_store.shape[2], cap)
            compact = reduce_rows(partial_value, row_count, cap // grain, place + 1)
            return expand(slot, owner, compact, siblings, col_blocks)
        return run

    upper, slots = lax.switch(level, [branch(place, cap) for place, cap in enumerate(caps)], anc_inverse, panels)
    lower, diag = finish(slots, own, base, row_count)
    return upper, lower[None], diag[None]


def solution(mesh):
    return jax.shard_map(
        per_device,
        mesh=mesh,
        in_specs=(P("row", "col"), P("col", "row", None), P("col", None, None), P(), P(), P()),
        out_specs=(P(None, "row", "col"), P("col", "row", None), P("col", None, None)),
        check_vma=False,
    )
```

```python
import functools

import jax
import jax.numpy as jnp
from jax import lax
from jax.experimental import pallas as pl
from jax.experimental.pallas import tpu as pltpu
from jax.sharding import PartitionSpec as P

BLK = 128
MESH = pl.DeviceIdType.MESH


def listed_table(block_lists, block_counts, block_total):
    block_ids = jnp.arange(block_total, dtype=jnp.int32)
    valid_entry = jnp.arange(block_lists.shape[1], dtype=jnp.int32)[None, :] < block_counts[:, None]
    entry_hits = (block_lists[:, :, None] == block_ids[None, None, :]) & valid_entry[:, :, None]
    return jnp.any(entry_hits, axis=1)


def product_kernel(siblings, tile_blocks, col_blocks, row_blocks,
                   slot_ref, rows_ref, count_ref, column_ref,
                   a_ref, panels_ref, out_ref, a_high, a_low, p_high, p_low, acc):
    stripe = pl.program_id(0)
    width = out_ref.shape[0]

    @pl.when(stripe == 0)
    def _():
        for sibling in range(siblings):
            column = column_ref[sibling]

            @pl.loop(0, row_blocks)
            def _(block):
                lanes = pl.ds(pl.multiple_of(block * BLK, BLK), BLK)
                value = panels_ref[pl.ds(pl.multiple_of(column * width, width), width), lanes]
                high = value.astype(jnp.bfloat16)
                p_high[sibling, block] = high
                p_low[sibling, block] = (value - high.astype(jnp.float32)).astype(jnp.bfloat16)

            p_high[sibling, row_blocks] = jnp.zeros(p_high.shape[2:], jnp.bfloat16)
            p_low[sibling, row_blocks] = jnp.zeros(p_low.shape[2:], jnp.bfloat16)

    @pl.loop(0, row_blocks)
    def _(block):
        rows = pl.ds(pl.multiple_of(block * BLK, BLK), BLK)
        value = a_ref[rows, :]
        high = value.astype(jnp.bfloat16)
        a_high[block] = high
        a_low[block] = (value - high.astype(jnp.float32)).astype(jnp.bfloat16)

    for sibling in range(siblings):
        acc[...] = jnp.zeros_like(acc)
        base = sibling * (row_blocks + 1)

        @pl.loop(0, (count_ref[sibling] + 1) // 2)
        def _(pair):
            first = rows_ref[base + 2 * pair]
            second = rows_ref[base + 2 * pair + 1]
            second_a = jnp.minimum(second, row_blocks - 1)
            ph = [p_high[sibling, first], p_high[sibling, second]]
            plo = [p_low[sibling, first], p_low[sibling, second]]
            ah = [a_high[first], a_high[second_a]]
            al = [a_low[first], a_low[second_a]]
            left = jnp.concatenate(ph + ph + plo, axis=1)
            right = jnp.concatenate(ah + al + ah, axis=0)
            acc[...] += jnp.dot(left, right, preferred_element_type=jnp.float32)

        for block in range(tile_blocks):
            slot = slot_ref[sibling * col_blocks + stripe * tile_blocks + block]

            @pl.when(slot >= 0)
            def _():
                out_ref[:, pl.ds(pl.multiple_of(slot * BLK, BLK), BLK)] = (
                    -acc[:, block * BLK:(block + 1) * BLK]
                )


def product(slot, rows, counts, columns, anc, panels, width, cap):
    siblings = counts.shape[0]
    depth, cells = anc.shape
    row_blocks, col_blocks = depth // BLK, cells // BLK
    tile_blocks = next(n for n in (4, 2, 1) if col_blocks % n == 0)
    tile = tile_blocks * BLK
    return pl.pallas_call(
        functools.partial(product_kernel, siblings, tile_blocks, col_blocks, row_blocks),
        out_shape=jax.ShapeDtypeStruct((width, cap * BLK), jnp.float32),
        grid_spec=pltpu.PrefetchScalarGridSpec(
            num_scalar_prefetch=4,
            grid=(col_blocks // tile_blocks,),
            in_specs=[
                pl.BlockSpec((depth, tile), lambda i, *_: (0, i)),
                pl.BlockSpec(panels.shape, lambda i, *_: (0, 0), pipeline_mode=pl.Buffered(1)),
            ],
            out_specs=pl.BlockSpec((width, cap * BLK), lambda i, *_: (0, 0), pipeline_mode=pl.Buffered(1)),
            scratch_shapes=[
                pltpu.VMEM((row_blocks, BLK, tile), jnp.bfloat16),
                pltpu.VMEM((row_blocks, BLK, tile), jnp.bfloat16),
                pltpu.VMEM((siblings, row_blocks + 1, width, BLK), jnp.bfloat16),
                pltpu.VMEM((siblings, row_blocks + 1, width, BLK), jnp.bfloat16),
                pltpu.VMEM((width, tile), jnp.float32),
            ],
        ),
        compiler_params=pltpu.CompilerParams(
            dimension_semantics=("arbitrary",), vmem_limit_bytes=63 * 1024 * 1000
        ),
    )(slot, rows, counts, columns, anc, panels)


def flip_kernel(value_ref, out_ref):
    out_ref[...] = value_ref[...].T


def flipped(value):
    depth, width = value.shape
    step = next(n for n in (512, 256, 128) if depth % n == 0)
    return pl.pallas_call(
        flip_kernel,
        out_shape=jax.ShapeDtypeStruct((width, depth), value.dtype),
        grid=(depth // step,),
        in_specs=[pl.BlockSpec((step, width), lambda i: (i, 0))],
        out_specs=pl.BlockSpec((width, step), lambda i: (0, i)),
    )(value)


def expand_kernel(siblings, col_count, col_blocks, slot_ref, owner_ref, compact_ref, upper_ref, slots_ref):
    @pl.loop(0, col_blocks)
    def _(block):
        lanes = pl.ds(pl.multiple_of(block * BLK, BLK), BLK)
        for sibling in range(siblings):
            slot = slot_ref[sibling * col_blocks + block]
            at = pl.ds(pl.multiple_of(jnp.maximum(slot, 0) * BLK, BLK), BLK)
            value = compact_ref[:, at]
            upper_ref[sibling, :, lanes] = jnp.where(slot >= 0, value, jnp.zeros_like(value))

    for column in range(col_count):
        sibling = owner_ref[column]
        value = upper_ref[jnp.maximum(sibling, 0)]
        slots_ref[column] = jnp.where(sibling >= 0, value, jnp.zeros_like(value))


def expand(slot, owner, compact, siblings, col_blocks):
    col_count = owner.shape[0]
    rows = compact.shape[0]
    return pl.pallas_call(
        functools.partial(expand_kernel, siblings, col_count, col_blocks),
        out_shape=(
            jax.ShapeDtypeStruct((siblings, rows, col_blocks * BLK), jnp.float32),
            jax.ShapeDtypeStruct((col_count, rows, col_blocks * BLK), jnp.float32),
        ),
        in_specs=[pl.BlockSpec(memory_space=pltpu.SMEM)] * 2 + [pl.BlockSpec(memory_space=pltpu.VMEM)],
        out_specs=(pl.BlockSpec(memory_space=pltpu.VMEM),) * 2,
    )(slot, owner, compact)


def reduce_kernel(line, flat_first, chunks,
                  partial_ref, out_ref,
                  pair_buf, up_buf, down_buf, flat_up, flat_down, flat_sum, flat_pair,
                  pair_send, pair_recv, up_send, up_recv, down_send, down_recv, flat_send, flat_recv):
    r, c = lax.axis_index("row"), lax.axis_index("col")
    z, y = r // 2, lax.rem(r, 2)
    other = 1 - y
    width = out_ref.shape[1] // chunks
    last, lag = line - 1, 2
    late = chunks - flat_first

    def lanes(chunk):
        return pl.ds(pl.multiple_of(chunk * width, width), width)

    barrier = pltpu.get_barrier_semaphore()
    pl.semaphore_signal(barrier, inc=1, device_id=(z * 2 + other, c), device_id_type=MESH)

    @pl.when(z > 0)
    def _():
        pl.semaphore_signal(barrier, inc=1, device_id=(r - 2, c), device_id_type=MESH)

    @pl.when(z < last)
    def _():
        pl.semaphore_signal(barrier, inc=1, device_id=(r + 2, c), device_id_type=MESH)

    pl.semaphore_wait(barrier, 1 + (z > 0).astype(jnp.int32) + (z < last).astype(jnp.int32))

    def pair_copy(k):
        return pltpu.make_async_remote_copy(
            src_ref=partial_ref.at[:, other, :, lanes(k + flat_first)],
            dst_ref=pair_buf.at[k],
            send_sem=pair_send.at[k],
            recv_sem=pair_recv.at[k],
            device_id=(z * 2 + other, c),
            device_id_type=MESH,
        )

    def flat_copy(k):
        return pltpu.make_async_remote_copy(
            src_ref=flat_sum.at[k, other],
            dst_ref=flat_pair.at[k],
            send_sem=flat_send.at[k],
            recv_sem=flat_recv.at[k],
            device_id=(z * 2 + other, c),
            device_id_type=MESH,
        )

    def up_copy(buf, k, slot, at):
        return pltpu.make_async_remote_copy(
            src_ref=buf.at[k, pl.ds(at, last - at)],
            dst_ref=buf.at[k, pl.ds(at, last - at)],
            send_sem=up_send.at[slot],
            recv_sem=up_recv.at[slot],
            device_id=(r + 2, c),
            device_id_type=MESH,
        )

    def down_copy(buf, k, slot, at):
        return pltpu.make_async_remote_copy(
            src_ref=buf.at[k, pl.ds(0, at)],
            dst_ref=buf.at[k, pl.ds(0, at)],
            send_sem=down_send.at[slot],
            recv_sem=down_recv.at[slot],
            device_id=(r - 2, c),
            device_id_type=MESH,
        )

    def flat(k):
        def own(place):
            return partial_ref[place, :, :, lanes(k)]

        def finish(value):
            flat_sum[k] = value
            flat_copy(k).start()

        return flat_up, flat_down, k, own, finish

    def paired(k):
        k = k - flat_first

        def own(place):
            return pair_buf[k, place]

        def finish(value):
            out_ref[:, lanes(k + flat_first)] = value

        return up_buf, down_buf, k, own, finish

    def total(at, up, down, k, own, finish):
        value = own(at)
        if at > 0:
            value = value + up[k, at - 1]
        if at < last:
            value = value + down[k, at]
        finish(value)

    def pass_up(at, slot, up, down, k, own, finish):
        if at > 0:
            up_copy(up, k, slot, at - 1).wait_recv()
        for place in range(at + 1, line):
            if at > 0:
                up[k, place - 1] = up[k, place - 1] + own(place)
            else:
                up[k, place - 1] = own(place)
        if at < last:
            up_copy(up, k, slot, at).start()
        if 2 * at > last:
            total(at, up, down, k, own, finish)

    def pass_down(at, slot, up, down, k, own, finish):
        if at < last:
            down_copy(down, k, slot, at + 1).wait_recv()
        for place in range(at):
            if at < last:
                down[k, place] = down[k, place] + own(place)
            else:
                down[k, place] = own(place)
        if at > 0:
            down_copy(down, k, slot, at).start()
        if 2 * at <= last:
            total(at, up, down, k, own, finish)

    def either(step, at, slot):
        @pl.when((slot >= 0) & (slot < flat_first))
        def _():
            step(at, slot, *flat(slot))

        @pl.when((slot >= flat_first) & (slot < chunks))
        def _():
            step(at, slot, *paired(slot))

    @pl.loop(0, late)
    def _(k):
        pair_copy(k).start()

    @pl.loop(0, chunks + lag * last)
    def _(i):
        @pl.when((i >= flat_first) & (i < chunks))
        def _():
            k = i - flat_first
            pair_copy(k).wait_recv()
            for place in range(line):
                pair_buf[k, place] = pair_buf[k, place] + partial_ref[place, y, :, lanes(i)]

        for at in range(line):
            @pl.when(z == at)
            def _():
                either(pass_up, at, i - lag * at)
                either(pass_down, at, i - lag * (last - at))

    @pl.loop(0, flat_first)
    def _(k):
        flat_copy(k).wait_recv()
        out_ref[:, lanes(k)] = flat_sum[k, y] + flat_pair[k]

    @pl.loop(0, late)
    def _(k):
        pair_copy(k).wait_send()

    @pl.loop(0, flat_first)
    def _(k):
        flat_copy(k).wait_send()

    for at in range(line):
        @pl.when(z == at)
        def _():
            for buf, start, stop, shift in ((flat_up, 0, flat_first, 0), (up_buf, 0, late, flat_first)):
                if at < last:
                    @pl.loop(start, stop)
                    def _(k):
                        up_copy(buf, k, k + shift, at).wait_send()
            for buf, start, stop, shift in ((flat_down, 0, flat_first, 0), (down_buf, 0, late, flat_first)):
                if at > 0:
                    @pl.loop(start, stop)
                    def _(k):
                        down_copy(buf, k, k + shift, at).wait_send()


def reduce_rows(value, row_count, chunks, collective):
    width, columns = value.shape
    line, slice_rows = row_count // 2, width // row_count
    lanes = columns // chunks
    flat_first = (chunks + 3) // 6
    late = chunks - flat_first
    vmem = pl.BlockSpec(memory_space=pltpu.VMEM)
    dma = pltpu.SemaphoreType.DMA
    return pl.pallas_call(
        functools.partial(reduce_kernel, line, flat_first, chunks),
        out_shape=jax.ShapeDtypeStruct((slice_rows, columns), jnp.float32),
        in_specs=[vmem],
        out_specs=vmem,
        scratch_shapes=[
            pltpu.VMEM((late, line, slice_rows, lanes), jnp.float32),
            pltpu.VMEM((late, line - 1, slice_rows, lanes), jnp.float32),
            pltpu.VMEM((late, line - 1, slice_rows, lanes), jnp.float32),
            pltpu.VMEM((flat_first, line - 1, 2, slice_rows, lanes), jnp.float32),
            pltpu.VMEM((flat_first, line - 1, 2, slice_rows, lanes), jnp.float32),
            pltpu.VMEM((flat_first, 2, slice_rows, lanes), jnp.float32),
            pltpu.VMEM((flat_first, slice_rows, lanes), jnp.float32),
            dma((late,)),
            dma((late,)),
            dma((chunks,)),
            dma((chunks,)),
            dma((chunks,)),
            dma((chunks,)),
            dma((flat_first,)),
            dma((flat_first,)),
        ],
        compiler_params=pltpu.CompilerParams(
            collective_id=collective, has_side_effects=True, vmem_limit_bytes=63 * 1024 * 1000
        ),
    )(value.reshape(line, 2, slice_rows, columns))


def finish_kernel(row_count, col_count,
                  slots_ref, own_ref, base_ref, lower_ref, diag_ref,
                  stage, picked, inner, part, reduced, total,
                  stage_send, stage_recv, send_sem, recv_sem, part_send, part_recv, total_send, total_recv):
    r, c = lax.axis_index("row"), lax.axis_index("col")
    ratio = row_count // col_count
    slice_rows, cells = picked.shape[1], picked.shape[2]

    barrier = pltpu.get_barrier_semaphore()
    for peer in range(row_count):
        @pl.when(peer != r)
        def _():
            pl.semaphore_signal(barrier, inc=1, device_id=(peer, c), device_id_type=MESH)
    for peer in range(col_count):
        @pl.when(peer != c)
        def _():
            pl.semaphore_signal(barrier, inc=1, device_id=(r, peer), device_id_type=MESH)
    pl.semaphore_wait(barrier, row_count + col_count - 2)

    def near(offset):
        pair = lax.rem(c // 2 + offset // 2, col_count // 2)
        return pair * 2 + lax.rem(lax.rem(c, 2) + offset % 2, 2)

    def column_copy(target):
        return pltpu.make_async_remote_copy(
            src_ref=slots_ref.at[target],
            dst_ref=stage.at[c],
            send_sem=stage_send.at[target],
            recv_sem=stage_recv.at[c],
            device_id=(r, target),
            device_id_type=MESH,
        )

    def column_arrived(source):
        return pltpu.make_async_remote_copy(
            src_ref=slots_ref.at[source],
            dst_ref=stage.at[source],
            send_sem=stage_send.at[source],
            recv_sem=stage_recv.at[source],
            device_id=(r, source),
            device_id_type=MESH,
        )

    def row_copy(held, source, k):
        target = source * ratio + k
        return pltpu.make_async_remote_copy(
            src_ref=held.at[source, :, pl.ds(k * cells, cells)],
            dst_ref=picked.at[r],
            send_sem=send_sem.at[target],
            recv_sem=recv_sem.at[r],
            device_id=(target, c),
            device_id_type=MESH,
        )

    def row_local(held, source, k):
        return pltpu.make_async_copy(
            held.at[source, :, pl.ds(k * cells, cells)], picked.at[r], recv_sem.at[r]
        )

    def row_arrived(source):
        return pltpu.make_async_remote_copy(
            src_ref=picked.at[source],
            dst_ref=picked.at[source],
            send_sem=send_sem.at[source],
            recv_sem=recv_sem.at[source],
            device_id=(source, c),
            device_id_type=MESH,
        )

    for offset in range(2, col_count):
        column_copy(near(offset)).start()
    column_copy(near(1)).start()
    for offset in range(col_count):
        source = near(offset)
        held = stage if offset else slots_ref
        if offset:
            column_arrived(source).wait_recv()
        for k in range(ratio):
            @pl.when(source * ratio + k == r)
            def _():
                row_local(held, source, k).start()

            @pl.when(source * ratio + k != r)
            def _():
                row_copy(held, source, k).start()

    for offset in range(col_count):
        source = near(offset)
        held = stage if offset else slots_ref
        for k in range(ratio):
            @pl.when(source * ratio + k == r)
            def _():
                row_local(held, source, k).wait()
    for source in range(row_count):
        @pl.when(source != r)
        def _():
            row_arrived(source).wait_recv()

    step = 256 if cells % 256 == 0 else BLK
    inner[...] = jnp.zeros_like(inner)

    @pl.loop(0, cells // step)
    def _(i):
        at = pl.ds(pl.multiple_of(i * step, step), step)
        block = picked[:, :, at].reshape(row_count * slice_rows, step)
        inner[...] += jnp.dot(
            block, own_ref[at, :], precision=lax.Precision.HIGHEST, preferred_element_type=jnp.float32
        )

    def part_copy(peer):
        return pltpu.make_async_remote_copy(
            src_ref=inner.at[pl.ds(peer * slice_rows, slice_rows), :],
            dst_ref=part.at[r],
            send_sem=part_send.at[peer],
            recv_sem=part_recv.at[r],
            device_id=(peer, c),
            device_id_type=MESH,
        )

    def part_arrived(peer):
        return pltpu.make_async_remote_copy(
            src_ref=inner.at[pl.ds(0, slice_rows), :],
            dst_ref=part.at[peer],
            send_sem=part_send.at[peer],
            recv_sem=part_recv.at[peer],
            device_id=(peer, c),
            device_id_type=MESH,
        )

    def total_copy(peer):
        return pltpu.make_async_remote_copy(
            src_ref=reduced,
            dst_ref=total.at[r],
            send_sem=total_send.at[peer],
            recv_sem=total_recv.at[r],
            device_id=(peer, c),
            device_id_type=MESH,
        )

    def total_arrived(peer):
        return pltpu.make_async_remote_copy(
            src_ref=reduced,
            dst_ref=total.at[peer],
            send_sem=total_send.at[peer],
            recv_sem=total_recv.at[peer],
            device_id=(peer, c),
            device_id_type=MESH,
        )

    def peers(action):
        for peer in range(row_count):
            @pl.when(peer != r)
            def _():
                action(peer)

    peers(lambda peer: part_copy(peer).start())
    peers(lambda peer: part_arrived(peer).wait_recv())
    mine = inner[pl.ds(pl.multiple_of(r * slice_rows, slice_rows), slice_rows), :]
    for peer in range(row_count):
        @pl.when(peer == r)
        def _():
            part[peer] = mine
    value = part[0]
    for peer in range(1, row_count):
        value = value + part[peer]
    reduced[...] = value
    peers(lambda peer: total_copy(peer).start())

    @pl.loop(0, cells // step)
    def _(i):
        at = pl.ds(pl.multiple_of(i * step, step), step)
        block = picked[:, :, at].reshape(row_count * slice_rows, step)
        lower_ref[at, :] = block.T

    peers(lambda peer: total_arrived(peer).wait_recv())
    for peer in range(row_count):
        @pl.when(peer == r)
        def _():
            total[peer] = reduced[...]
    diag_ref[...] = base_ref[...] - total[...].reshape(diag_ref.shape)

    for offset in range(col_count):
        source = near(offset)
        held = stage if offset else slots_ref
        if offset:
            column_copy(source).wait_send()
        for k in range(ratio):
            @pl.when(source * ratio + k != r)
            def _():
                row_copy(held, source, k).wait_send()
    peers(lambda peer: part_copy(peer).wait_send())
    peers(lambda peer: total_copy(peer).wait_send())


def finish(slots, own, base, row_count):
    col_count, slice_rows, _ = slots.shape
    cells, width = own.shape
    vmem = pl.BlockSpec(memory_space=pltpu.VMEM)
    dma = pltpu.SemaphoreType.DMA
    return pl.pallas_call(
        functools.partial(finish_kernel, row_count, col_count),
        out_shape=(
            jax.ShapeDtypeStruct((cells, width), jnp.float32),
            jax.ShapeDtypeStruct((width, width), jnp.float32),
        ),
        in_specs=[vmem] * 3,
        out_specs=(vmem, vmem),
        scratch_shapes=[
            pltpu.VMEM(slots.shape, jnp.float32),
            pltpu.VMEM((row_count, slice_rows, cells), jnp.float32),
            pltpu.VMEM((width, width), jnp.float32),
            pltpu.VMEM((row_count, slice_rows, width), jnp.float32),
            pltpu.VMEM((slice_rows, width), jnp.float32),
            pltpu.VMEM((row_count, slice_rows, width), jnp.float32),
            dma((col_count,)),
            dma((col_count,)),
            dma((row_count,)),
            dma((row_count,)),
            dma((row_count,)),
            dma((row_count,)),
            dma((row_count,)),
            dma((row_count,)),
        ],
        compiler_params=pltpu.CompilerParams(collective_id=0, has_side_effects=True),
    )(slots, own, base)


def per_device(anc_inverse, l_store, diag_inv, block_lists, block_counts, sibling_columns):
    siblings = block_lists.shape[0]
    row_count, col_count = lax.axis_size("row"), lax.axis_size("col")
    r, c = lax.axis_index("row"), lax.axis_index("col")
    row_blocks, col_blocks = anc_inverse.shape[0] // BLK, anc_inverse.shape[1] // BLK
    panels = lax.all_gather(flipped(l_store[0]), "col", tiled=True)

    table = listed_table(block_lists, block_counts, row_blocks * row_count)
    row_listed = lax.dynamic_slice_in_dim(table, r * row_blocks, row_blocks, axis=1)
    col_listed = lax.dynamic_slice_in_dim(table, c * col_blocks, col_blocks, axis=1)
    row_ints = row_listed.astype(jnp.int32)
    counts = jnp.sum(row_ints, axis=1)
    place = jnp.cumsum(row_ints, axis=1) - 1
    ids = jnp.arange(row_blocks, dtype=jnp.int32)
    entry = jnp.arange(row_blocks + 1, dtype=jnp.int32)
    hits = row_listed[:, :, None] & (place[:, :, None] == entry[None, None, :])
    rows = jnp.sum(jnp.where(hits, ids[None, :, None], 0), axis=1)
    rows = jnp.where(entry[None, :] < counts[:, None], rows, row_blocks).astype(jnp.int32).reshape(-1)

    flat = col_listed.reshape(-1)
    slot = jnp.where(flat, jnp.cumsum(flat.astype(jnp.int32)) - 1, -1).astype(jnp.int32)
    per_column = jnp.sum(table.reshape(siblings, col_count, col_blocks).astype(jnp.int32), axis=(0, 2))
    needed = jnp.max(per_column)
    slots_all = siblings * col_blocks
    grain = -(-slots_all // 40)
    caps = [grain * n for n in (19, 21, 23, 25, 28, 32, 40)]
    level = jnp.sum((needed > jnp.array(caps[:-1], jnp.int32)).astype(jnp.int32))

    match = sibling_columns[:, None] == jnp.arange(col_count, dtype=jnp.int32)[None, :]
    owner = jnp.max(
        jnp.where(match, jnp.arange(siblings, dtype=jnp.int32)[:, None], -1), axis=0
    ).astype(jnp.int32)
    mine = sibling_columns == c
    own_listed = jnp.any(row_listed & mine[:, None], axis=0)
    own = l_store[0] * jnp.repeat(own_listed.astype(jnp.float32), BLK)[:, None]
    base = jnp.sum(mine.astype(jnp.float32)) * diag_inv[0]

    def branch(place, cap):
        def run(anc, panels):
            partial_value = product(slot, rows, counts, sibling_columns, anc, panels, l_store.shape[2], cap)
            compact = reduce_rows(partial_value, row_count, cap // grain, place + 1)
            return expand(slot, owner, compact, siblings, col_blocks)
        return run

    upper, slots = lax.switch(level, [branch(place, cap) for place, cap in enumerate(caps)], anc_inverse, panels)
    lower, diag = finish(slots, own, base, row_count)
    return upper, lower[None], diag[None]


def solution(mesh):
    return jax.shard_map(
        per_device,
        mesh=mesh,
        in_specs=(P("row", "col"), P("col", "row", None), P("col", None, None), P(), P(), P()),
        out_specs=(P(None, "row", "col"), P("col", "row", None), P("col", None, None)),
        check_vma=False,
    )
```

```python
import functools

import jax
import jax.numpy as jnp
from jax import lax
from jax.experimental import pallas as pl
from jax.experimental.pallas import tpu as pltpu
from jax.sharding import PartitionSpec as P

BLK = 128
GROUP = 4
MESH = pl.DeviceIdType.MESH


def listed_table(block_lists, block_counts, block_total):
    block_ids = jnp.arange(block_total, dtype=jnp.int32)
    valid_entry = jnp.arange(block_lists.shape[1], dtype=jnp.int32)[None, :] < block_counts[:, None]
    entry_hits = (block_lists[:, :, None] == block_ids[None, None, :]) & valid_entry[:, :, None]
    return jnp.any(entry_hits, axis=1)


def product_kernel(members, tile_blocks, col_blocks, row_blocks, joins,
                   slot_ref, rows_ref, count_ref, a_ref, *refs):
    panel_refs, refs = refs[:members], refs[members + joins:]
    out_ref, a_high, a_low, p_high, p_low, stage, sent = refs
    stripe, stripes = pl.program_id(0), pl.num_programs(0)
    group = p_high.shape[3] // BLK
    listed = p_high.shape[1] * group

    @pl.when(stripe == 0)
    def _():
        for member in range(members):
            @pl.loop(0, count_ref[member])
            def _(i):
                rows = pl.ds(pl.multiple_of(rows_ref[member * listed + i] * BLK, BLK), BLK)
                lanes = pl.ds(pl.multiple_of(lax.rem(i, group) * BLK, BLK), BLK)
                value = -panel_refs[member][rows, :].T
                high = value.astype(jnp.bfloat16)
                p_high[member, i // group, :, lanes] = high
                p_low[member, i // group, :, lanes] = (value - high.astype(jnp.float32)).astype(jnp.bfloat16)

            @pl.loop(count_ref[member], (count_ref[member] + group - 1) // group * group)
            def _(i):
                lanes = pl.ds(pl.multiple_of(lax.rem(i, group) * BLK, BLK), BLK)
                zero = jnp.zeros((p_high.shape[2], BLK), jnp.bfloat16)
                p_high[member, i // group, :, lanes] = zero
                p_low[member, i // group, :, lanes] = zero

    @pl.loop(0, row_blocks)
    def _(block):
        rows = pl.ds(pl.multiple_of(block * BLK, BLK), BLK)
        value = a_ref[rows, :]
        high = value.astype(jnp.bfloat16)
        a_high[block] = high
        a_low[block] = (value - high.astype(jnp.float32)).astype(jnp.bfloat16)

    def slot_of(member, block, at):
        return slot_ref[member * col_blocks + at * tile_blocks + block]

    def slot_copy(member, block, slot):
        return pltpu.make_async_copy(
            stage.at[member, :, pl.ds(block * BLK, BLK)],
            out_ref.at[:, pl.ds(pl.multiple_of(slot * BLK, BLK), BLK)],
            sent.at[member, block],
        )

    def settle(member, at):
        for block in range(tile_blocks):
            slot = slot_of(member, block, at)

            @pl.when(slot >= 0)
            def _():
                slot_copy(member, block, slot).wait()

    for member in range(members):
        @pl.when(stripe > 0)
        def _():
            settle(member, stripe - 1)

        stage[member] = jnp.zeros(stage.shape[1:], jnp.float32)

        @pl.loop(0, (count_ref[member] + group - 1) // group)
        def _(k):
            at = [rows_ref[member * listed + k * group + u] for u in range(group)]
            ph, plo = p_high[member, k], p_low[member, k]
            ah, al = [a_high[i] for i in at], [a_low[i] for i in at]
            left = jnp.concatenate([ph, ph, plo], axis=1)
            right = jnp.concatenate(ah + al + ah, axis=0)
            stage[member] += jnp.dot(left, right, preferred_element_type=jnp.float32)

        for block in range(tile_blocks):
            slot = slot_of(member, block, stripe)

            @pl.when(slot >= 0)
            def _():
                slot_copy(member, block, slot).start()

    @pl.when(stripe == stripes - 1)
    def _():
        for member in range(members):
            settle(member, stripe)


def product(slot, rows, counts, anc, panels, slots_all, partial_value=None):
    members = counts.shape[0]
    depth, cells = anc.shape
    width = panels[0].shape[1]
    row_blocks, col_blocks = depth // BLK, cells // BLK
    tile_blocks = next(n for n in (8, 4, 2, 1) if col_blocks % n == 0)
    tile = tile_blocks * BLK
    groups = rows.shape[1] // GROUP
    joins = () if partial_value is None else (partial_value,)
    held = pl.BlockSpec((depth, width), lambda i, *_: (0, 0), pipeline_mode=pl.Buffered(1))
    return pl.pallas_call(
        functools.partial(product_kernel, members, tile_blocks, col_blocks, row_blocks, len(joins)),
        out_shape=jax.ShapeDtypeStruct((width, slots_all * BLK), jnp.float32),
        grid_spec=pltpu.PrefetchScalarGridSpec(
            num_scalar_prefetch=3,
            grid=(col_blocks // tile_blocks,),
            in_specs=[pl.BlockSpec((depth, tile), lambda i, *_: (0, i))]
            + [held] * members
            + [pl.BlockSpec(memory_space=pl.ANY)] * len(joins),
            out_specs=pl.BlockSpec(memory_space=pl.ANY),
            scratch_shapes=[
                pltpu.VMEM((row_blocks, BLK, tile), jnp.bfloat16),
                pltpu.VMEM((row_blocks, BLK, tile), jnp.bfloat16),
                pltpu.VMEM((members, groups, width, GROUP * BLK), jnp.bfloat16),
                pltpu.VMEM((members, groups, width, GROUP * BLK), jnp.bfloat16),
                pltpu.VMEM((members, width, tile), jnp.float32),
                pltpu.SemaphoreType.DMA((members, tile_blocks)),
            ],
        ),
        input_output_aliases={4 + members: 0} if joins else {},
        cost_estimate=pl.CostEstimate(
            flops=2 * 3 * members * depth * cells * width // 2,
            bytes_accessed=4 * depth * cells + 4 * members * width * cells,
            transcendentals=0,
        ),
        compiler_params=pltpu.CompilerParams(
            dimension_semantics=("arbitrary",), vmem_limit_bytes=63 * 1024 * 1000
        ),
    )(slot.reshape(-1), rows.reshape(-1), counts, anc, *panels, *joins)


def expand_kernel(siblings, col_count, col_blocks, slot_ref, owner_ref, compact_ref, upper_ref, slots_ref):
    @pl.loop(0, col_blocks)
    def _(block):
        lanes = pl.ds(pl.multiple_of(block * BLK, BLK), BLK)
        for sibling in range(siblings):
            slot = slot_ref[sibling * col_blocks + block]
            at = pl.ds(pl.multiple_of(jnp.maximum(slot, 0) * BLK, BLK), BLK)
            value = compact_ref[:, at]
            upper_ref[sibling, :, lanes] = jnp.where(slot >= 0, value, jnp.zeros_like(value))

    for column in range(col_count):
        sibling = owner_ref[column]
        value = upper_ref[jnp.maximum(sibling, 0)]
        slots_ref[column] = jnp.where(sibling >= 0, value, jnp.zeros_like(value))


def expand(slot, owner, compact, siblings, col_blocks):
    col_count = owner.shape[0]
    rows = compact.shape[0]
    return pl.pallas_call(
        functools.partial(expand_kernel, siblings, col_count, col_blocks),
        out_shape=(
            jax.ShapeDtypeStruct((siblings, rows, col_blocks * BLK), jnp.float32),
            jax.ShapeDtypeStruct((col_count, rows, col_blocks * BLK), jnp.float32),
        ),
        in_specs=[pl.BlockSpec(memory_space=pltpu.SMEM)] * 2 + [pl.BlockSpec(memory_space=pltpu.VMEM)],
        out_specs=(pl.BlockSpec(memory_space=pltpu.VMEM),) * 2,
    )(slot, owner, compact)


def reduce_kernel(line, flat_first, chunks,
                  partial_ref, out_ref,
                  mine, flat_mine, pair_buf, up_buf, down_buf, flat_up, flat_down, flat_sum, flat_pair,
                  mine_sem, flat_sem, pair_send, pair_recv, up_send, up_recv, down_send, down_recv, flat_send, flat_recv):
    r, c = lax.axis_index("row"), lax.axis_index("col")
    z, y = r // 2, lax.rem(r, 2)
    other = 1 - y
    width = out_ref.shape[1] // chunks
    last, lag = line - 1, 2
    late = chunks - flat_first

    def lanes(chunk):
        return pl.ds(pl.multiple_of(chunk * width, width), width)

    def flat_load(k):
        return pltpu.make_async_copy(partial_ref.at[:, :, :, lanes(k)], flat_mine.at[k], flat_sem.at[k])

    def pair_load(k):
        return pltpu.make_async_copy(
            partial_ref.at[:, y, :, lanes(k + flat_first)], mine.at[k], mine_sem.at[k]
        )

    @pl.loop(0, flat_first)
    def _(k):
        flat_load(k).start()

    barrier = pltpu.get_barrier_semaphore()
    pl.semaphore_signal(barrier, inc=1, device_id=(z * 2 + other, c), device_id_type=MESH)

    @pl.when(z > 0)
    def _():
        pl.semaphore_signal(barrier, inc=1, device_id=(r - 2, c), device_id_type=MESH)

    @pl.when(z < last)
    def _():
        pl.semaphore_signal(barrier, inc=1, device_id=(r + 2, c), device_id_type=MESH)

    pl.semaphore_wait(barrier, 1 + (z > 0).astype(jnp.int32) + (z < last).astype(jnp.int32))

    def pair_copy(k):
        return pltpu.make_async_remote_copy(
            src_ref=partial_ref.at[:, other, :, lanes(k + flat_first)],
            dst_ref=pair_buf.at[k],
            send_sem=pair_send.at[k],
            recv_sem=pair_recv.at[k],
            device_id=(z * 2 + other, c),
            device_id_type=MESH,
        )

    def flat_copy(k):
        return pltpu.make_async_remote_copy(
            src_ref=flat_sum.at[k, other],
            dst_ref=flat_pair.at[k],
            send_sem=flat_send.at[k],
            recv_sem=flat_recv.at[k],
            device_id=(z * 2 + other, c),
            device_id_type=MESH,
        )

    def up_copy(buf, k, slot, at):
        return pltpu.make_async_remote_copy(
            src_ref=buf.at[k, pl.ds(at, last - at)],
            dst_ref=buf.at[k, pl.ds(at, last - at)],
            send_sem=up_send.at[slot],
            recv_sem=up_recv.at[slot],
            device_id=(r + 2, c),
            device_id_type=MESH,
        )

    def down_copy(buf, k, slot, at):
        return pltpu.make_async_remote_copy(
            src_ref=buf.at[k, pl.ds(0, at)],
            dst_ref=buf.at[k, pl.ds(0, at)],
            send_sem=down_send.at[slot],
            recv_sem=down_recv.at[slot],
            device_id=(r - 2, c),
            device_id_type=MESH,
        )

    def flat(k):
        def own(place):
            return flat_mine[k, place]

        def finish(value):
            flat_sum[k] = value
            flat_copy(k).start()

        return flat_up, flat_down, k, own, finish

    def paired(k):
        k = k - flat_first

        def own(place):
            return pair_buf[k, place]

        def finish(value):
            out_ref[:, lanes(k + flat_first)] = value

        return up_buf, down_buf, k, own, finish

    def total(at, up, down, k, own, finish):
        value = own(at)
        if at > 0:
            value = value + up[k, at - 1]
        if at < last:
            value = value + down[k, at]
        finish(value)

    def pass_up(at, slot, up, down, k, own, finish):
        if at > 0:
            up_copy(up, k, slot, at - 1).wait_recv()
        for place in range(at + 1, line):
            if at > 0:
                up[k, place - 1] = up[k, place - 1] + own(place)
            else:
                up[k, place - 1] = own(place)
        if at < last:
            up_copy(up, k, slot, at).start()
        if 2 * at > last:
            total(at, up, down, k, own, finish)

    def pass_down(at, slot, up, down, k, own, finish):
        if at < last:
            down_copy(down, k, slot, at + 1).wait_recv()
        for place in range(at):
            if at < last:
                down[k, place] = down[k, place] + own(place)
            else:
                down[k, place] = own(place)
        if at > 0:
            down_copy(down, k, slot, at).start()
        if 2 * at <= last:
            total(at, up, down, k, own, finish)

    def either(step, at, slot):
        @pl.when((slot >= 0) & (slot < flat_first))
        def _():
            step(at, slot, *flat(slot))

        @pl.when((slot >= flat_first) & (slot < chunks))
        def _():
            step(at, slot, *paired(slot))

    @pl.loop(0, late)
    def _(k):
        pair_copy(k).start()
        pair_load(k).start()

    @pl.loop(0, chunks + lag * last)
    def _(i):
        @pl.when(i < flat_first)
        def _():
            flat_load(i).wait()

        @pl.when((i >= flat_first) & (i < chunks))
        def _():
            k = i - flat_first
            pair_load(k).wait()
            pair_copy(k).wait_recv()
            for place in range(line):
                pair_buf[k, place] = pair_buf[k, place] + mine[k, place]

        for at in range(line):
            @pl.when(z == at)
            def _():
                either(pass_up, at, i - lag * at)
                either(pass_down, at, i - lag * (last - at))

    @pl.loop(0, flat_first)
    def _(k):
        flat_copy(k).wait_recv()
        out_ref[:, lanes(k)] = flat_sum[k, y] + flat_pair[k]

    @pl.loop(0, late)
    def _(k):
        pair_copy(k).wait_send()

    @pl.loop(0, flat_first)
    def _(k):
        flat_copy(k).wait_send()

    for at in range(line):
        @pl.when(z == at)
        def _():
            for buf, start, stop, shift in ((flat_up, 0, flat_first, 0), (up_buf, 0, late, flat_first)):
                if at < last:
                    @pl.loop(start, stop)
                    def _(k):
                        up_copy(buf, k, k + shift, at).wait_send()
            for buf, start, stop, shift in ((flat_down, 0, flat_first, 0), (down_buf, 0, late, flat_first)):
                if at > 0:
                    @pl.loop(start, stop)
                    def _(k):
                        down_copy(buf, k, k + shift, at).wait_send()


def reduce_rows(value, row_count, chunks, lanes, collective):
    width, columns = value.shape
    line, slice_rows = row_count // 2, width // row_count
    flat_first = (chunks + 3) // 6
    late = chunks - flat_first
    vmem = pl.BlockSpec(memory_space=pltpu.VMEM)
    dma = pltpu.SemaphoreType.DMA
    return pl.pallas_call(
        functools.partial(reduce_kernel, line, flat_first, chunks),
        out_shape=jax.ShapeDtypeStruct((slice_rows, chunks * lanes), jnp.float32),
        in_specs=[pl.BlockSpec(memory_space=pl.ANY)],
        out_specs=vmem,
        scratch_shapes=[
            pltpu.VMEM((late, line, slice_rows, lanes), jnp.float32),
            pltpu.VMEM((flat_first, line, 2, slice_rows, lanes), jnp.float32),
            pltpu.VMEM((late, line, slice_rows, lanes), jnp.float32),
            pltpu.VMEM((late, line - 1, slice_rows, lanes), jnp.float32),
            pltpu.VMEM((late, line - 1, slice_rows, lanes), jnp.float32),
            pltpu.VMEM((flat_first, line - 1, 2, slice_rows, lanes), jnp.float32),
            pltpu.VMEM((flat_first, line - 1, 2, slice_rows, lanes), jnp.float32),
            pltpu.VMEM((flat_first, 2, slice_rows, lanes), jnp.float32),
            pltpu.VMEM((flat_first, slice_rows, lanes), jnp.float32),
            dma((late,)),
            dma((flat_first,)),
            dma((late,)),
            dma((late,)),
            dma((chunks,)),
            dma((chunks,)),
            dma((chunks,)),
            dma((chunks,)),
            dma((flat_first,)),
            dma((flat_first,)),
        ],
        compiler_params=pltpu.CompilerParams(
            collective_id=collective, has_side_effects=True, vmem_limit_bytes=63 * 1024 * 1000
        ),
    )(value.reshape(line, 2, slice_rows, columns))


def finish_kernel(row_count, col_count,
                  slots_ref, own_ref, base_ref, lower_ref, diag_ref,
                  stage, picked, inner, part, reduced, total,
                  stage_send, stage_recv, send_sem, recv_sem, part_send, part_recv, total_send, total_recv):
    r, c = lax.axis_index("row"), lax.axis_index("col")
    ratio = row_count // col_count
    slice_rows, cells = picked.shape[1], picked.shape[2]

    barrier = pltpu.get_barrier_semaphore()
    for peer in range(row_count):
        @pl.when(peer != r)
        def _():
            pl.semaphore_signal(barrier, inc=1, device_id=(peer, c), device_id_type=MESH)
    for peer in range(col_count):
        @pl.when(peer != c)
        def _():
            pl.semaphore_signal(barrier, inc=1, device_id=(r, peer), device_id_type=MESH)
    pl.semaphore_wait(barrier, row_count + col_count - 2)

    def near(offset):
        pair = lax.rem(c // 2 + offset // 2, col_count // 2)
        return pair * 2 + lax.rem(lax.rem(c, 2) + offset % 2, 2)

    def column_copy(target):
        return pltpu.make_async_remote_copy(
            src_ref=slots_ref.at[target],
            dst_ref=stage.at[c],
            send_sem=stage_send.at[target],
            recv_sem=stage_recv.at[c],
            device_id=(r, target),
            device_id_type=MESH,
        )

    def column_arrived(source):
        return pltpu.make_async_remote_copy(
            src_ref=slots_ref.at[source],
            dst_ref=stage.at[source],
            send_sem=stage_send.at[source],
            recv_sem=stage_recv.at[source],
            device_id=(r, source),
            device_id_type=MESH,
        )

    def row_copy(held, source, k):
        target = source * ratio + k
        return pltpu.make_async_remote_copy(
            src_ref=held.at[source, :, pl.ds(k * cells, cells)],
            dst_ref=picked.at[r],
            send_sem=send_sem.at[target],
            recv_sem=recv_sem.at[r],
            device_id=(target, c),
            device_id_type=MESH,
        )

    def row_local(held, source, k):
        return pltpu.make_async_copy(
            held.at[source, :, pl.ds(k * cells, cells)], picked.at[r], recv_sem.at[r]
        )

    def row_arrived(source):
        return pltpu.make_async_remote_copy(
            src_ref=picked.at[source],
            dst_ref=picked.at[source],
            send_sem=send_sem.at[source],
            recv_sem=recv_sem.at[source],
            device_id=(source, c),
            device_id_type=MESH,
        )

    for offset in range(2, col_count):
        column_copy(near(offset)).start()
    column_copy(near(1)).start()
    for offset in range(col_count):
        source = near(offset)
        held = stage if offset else slots_ref
        if offset:
            column_arrived(source).wait_recv()
        for k in range(ratio):
            @pl.when(source * ratio + k == r)
            def _():
                row_local(held, source, k).start()

            @pl.when(source * ratio + k != r)
            def _():
                row_copy(held, source, k).start()

    for offset in range(col_count):
        source = near(offset)
        held = stage if offset else slots_ref
        for k in range(ratio):
            @pl.when(source * ratio + k == r)
            def _():
                row_local(held, source, k).wait()
    for source in range(row_count):
        @pl.when(source != r)
        def _():
            row_arrived(source).wait_recv()

    step = 256 if cells % 256 == 0 else BLK
    inner[...] = jnp.zeros_like(inner)

    @pl.loop(0, cells // step)
    def _(i):
        at = pl.ds(pl.multiple_of(i * step, step), step)
        block = picked[:, :, at].reshape(row_count * slice_rows, step)
        inner[...] += jnp.dot(
            block, own_ref[at, :], precision=lax.Precision.HIGHEST, preferred_element_type=jnp.float32
        )

    def part_copy(peer):
        return pltpu.make_async_remote_copy(
            src_ref=inner.at[pl.ds(peer * slice_rows, slice_rows), :],
            dst_ref=part.at[r],
            send_sem=part_send.at[peer],
            recv_sem=part_recv.at[r],
            device_id=(peer, c),
            device_id_type=MESH,
        )

    def part_arrived(peer):
        return pltpu.make_async_remote_copy(
            src_ref=inner.at[pl.ds(0, slice_rows), :],
            dst_ref=part.at[peer],
            send_sem=part_send.at[peer],
            recv_sem=part_recv.at[peer],
            device_id=(peer, c),
            device_id_type=MESH,
        )

    def total_copy(peer):
        return pltpu.make_async_remote_copy(
            src_ref=reduced,
            dst_ref=total.at[r],
            send_sem=total_send.at[peer],
            recv_sem=total_recv.at[r],
            device_id=(peer, c),
            device_id_type=MESH,
        )

    def total_arrived(peer):
        return pltpu.make_async_remote_copy(
            src_ref=reduced,
            dst_ref=total.at[peer],
            send_sem=total_send.at[peer],
            recv_sem=total_recv.at[peer],
            device_id=(peer, c),
            device_id_type=MESH,
        )

    def peers(action):
        for peer in range(row_count):
            @pl.when(peer != r)
            def _():
                action(peer)

    peers(lambda peer: part_copy(peer).start())
    peers(lambda peer: part_arrived(peer).wait_recv())
    mine = inner[pl.ds(pl.multiple_of(r * slice_rows, slice_rows), slice_rows), :]
    for peer in range(row_count):
        @pl.when(peer == r)
        def _():
            part[peer] = mine
    value = part[0]
    for peer in range(1, row_count):
        value = value + part[peer]
    reduced[...] = value
    peers(lambda peer: total_copy(peer).start())

    @pl.loop(0, cells // step)
    def _(i):
        at = pl.ds(pl.multiple_of(i * step, step), step)
        block = picked[:, :, at].reshape(row_count * slice_rows, step)
        lower_ref[at, :] = block.T

    peers(lambda peer: total_arrived(peer).wait_recv())
    for peer in range(row_count):
        @pl.when(peer == r)
        def _():
            total[peer] = reduced[...]
    diag_ref[...] = base_ref[...] - total[...].reshape(diag_ref.shape)

    for offset in range(col_count):
        source = near(offset)
        held = stage if offset else slots_ref
        if offset:
            column_copy(source).wait_send()
        for k in range(ratio):
            @pl.when(source * ratio + k != r)
            def _():
                row_copy(held, source, k).wait_send()
    peers(lambda peer: part_copy(peer).wait_send())
    peers(lambda peer: total_copy(peer).wait_send())


def finish(slots, own, base, row_count):
    col_count, slice_rows, _ = slots.shape
    cells, width = own.shape
    vmem = pl.BlockSpec(memory_space=pltpu.VMEM)
    dma = pltpu.SemaphoreType.DMA
    return pl.pallas_call(
        functools.partial(finish_kernel, row_count, col_count),
        out_shape=(
            jax.ShapeDtypeStruct((cells, width), jnp.float32),
            jax.ShapeDtypeStruct((width, width), jnp.float32),
        ),
        in_specs=[vmem] * 3,
        out_specs=(vmem, vmem),
        scratch_shapes=[
            pltpu.VMEM(slots.shape, jnp.float32),
            pltpu.VMEM((row_count, slice_rows, cells), jnp.float32),
            pltpu.VMEM((width, width), jnp.float32),
            pltpu.VMEM((row_count, slice_rows, width), jnp.float32),
            pltpu.VMEM((slice_rows, width), jnp.float32),
            pltpu.VMEM((row_count, slice_rows, width), jnp.float32),
            dma((col_count,)),
            dma((col_count,)),
            dma((row_count,)),
            dma((row_count,)),
            dma((row_count,)),
            dma((row_count,)),
            dma((row_count,)),
            dma((row_count,)),
        ],
        compiler_params=pltpu.CompilerParams(collective_id=0, has_side_effects=True),
    )(slots, own, base)


def per_device(anc_inverse, l_store, diag_inv, block_lists, block_counts, sibling_columns):
    siblings = block_lists.shape[0]
    row_count, col_count = lax.axis_size("row"), lax.axis_size("col")
    r, c = lax.axis_index("row"), lax.axis_index("col")
    row_blocks, col_blocks = anc_inverse.shape[0] // BLK, anc_inverse.shape[1] // BLK
    pairs = col_count // 2
    mate = [(k, k + 1 - 2 * (k % 2)) for k in range(col_count)]
    panel = l_store[0]
    near = [panel, lax.ppermute(panel, "col", mate)]
    moved = [
        lax.ppermute(panel, "col", [(k, (k + 2 * step) % col_count) for k in range(col_count)])
        for step in range(1, pairs)
    ]

    table = listed_table(block_lists, block_counts, row_blocks * row_count)
    row_listed = lax.dynamic_slice_in_dim(table, r * row_blocks, row_blocks, axis=1)
    col_listed = lax.dynamic_slice_in_dim(table, c * col_blocks, col_blocks, axis=1)
    row_ints = row_listed.astype(jnp.int32)
    counts = jnp.sum(row_ints, axis=1)
    place = jnp.cumsum(row_ints, axis=1) - 1
    ids = jnp.arange(row_blocks, dtype=jnp.int32)
    entry = jnp.arange(-(-row_blocks // GROUP) * GROUP, dtype=jnp.int32)
    hits = row_listed[:, :, None] & (place[:, :, None] == entry[None, None, :])
    rows = jnp.sum(jnp.where(hits, ids[None, :, None], 0), axis=1).astype(jnp.int32)

    flat = col_listed.reshape(-1)
    slot = jnp.where(flat, jnp.cumsum(flat.astype(jnp.int32)) - 1, -1).astype(jnp.int32)
    per_column = jnp.sum(table.reshape(siblings, col_count, col_blocks).astype(jnp.int32), axis=(0, 2))
    needed = jnp.max(per_column)
    slots_all = -(-siblings * col_blocks // 40) * 40
    grain = slots_all // 40
    caps = [grain * n for n in (19, 21, 23, 25, 28, 32, 40)]
    level = jnp.sum((needed > jnp.array(caps[:-1], jnp.int32)).astype(jnp.int32))

    match = sibling_columns[:, None] == jnp.arange(col_count, dtype=jnp.int32)[None, :]
    owner = jnp.max(
        jnp.where(match, jnp.arange(siblings, dtype=jnp.int32)[:, None], -1), axis=0
    ).astype(jnp.int32)
    mine = sibling_columns == c
    own_listed = jnp.any(row_listed & mine[:, None], axis=0)
    own = l_store[0] * jnp.repeat(own_listed.astype(jnp.float32), BLK)[:, None]
    base = jnp.sum(mine.astype(jnp.float32)) * diag_inv[0]

    slot_rows = slot.reshape(siblings, col_blocks)

    def pick(column):
        sibling = lax.dynamic_index_in_dim(owner, column, keepdims=False)
        at = jnp.maximum(sibling, 0)
        there = sibling >= 0
        return (
            jnp.where(there, slot_rows[at], -1),
            rows[at],
            jnp.where(there, counts[at], 0),
        )

    def tables(columns):
        found = [pick(column) for column in columns]
        return [jnp.stack(part) for part in zip(*found)]

    mate_of = c + 1 - 2 * (c % 2)
    near_columns = [c, mate_of]
    far_columns = []
    for step in range(1, pairs):
        far_columns += [lax.rem(c - 2 * step + col_count, col_count), lax.rem(mate_of - 2 * step + col_count, col_count)]
    partial_value = product(*tables(near_columns), anc_inverse, near, slots_all)
    if moved:
        moved, partial_value = lax.optimization_barrier((moved, partial_value))
        far = [panel for one in moved for panel in (one, lax.ppermute(one, "col", mate))]
        partial_value = product(*tables(far_columns), anc_inverse, far, slots_all, partial_value)

    def branch(place, cap):
        def run(value):
            compact = reduce_rows(value, row_count, cap // grain, grain * BLK, place + 1)
            return expand(slot, owner, compact, siblings, col_blocks)
        return run

    upper, slots = lax.switch(level, [branch(place, cap) for place, cap in enumerate(caps)], partial_value)
    lower, diag = finish(slots, own, base, row_count)
    return upper, lower[None], diag[None]


def solution(mesh):
    return jax.shard_map(
        per_device,
        mesh=mesh,
        in_specs=(P("row", "col"), P("col", "row", None), P("col", None, None), P(), P(), P()),
        out_specs=(P(None, "row", "col"), P("col", "row", None), P("col", None, None)),
        check_vma=False,
    )
```

```python
import functools

import jax
import jax.numpy as jnp
from jax import lax
from jax.experimental import pallas as pl
from jax.experimental.pallas import tpu as pltpu
from jax.sharding import PartitionSpec as P

BLK = 128
GROUP = 4
MESH = pl.DeviceIdType.MESH


def listed_table(block_lists, block_counts, block_total):
    block_ids = jnp.arange(block_total, dtype=jnp.int32)
    valid_entry = jnp.arange(block_lists.shape[1], dtype=jnp.int32)[None, :] < block_counts[:, None]
    entry_hits = (block_lists[:, :, None] == block_ids[None, None, :]) & valid_entry[:, :, None]
    return jnp.any(entry_hits, axis=1)


def product_kernel(members, tile_blocks, col_blocks, row_blocks, joins,
                   slot_ref, rows_ref, count_ref, a_ref, *refs):
    panel_refs, refs = refs[:members], refs[members + joins:]
    out_ref, a_high, a_low, p_high, p_low, stage, sent = refs
    stripe, stripes = pl.program_id(0), pl.num_programs(0)
    group = p_high.shape[3] // BLK
    listed = p_high.shape[1] * group

    @pl.when(stripe == 0)
    def _():
        for member in range(members):
            @pl.loop(0, count_ref[member])
            def _(i):
                rows = pl.ds(pl.multiple_of(rows_ref[member * listed + i] * BLK, BLK), BLK)
                lanes = pl.ds(pl.multiple_of(lax.rem(i, group) * BLK, BLK), BLK)
                value = -panel_refs[member][rows, :].T
                high = value.astype(jnp.bfloat16)
                p_high[member, i // group, :, lanes] = high
                p_low[member, i // group, :, lanes] = (value - high.astype(jnp.float32)).astype(jnp.bfloat16)

            @pl.loop(count_ref[member], (count_ref[member] + group - 1) // group * group)
            def _(i):
                lanes = pl.ds(pl.multiple_of(lax.rem(i, group) * BLK, BLK), BLK)
                zero = jnp.zeros((p_high.shape[2], BLK), jnp.bfloat16)
                p_high[member, i // group, :, lanes] = zero
                p_low[member, i // group, :, lanes] = zero

    @pl.loop(0, row_blocks)
    def _(block):
        rows = pl.ds(pl.multiple_of(block * BLK, BLK), BLK)
        value = a_ref[rows, :]
        high = value.astype(jnp.bfloat16)
        a_high[block] = high
        a_low[block] = (value - high.astype(jnp.float32)).astype(jnp.bfloat16)

    def slot_of(member, block, at):
        return slot_ref[member * col_blocks + at * tile_blocks + block]

    def slot_copy(member, block, slot):
        return pltpu.make_async_copy(
            stage.at[member, :, pl.ds(block * BLK, BLK)],
            out_ref.at[:, pl.ds(pl.multiple_of(slot * BLK, BLK), BLK)],
            sent.at[member, block],
        )

    def settle(member, at):
        for block in range(tile_blocks):
            slot = slot_of(member, block, at)

            @pl.when(slot >= 0)
            def _():
                slot_copy(member, block, slot).wait()

    for member in range(members):
        @pl.when(stripe > 0)
        def _():
            settle(member, stripe - 1)

        stage[member] = jnp.zeros(stage.shape[1:], jnp.float32)

        @pl.loop(0, (count_ref[member] + group - 1) // group)
        def _(k):
            at = [rows_ref[member * listed + k * group + u] for u in range(group)]
            ph, plo = p_high[member, k], p_low[member, k]
            ah, al = [a_high[i] for i in at], [a_low[i] for i in at]
            left = jnp.concatenate([ph, ph, plo], axis=1)
            right = jnp.concatenate(ah + al + ah, axis=0)
            stage[member] += jnp.dot(left, right, preferred_element_type=jnp.float32)

        for block in range(tile_blocks):
            slot = slot_of(member, block, stripe)

            @pl.when(slot >= 0)
            def _():
                slot_copy(member, block, slot).start()

    @pl.when(stripe == stripes - 1)
    def _():
        for member in range(members):
            settle(member, stripe)


def product(slot, rows, counts, anc, panels, slots_all, partial_value=None):
    members = counts.shape[0]
    depth, cells = anc.shape
    width = panels[0].shape[1]
    row_blocks, col_blocks = depth // BLK, cells // BLK
    tile_blocks = next(n for n in (8, 4, 2, 1) if col_blocks % n == 0)
    tile = tile_blocks * BLK
    groups = rows.shape[1] // GROUP
    joins = () if partial_value is None else (partial_value,)
    held = pl.BlockSpec((depth, width), lambda i, *_: (0, 0), pipeline_mode=pl.Buffered(1))
    return pl.pallas_call(
        functools.partial(product_kernel, members, tile_blocks, col_blocks, row_blocks, len(joins)),
        out_shape=jax.ShapeDtypeStruct((width, slots_all * BLK), jnp.float32),
        grid_spec=pltpu.PrefetchScalarGridSpec(
            num_scalar_prefetch=3,
            grid=(col_blocks // tile_blocks,),
            in_specs=[pl.BlockSpec((depth, tile), lambda i, *_: (0, i))]
            + [held] * members
            + [pl.BlockSpec(memory_space=pl.ANY)] * len(joins),
            out_specs=pl.BlockSpec(memory_space=pl.ANY),
            scratch_shapes=[
                pltpu.VMEM((row_blocks, BLK, tile), jnp.bfloat16),
                pltpu.VMEM((row_blocks, BLK, tile), jnp.bfloat16),
                pltpu.VMEM((members, groups, width, GROUP * BLK), jnp.bfloat16),
                pltpu.VMEM((members, groups, width, GROUP * BLK), jnp.bfloat16),
                pltpu.VMEM((members, width, tile), jnp.float32),
                pltpu.SemaphoreType.DMA((members, tile_blocks)),
            ],
        ),
        input_output_aliases={4 + members: 0} if joins else {},
        cost_estimate=pl.CostEstimate(
            flops=2 * 3 * members * depth * cells * width // 2,
            bytes_accessed=4 * depth * cells + 4 * members * width * cells,
            transcendentals=0,
        ),
        compiler_params=pltpu.CompilerParams(
            dimension_semantics=("arbitrary",), vmem_limit_bytes=63 * 1024 * 1000
        ),
    )(slot.reshape(-1), rows.reshape(-1), counts, anc, *panels, *joins)


def expand_kernel(siblings, col_count, col_blocks, slot_ref, owner_ref, compact_ref, upper_ref, slots_ref):
    @pl.loop(0, col_blocks)
    def _(block):
        lanes = pl.ds(pl.multiple_of(block * BLK, BLK), BLK)
        for sibling in range(siblings):
            slot = slot_ref[sibling * col_blocks + block]
            at = pl.ds(pl.multiple_of(jnp.maximum(slot, 0) * BLK, BLK), BLK)
            value = compact_ref[:, at]
            upper_ref[sibling, :, lanes] = jnp.where(slot >= 0, value, jnp.zeros_like(value))

    for column in range(col_count):
        sibling = owner_ref[column]
        value = upper_ref[jnp.maximum(sibling, 0)]
        slots_ref[column] = jnp.where(sibling >= 0, value, jnp.zeros_like(value))


def expand(slot, owner, compact, siblings, col_blocks):
    col_count = owner.shape[0]
    rows = compact.shape[0]
    return pl.pallas_call(
        functools.partial(expand_kernel, siblings, col_count, col_blocks),
        out_shape=(
            jax.ShapeDtypeStruct((siblings, rows, col_blocks * BLK), jnp.float32),
            jax.ShapeDtypeStruct((col_count, rows, col_blocks * BLK), jnp.float32),
        ),
        in_specs=[pl.BlockSpec(memory_space=pltpu.SMEM)] * 2 + [pl.BlockSpec(memory_space=pltpu.VMEM)],
        out_specs=(pl.BlockSpec(memory_space=pltpu.VMEM),) * 2,
    )(slot, owner, compact)


def reduce_kernel(line, flat_first, chunks,
                  partial_ref, out_ref,
                  mine, flat_mine, pair_buf, up_buf, down_buf, flat_up, flat_down, flat_sum, flat_pair,
                  mine_sem, flat_sem, pair_send, pair_recv, up_send, up_recv, down_send, down_recv, flat_send, flat_recv):
    r, c = lax.axis_index("row"), lax.axis_index("col")
    z, y = r // 2, lax.rem(r, 2)
    other = 1 - y
    width = out_ref.shape[1] // chunks
    last, lag = line - 1, 2
    late = chunks - flat_first

    def lanes(chunk):
        return pl.ds(pl.multiple_of(chunk * width, width), width)

    def flat_load(k):
        return pltpu.make_async_copy(partial_ref.at[:, :, :, lanes(k)], flat_mine.at[k], flat_sem.at[k])

    def pair_load(k):
        return pltpu.make_async_copy(
            partial_ref.at[:, y, :, lanes(k + flat_first)], mine.at[k], mine_sem.at[k]
        )

    @pl.loop(0, flat_first)
    def _(k):
        flat_load(k).start()

    barrier = pltpu.get_barrier_semaphore()
    pl.semaphore_signal(barrier, inc=1, device_id=(z * 2 + other, c), device_id_type=MESH)

    @pl.when(z > 0)
    def _():
        pl.semaphore_signal(barrier, inc=1, device_id=(r - 2, c), device_id_type=MESH)

    @pl.when(z < last)
    def _():
        pl.semaphore_signal(barrier, inc=1, device_id=(r + 2, c), device_id_type=MESH)

    pl.semaphore_wait(barrier, 1 + (z > 0).astype(jnp.int32) + (z < last).astype(jnp.int32))

    def pair_copy(k):
        return pltpu.make_async_remote_copy(
            src_ref=partial_ref.at[:, other, :, lanes(k + flat_first)],
            dst_ref=pair_buf.at[k],
            send_sem=pair_send.at[k],
            recv_sem=pair_recv.at[k],
            device_id=(z * 2 + other, c),
            device_id_type=MESH,
        )

    def flat_copy(k):
        return pltpu.make_async_remote_copy(
            src_ref=flat_sum.at[k, other],
            dst_ref=flat_pair.at[k],
            send_sem=flat_send.at[k],
            recv_sem=flat_recv.at[k],
            device_id=(z * 2 + other, c),
            device_id_type=MESH,
        )

    def up_copy(buf, k, slot, at):
        return pltpu.make_async_remote_copy(
            src_ref=buf.at[k, pl.ds(at, last - at)],
            dst_ref=buf.at[k, pl.ds(at, last - at)],
            send_sem=up_send.at[slot],
            recv_sem=up_recv.at[slot],
            device_id=(r + 2, c),
            device_id_type=MESH,
        )

    def down_copy(buf, k, slot, at):
        return pltpu.make_async_remote_copy(
            src_ref=buf.at[k, pl.ds(0, at)],
            dst_ref=buf.at[k, pl.ds(0, at)],
            send_sem=down_send.at[slot],
            recv_sem=down_recv.at[slot],
            device_id=(r - 2, c),
            device_id_type=MESH,
        )

    def flat(k):
        def own(place):
            return flat_mine[k, place]

        def finish(value):
            flat_sum[k] = value
            flat_copy(k).start()

        return flat_up, flat_down, k, own, finish

    def paired(k):
        k = k - flat_first

        def own(place):
            return pair_buf[k, place]

        def finish(value):
            out_ref[:, lanes(k + flat_first)] = value

        return up_buf, down_buf, k, own, finish

    def total(at, up, down, k, own, finish):
        value = own(at)
        if at > 0:
            value = value + up[k, at - 1]
        if at < last:
            value = value + down[k, at]
        finish(value)

    def pass_up(at, slot, up, down, k, own, finish):
        if at > 0:
            up_copy(up, k, slot, at - 1).wait_recv()
        for place in range(at + 1, line):
            if at > 0:
                up[k, place - 1] = up[k, place - 1] + own(place)
            else:
                up[k, place - 1] = own(place)
        if at < last:
            up_copy(up, k, slot, at).start()
        if 2 * at > last:
            total(at, up, down, k, own, finish)

    def pass_down(at, slot, up, down, k, own, finish):
        if at < last:
            down_copy(down, k, slot, at + 1).wait_recv()
        for place in range(at):
            if at < last:
                down[k, place] = down[k, place] + own(place)
            else:
                down[k, place] = own(place)
        if at > 0:
            down_copy(down, k, slot, at).start()
        if 2 * at <= last:
            total(at, up, down, k, own, finish)

    def either(step, at, slot):
        @pl.when((slot >= 0) & (slot < flat_first))
        def _():
            step(at, slot, *flat(slot))

        @pl.when((slot >= flat_first) & (slot < chunks))
        def _():
            step(at, slot, *paired(slot))

    @pl.loop(0, late)
    def _(k):
        pair_copy(k).start()
        pair_load(k).start()

    @pl.loop(0, chunks + lag * last)
    def _(i):
        @pl.when(i < flat_first)
        def _():
            flat_load(i).wait()

        @pl.when((i >= flat_first) & (i < chunks))
        def _():
            k = i - flat_first
            pair_load(k).wait()
            pair_copy(k).wait_recv()
            for place in range(line):
                pair_buf[k, place] = pair_buf[k, place] + mine[k, place]

        for at in range(line):
            @pl.when(z == at)
            def _():
                either(pass_up, at, i - lag * at)
                either(pass_down, at, i - lag * (last - at))

    @pl.loop(0, flat_first)
    def _(k):
        flat_copy(k).wait_recv()
        out_ref[:, lanes(k)] = flat_sum[k, y] + flat_pair[k]

    @pl.loop(0, late)
    def _(k):
        pair_copy(k).wait_send()

    @pl.loop(0, flat_first)
    def _(k):
        flat_copy(k).wait_send()

    for at in range(line):
        @pl.when(z == at)
        def _():
            for buf, start, stop, shift in ((flat_up, 0, flat_first, 0), (up_buf, 0, late, flat_first)):
                if at < last:
                    @pl.loop(start, stop)
                    def _(k):
                        up_copy(buf, k, k + shift, at).wait_send()
            for buf, start, stop, shift in ((flat_down, 0, flat_first, 0), (down_buf, 0, late, flat_first)):
                if at > 0:
                    @pl.loop(start, stop)
                    def _(k):
                        down_copy(buf, k, k + shift, at).wait_send()


def reduce_rows(value, row_count, chunks, lanes, collective):
    width, columns = value.shape
    line, slice_rows = row_count // 2, width // row_count
    flat_first = (chunks + 3) // 6
    late = chunks - flat_first
    vmem = pl.BlockSpec(memory_space=pltpu.VMEM)
    dma = pltpu.SemaphoreType.DMA
    return pl.pallas_call(
        functools.partial(reduce_kernel, line, flat_first, chunks),
        out_shape=jax.ShapeDtypeStruct((slice_rows, chunks * lanes), jnp.float32),
        in_specs=[pl.BlockSpec(memory_space=pl.ANY)],
        out_specs=vmem,
        scratch_shapes=[
            pltpu.VMEM((late, line, slice_rows, lanes), jnp.float32),
            pltpu.VMEM((flat_first, line, 2, slice_rows, lanes), jnp.float32),
            pltpu.VMEM((late, line, slice_rows, lanes), jnp.float32),
            pltpu.VMEM((late, line - 1, slice_rows, lanes), jnp.float32),
            pltpu.VMEM((late, line - 1, slice_rows, lanes), jnp.float32),
            pltpu.VMEM((flat_first, line - 1, 2, slice_rows, lanes), jnp.float32),
            pltpu.VMEM((flat_first, line - 1, 2, slice_rows, lanes), jnp.float32),
            pltpu.VMEM((flat_first, 2, slice_rows, lanes), jnp.float32),
            pltpu.VMEM((flat_first, slice_rows, lanes), jnp.float32),
            dma((late,)),
            dma((flat_first,)),
            dma((late,)),
            dma((late,)),
            dma((chunks,)),
            dma((chunks,)),
            dma((chunks,)),
            dma((chunks,)),
            dma((flat_first,)),
            dma((flat_first,)),
        ],
        compiler_params=pltpu.CompilerParams(
            collective_id=collective, has_side_effects=True, vmem_limit_bytes=63 * 1024 * 1000
        ),
    )(value.reshape(line, 2, slice_rows, columns))


def finish_kernel(row_count, col_count,
                  owner_ref, slots_ref, own_ref, base_ref, lower_ref, diag_ref,
                  stage, picked, inner, part, reduced, total,
                  stage_send, stage_recv, send_sem, recv_sem, part_send, part_recv, total_send, total_recv):
    r, c = lax.axis_index("row"), lax.axis_index("col")
    ratio = row_count // col_count
    slice_rows, cells = picked.shape[1], picked.shape[2]

    barrier = pltpu.get_barrier_semaphore()
    for peer in range(row_count):
        @pl.when(peer != r)
        def _():
            pl.semaphore_signal(barrier, inc=1, device_id=(peer, c), device_id_type=MESH)
    for peer in range(col_count):
        @pl.when(peer != c)
        def _():
            pl.semaphore_signal(barrier, inc=1, device_id=(r, peer), device_id_type=MESH)
    pl.semaphore_wait(barrier, row_count + col_count - 2)

    def near(offset):
        pair = lax.rem(c // 2 + offset // 2, col_count // 2)
        return pair * 2 + lax.rem(lax.rem(c, 2) + offset % 2, 2)

    def piece(k):
        return pl.ds(k * cells, cells)

    def column_copy(target, k):
        return pltpu.make_async_remote_copy(
            src_ref=slots_ref.at[target, :, piece(k)],
            dst_ref=stage.at[c, :, piece(k)],
            send_sem=stage_send.at[target, k],
            recv_sem=stage_recv.at[c, k],
            device_id=(r, target),
            device_id_type=MESH,
        )

    def column_arrived(source, k):
        return pltpu.make_async_remote_copy(
            src_ref=slots_ref.at[source, :, piece(k)],
            dst_ref=stage.at[source, :, piece(k)],
            send_sem=stage_send.at[source, k],
            recv_sem=stage_recv.at[source, k],
            device_id=(r, source),
            device_id_type=MESH,
        )

    def row_copy(held, source, k):
        target = source * ratio + k
        return pltpu.make_async_remote_copy(
            src_ref=held.at[source, :, piece(k)],
            dst_ref=picked.at[r],
            send_sem=send_sem.at[target],
            recv_sem=recv_sem.at[r],
            device_id=(target, c),
            device_id_type=MESH,
        )

    def row_local(held, source, k):
        return pltpu.make_async_copy(
            held.at[source, :, piece(k)], picked.at[r], recv_sem.at[r]
        )

    def row_arrived(source):
        return pltpu.make_async_remote_copy(
            src_ref=picked.at[source],
            dst_ref=picked.at[source],
            send_sem=send_sem.at[source],
            recv_sem=recv_sem.at[source],
            device_id=(source, c),
            device_id_type=MESH,
        )

    for offset in (*range(2, col_count), 1):
        for k in range(ratio):
            column_copy(near(offset), k).start()
    for offset in range(col_count):
        source = near(offset)
        held = stage if offset else slots_ref
        for k in range(ratio):
            if offset:
                column_arrived(source, k).wait_recv()

            @pl.when(source * ratio + k == r)
            def _():
                row_local(held, source, k).start()

            @pl.when(source * ratio + k != r)
            def _():
                row_copy(held, source, k).start()

    def part_copy(peer):
        return pltpu.make_async_remote_copy(
            src_ref=inner.at[pl.ds(pl.multiple_of(peer * slice_rows, slice_rows), slice_rows), :],
            dst_ref=part.at[r],
            send_sem=part_send.at[peer],
            recv_sem=part_recv.at[r],
            device_id=(peer, c),
            device_id_type=MESH,
        )

    def part_arrived(peer):
        return pltpu.make_async_remote_copy(
            src_ref=inner.at[pl.ds(0, slice_rows), :],
            dst_ref=part.at[peer],
            send_sem=part_send.at[peer],
            recv_sem=part_recv.at[peer],
            device_id=(peer, c),
            device_id_type=MESH,
        )

    def total_copy(peer):
        return pltpu.make_async_remote_copy(
            src_ref=reduced,
            dst_ref=total.at[r],
            send_sem=total_send.at[peer],
            recv_sem=total_recv.at[r],
            device_id=(peer, c),
            device_id_type=MESH,
        )

    def total_arrived(peer):
        return pltpu.make_async_remote_copy(
            src_ref=reduced,
            dst_ref=total.at[peer],
            send_sem=total_send.at[peer],
            recv_sem=total_recv.at[peer],
            device_id=(peer, c),
            device_id_type=MESH,
        )

    def peers(action):
        for peer in range(row_count):
            @pl.when(peer != r)
            def _():
                action(peer)

    step = 256 if cells % 256 == 0 else BLK
    half = row_count // 2
    group_rows = half * slice_rows
    inner[...] = jnp.zeros_like(inner)

    for turn in range(2):
        first = lax.rem(r // half + turn, 2) * half
        for at in range(half):
            @pl.when(first + at != r)
            def _():
                row_arrived(first + at).wait_recv()

            @pl.when(first + at == r)
            def _():
                for offset in range(col_count):
                    source = near(offset)
                    for k in range(ratio):
                        @pl.when(source * ratio + k == r)
                        def _():
                            row_local(stage if offset else slots_ref, source, k).wait()

        group = pl.ds(pl.multiple_of(first * slice_rows, group_rows), group_rows)

        @pl.loop(0, cells // step)
        def _(i):
            at = pl.ds(pl.multiple_of(i * step, step), step)
            block = picked[pl.ds(first, half), :, at].reshape(group_rows, step)
            inner[group, :] += jnp.dot(
                block, own_ref[at, :], precision=lax.Precision.HIGHEST, preferred_element_type=jnp.float32
            )

        for at in range(half):
            @pl.when(first + at != r)
            def _():
                part_copy(first + at).start()

    peers(lambda peer: part_arrived(peer).wait_recv())
    mine = inner[pl.ds(pl.multiple_of(r * slice_rows, slice_rows), slice_rows), :]
    for peer in range(row_count):
        @pl.when(peer == r)
        def _():
            part[peer] = mine
    value = part[0]
    for peer in range(1, row_count):
        value = value + part[peer]
    reduced[...] = value
    peers(lambda peer: total_copy(peer).start())

    @pl.loop(0, cells // step)
    def _(i):
        at = pl.ds(pl.multiple_of(i * step, step), step)
        block = picked[:, :, at].reshape(row_count * slice_rows, step)
        lower_ref[at, :] = block.T

    peers(lambda peer: total_arrived(peer).wait_recv())
    for peer in range(row_count):
        @pl.when(peer == r)
        def _():
            total[peer] = reduced[...]
    base = jnp.where(owner_ref[c] >= 0, base_ref[...], jnp.zeros_like(base_ref))
    diag_ref[...] = base - total[...].reshape(diag_ref.shape)

    for offset in range(col_count):
        source = near(offset)
        held = stage if offset else slots_ref
        if offset:
            for k in range(ratio):
                column_copy(source, k).wait_send()
        for k in range(ratio):
            @pl.when(source * ratio + k != r)
            def _():
                row_copy(held, source, k).wait_send()
    peers(lambda peer: part_copy(peer).wait_send())
    peers(lambda peer: total_copy(peer).wait_send())


def finish(owner, slots, own, base, row_count):
    col_count, slice_rows, _ = slots.shape
    cells, width = own.shape
    vmem = pl.BlockSpec(memory_space=pltpu.VMEM)
    dma = pltpu.SemaphoreType.DMA
    return pl.pallas_call(
        functools.partial(finish_kernel, row_count, col_count),
        out_shape=(
            jax.ShapeDtypeStruct((cells, width), jnp.float32),
            jax.ShapeDtypeStruct((width, width), jnp.float32),
        ),
        in_specs=[pl.BlockSpec(memory_space=pltpu.SMEM)] + [vmem] * 3,
        out_specs=(vmem, vmem),
        scratch_shapes=[
            pltpu.VMEM(slots.shape, jnp.float32),
            pltpu.VMEM((row_count, slice_rows, cells), jnp.float32),
            pltpu.VMEM((width, width), jnp.float32),
            pltpu.VMEM((row_count, slice_rows, width), jnp.float32),
            pltpu.VMEM((slice_rows, width), jnp.float32),
            pltpu.VMEM((row_count, slice_rows, width), jnp.float32),
            dma((col_count, row_count // col_count)),
            dma((col_count, row_count // col_count)),
            dma((row_count,)),
            dma((row_count,)),
            dma((row_count,)),
            dma((row_count,)),
            dma((row_count,)),
            dma((row_count,)),
        ],
        compiler_params=pltpu.CompilerParams(collective_id=0, has_side_effects=True),
    )(owner, slots, own, base)


def per_device(anc_inverse, l_store, diag_inv, block_lists, block_counts, sibling_columns):
    siblings = block_lists.shape[0]
    row_count, col_count = lax.axis_size("row"), lax.axis_size("col")
    r, c = lax.axis_index("row"), lax.axis_index("col")
    row_blocks, col_blocks = anc_inverse.shape[0] // BLK, anc_inverse.shape[1] // BLK
    pairs = col_count // 2
    mate = [(k, k + 1 - 2 * (k % 2)) for k in range(col_count)]
    panel = l_store[0]
    near = [panel, lax.ppermute(panel, "col", mate)]
    moved = [
        lax.ppermute(panel, "col", [(k, (k + 2 * step) % col_count) for k in range(col_count)])
        for step in range(1, pairs)
    ]

    table = listed_table(block_lists, block_counts, row_blocks * row_count)
    row_listed = lax.dynamic_slice_in_dim(table, r * row_blocks, row_blocks, axis=1)
    col_listed = lax.dynamic_slice_in_dim(table, c * col_blocks, col_blocks, axis=1)
    row_ints = row_listed.astype(jnp.int32)
    counts = jnp.sum(row_ints, axis=1)
    place = jnp.cumsum(row_ints, axis=1) - 1
    ids = jnp.arange(row_blocks, dtype=jnp.int32)
    entry = jnp.arange(-(-row_blocks // GROUP) * GROUP, dtype=jnp.int32)
    hits = row_listed[:, :, None] & (place[:, :, None] == entry[None, None, :])
    rows = jnp.sum(jnp.where(hits, ids[None, :, None], 0), axis=1).astype(jnp.int32)

    flat = col_listed.reshape(-1)
    slot = jnp.where(flat, jnp.cumsum(flat.astype(jnp.int32)) - 1, -1).astype(jnp.int32)
    per_column = jnp.sum(table.reshape(siblings, col_count, col_blocks).astype(jnp.int32), axis=(0, 2))
    needed = jnp.max(per_column)
    slots_all = -(-siblings * col_blocks // 40) * 40
    grain = slots_all // 40
    caps = [grain * n for n in (19, 21, 23, 25, 28, 32, 40)]
    level = jnp.sum((needed > jnp.array(caps[:-1], jnp.int32)).astype(jnp.int32))

    match = sibling_columns[:, None] == jnp.arange(col_count, dtype=jnp.int32)[None, :]
    owner = jnp.max(
        jnp.where(match, jnp.arange(siblings, dtype=jnp.int32)[:, None], -1), axis=0
    ).astype(jnp.int32)
    slot_rows = slot.reshape(siblings, col_blocks)

    def pick(column):
        sibling = lax.dynamic_index_in_dim(owner, column, keepdims=False)
        at = jnp.maximum(sibling, 0)
        there = sibling >= 0
        return (
            jnp.where(there, slot_rows[at], -1),
            rows[at],
            jnp.where(there, counts[at], 0),
        )

    def tables(columns):
        found = [pick(column) for column in columns]
        return [jnp.stack(part) for part in zip(*found)]

    mate_of = c + 1 - 2 * (c % 2)
    near_columns = [c, mate_of]
    far_columns = []
    for step in range(1, pairs):
        far_columns += [lax.rem(c - 2 * step + col_count, col_count), lax.rem(mate_of - 2 * step + col_count, col_count)]
    partial_value = product(*tables(near_columns), anc_inverse, near, slots_all)
    if moved:
        moved, partial_value = lax.optimization_barrier((moved, partial_value))
        far = [panel for one in moved for panel in (one, lax.ppermute(one, "col", mate))]
        partial_value = product(*tables(far_columns), anc_inverse, far, slots_all, partial_value)

    def branch(place, cap):
        def run(value):
            compact = reduce_rows(value, row_count, cap // grain, grain * BLK, place + 1)
            return expand(slot, owner, compact, siblings, col_blocks)
        return run

    upper, slots = lax.switch(level, [branch(place, cap) for place, cap in enumerate(caps)], partial_value)
    lower, diag = finish(owner, slots, l_store[0], diag_inv[0], row_count)
    return upper, lower[None], diag[None]


def solution(mesh):
    return jax.shard_map(
        per_device,
        mesh=mesh,
        in_specs=(P("row", "col"), P("col", "row", None), P("col", None, None), P(), P(), P()),
        out_specs=(P(None, "row", "col"), P("col", "row", None), P("col", None, None)),
        check_vma=False,
    )
```

```python
import functools

import jax
import jax.numpy as jnp
from jax import lax
from jax.experimental import pallas as pl
from jax.experimental.pallas import tpu as pltpu
from jax.sharding import PartitionSpec as P

BLK = 128
GROUP = 4
MESH = pl.DeviceIdType.MESH


def listed_table(block_lists, block_counts, block_total):
    block_ids = jnp.arange(block_total, dtype=jnp.int32)
    valid_entry = jnp.arange(block_lists.shape[1], dtype=jnp.int32)[None, :] < block_counts[:, None]
    entry_hits = (block_lists[:, :, None] == block_ids[None, None, :]) & valid_entry[:, :, None]
    return jnp.any(entry_hits, axis=1)


def product_kernel(members, tile_blocks, col_blocks, row_blocks, joins, saved,
                   slot_ref, rows_ref, count_ref, a_ref, *refs):
    panel_refs, refs = refs[:members], refs[members:]
    if joins:
        _, kept_high, kept_low, out_ref, highs, lows, p_high, p_low, stage, sent, kept = refs
    else:
        out_ref, kept_high, kept_low, highs, lows, p_high, p_low, stage, sent, kept = refs
    step, stripes = pl.program_id(0), pl.num_programs(0)
    split = stripes - saved

    def stripe_at(at):
        return jnp.where(at < split, saved + at, at - split) if joins else at

    stripe = stripe_at(step)
    side = lax.rem(step, 2) if joins else 0
    a_high, a_low = highs.at[side], lows.at[side]
    group = p_high.shape[3] // BLK
    listed = p_high.shape[1] * group

    def keep_copies(at):
        return (
            pltpu.make_async_copy(highs.at[0], kept_high.at[at], kept.at[0, 0]),
            pltpu.make_async_copy(lows.at[0], kept_low.at[at], kept.at[0, 1]),
        )

    def load_copies(at):
        to = lax.rem(at, 2)
        return (
            pltpu.make_async_copy(kept_high.at[at - split], highs.at[to], kept.at[to, 0]),
            pltpu.make_async_copy(kept_low.at[at - split], lows.at[to], kept.at[to, 1]),
        )

    @pl.when(step == 0)
    def _():
        for member in range(members):
            @pl.loop(0, count_ref[member])
            def _(i):
                rows = pl.ds(pl.multiple_of(rows_ref[member * listed + i] * BLK, BLK), BLK)
                lanes = pl.ds(pl.multiple_of(lax.rem(i, group) * BLK, BLK), BLK)
                value = -panel_refs[member][rows, :].T
                high = value.astype(jnp.bfloat16)
                p_high[member, i // group, :, lanes] = high
                p_low[member, i // group, :, lanes] = (value - high.astype(jnp.float32)).astype(jnp.bfloat16)

            @pl.loop(count_ref[member], (count_ref[member] + group - 1) // group * group)
            def _(i):
                lanes = pl.ds(pl.multiple_of(lax.rem(i, group) * BLK, BLK), BLK)
                zero = jnp.zeros((p_high.shape[2], BLK), jnp.bfloat16)
                p_high[member, i // group, :, lanes] = zero
                p_low[member, i // group, :, lanes] = zero

    def halve():
        @pl.loop(0, row_blocks)
        def _(block):
            rows = pl.ds(pl.multiple_of(block * BLK, BLK), BLK)
            value = a_ref[rows, :]
            high = value.astype(jnp.bfloat16)
            a_high[block] = high
            a_low[block] = (value - high.astype(jnp.float32)).astype(jnp.bfloat16)

    if joins:
        @pl.when((step + 1 >= split) & (step + 1 < stripes))
        def _():
            for copy in load_copies(step + 1):
                copy.start()

        pl.when(step < split)(halve)

        @pl.when(step >= split)
        def _():
            for copy in load_copies(step):
                copy.wait()
    else:
        @pl.when((step > 0) & (step <= saved))
        def _():
            for copy in keep_copies(step - 1):
                copy.wait()

        halve()

        @pl.when(step < saved)
        def _():
            for copy in keep_copies(step):
                copy.start()

    def slot_of(member, block, at):
        return slot_ref[member * col_blocks + at * tile_blocks + block]

    def slot_copy(member, block, slot):
        return pltpu.make_async_copy(
            stage.at[member, :, pl.ds(block * BLK, BLK)],
            out_ref.at[:, pl.ds(pl.multiple_of(slot * BLK, BLK), BLK)],
            sent.at[member, block],
        )

    def settle(member, at):
        for block in range(tile_blocks):
            slot = slot_of(member, block, at)

            @pl.when(slot >= 0)
            def _():
                slot_copy(member, block, slot).wait()

    for member in range(members):
        @pl.when(step > 0)
        def _():
            settle(member, stripe_at(step - 1))

        stage[member] = jnp.zeros(stage.shape[1:], jnp.float32)

        @pl.loop(0, (count_ref[member] + group - 1) // group)
        def _(k):
            at = [rows_ref[member * listed + k * group + u] for u in range(group)]
            ph, plo = p_high[member, k], p_low[member, k]
            ah, al = [a_high[i] for i in at], [a_low[i] for i in at]
            left = jnp.concatenate([ph, ph, plo], axis=1)
            right = jnp.concatenate(ah + al + ah, axis=0)
            stage[member] += jnp.dot(left, right, preferred_element_type=jnp.float32)

        for block in range(tile_blocks):
            slot = slot_of(member, block, stripe)

            @pl.when(slot >= 0)
            def _():
                slot_copy(member, block, slot).start()

    @pl.when(step == stripes - 1)
    def _():
        for member in range(members):
            settle(member, stripe)


def product(slot, rows, counts, anc, panels, slots_all, before=None):
    members = counts.shape[0]
    depth, cells = anc.shape
    width = panels[0].shape[1]
    row_blocks, col_blocks = depth // BLK, cells // BLK
    tile_blocks = next(n for n in (8, 4, 2, 1) if col_blocks % n == 0)
    tile = tile_blocks * BLK
    groups = rows.shape[1] // GROUP
    joins = () if before is None else tuple(before)
    stripes = col_blocks // tile_blocks
    saved = stripes - 1
    any_space = pl.BlockSpec(memory_space=pl.ANY)
    kept = jax.ShapeDtypeStruct((saved, row_blocks, BLK, tile), jnp.bfloat16)
    value = jax.ShapeDtypeStruct((width, slots_all * BLK), jnp.float32)
    sides = 2 if joins else 1
    first = saved if joins else 0
    held = pl.BlockSpec((depth, width), lambda i, *_: (0, 0), pipeline_mode=pl.Buffered(1))
    return pl.pallas_call(
        functools.partial(product_kernel, members, tile_blocks, col_blocks, row_blocks, len(joins), saved),
        out_shape=value if joins else (value, kept, kept),
        grid_spec=pltpu.PrefetchScalarGridSpec(
            num_scalar_prefetch=3,
            grid=(stripes,),
            in_specs=[pl.BlockSpec((depth, tile), lambda i, *_: (0, jnp.minimum(first + i, stripes - 1)))]
            + [held] * members
            + [any_space] * len(joins),
            out_specs=any_space if joins else (any_space,) * 3,
            scratch_shapes=[
                pltpu.VMEM((sides, row_blocks, BLK, tile), jnp.bfloat16),
                pltpu.VMEM((sides, row_blocks, BLK, tile), jnp.bfloat16),
                pltpu.VMEM((members, groups, width, GROUP * BLK), jnp.bfloat16),
                pltpu.VMEM((members, groups, width, GROUP * BLK), jnp.bfloat16),
                pltpu.VMEM((members, width, tile), jnp.float32),
                pltpu.SemaphoreType.DMA((members, tile_blocks)),
                pltpu.SemaphoreType.DMA((sides, 2)),
            ],
        ),
        input_output_aliases={4 + members: 0} if joins else {},
        cost_estimate=pl.CostEstimate(
            flops=2 * 3 * members * depth * cells * width // 2,
            bytes_accessed=4 * depth * cells + 4 * members * width * cells,
            transcendentals=0,
        ),
        compiler_params=pltpu.CompilerParams(
            dimension_semantics=("arbitrary",), vmem_limit_bytes=63 * 1024 * 1000
        ),
    )(slot.reshape(-1), rows.reshape(-1), counts, anc, *panels, *joins)


def expand_kernel(siblings, col_count, col_blocks, slot_ref, owner_ref, compact_ref, upper_ref, slots_ref):
    @pl.loop(0, col_blocks)
    def _(block):
        lanes = pl.ds(pl.multiple_of(block * BLK, BLK), BLK)
        for sibling in range(siblings):
            slot = slot_ref[sibling * col_blocks + block]
            at = pl.ds(pl.multiple_of(jnp.maximum(slot, 0) * BLK, BLK), BLK)
            value = compact_ref[:, at]
            upper_ref[sibling, :, lanes] = jnp.where(slot >= 0, value, jnp.zeros_like(value))

    for column in range(col_count):
        sibling = owner_ref[column]
        value = upper_ref[jnp.maximum(sibling, 0)]
        slots_ref[column] = jnp.where(sibling >= 0, value, jnp.zeros_like(value))


def expand(slot, owner, compact, siblings, col_blocks):
    col_count = owner.shape[0]
    rows = compact.shape[0]
    return pl.pallas_call(
        functools.partial(expand_kernel, siblings, col_count, col_blocks),
        out_shape=(
            jax.ShapeDtypeStruct((siblings, rows, col_blocks * BLK), jnp.float32),
            jax.ShapeDtypeStruct((col_count, rows, col_blocks * BLK), jnp.float32),
        ),
        in_specs=[pl.BlockSpec(memory_space=pltpu.SMEM)] * 2 + [pl.BlockSpec(memory_space=pltpu.VMEM)],
        out_specs=(pl.BlockSpec(memory_space=pltpu.VMEM),) * 2,
    )(slot, owner, compact)


def reduce_kernel(line, flat_first, chunks,
                  partial_ref, out_ref,
                  mine, flat_mine, pair_buf, up_buf, down_buf, flat_up, flat_down, flat_sum, flat_pair,
                  mine_sem, flat_sem, pair_send, pair_recv, up_send, up_recv, down_send, down_recv, flat_send, flat_recv):
    r, c = lax.axis_index("row"), lax.axis_index("col")
    z, y = r // 2, lax.rem(r, 2)
    other = 1 - y
    width = out_ref.shape[1] // chunks
    last, lag = line - 1, 2
    late = chunks - flat_first

    def lanes(chunk):
        return pl.ds(pl.multiple_of(chunk * width, width), width)

    def flat_load(k):
        return pltpu.make_async_copy(partial_ref.at[:, :, :, lanes(k)], flat_mine.at[k], flat_sem.at[k])

    def pair_load(k):
        return pltpu.make_async_copy(
            partial_ref.at[:, y, :, lanes(k + flat_first)], mine.at[k], mine_sem.at[k]
        )

    @pl.loop(0, flat_first)
    def _(k):
        flat_load(k).start()

    barrier = pltpu.get_barrier_semaphore()
    pl.semaphore_signal(barrier, inc=1, device_id=(z * 2 + other, c), device_id_type=MESH)

    @pl.when(z > 0)
    def _():
        pl.semaphore_signal(barrier, inc=1, device_id=(r - 2, c), device_id_type=MESH)

    @pl.when(z < last)
    def _():
        pl.semaphore_signal(barrier, inc=1, device_id=(r + 2, c), device_id_type=MESH)

    pl.semaphore_wait(barrier, 1 + (z > 0).astype(jnp.int32) + (z < last).astype(jnp.int32))

    def pair_copy(k):
        return pltpu.make_async_remote_copy(
            src_ref=partial_ref.at[:, other, :, lanes(k + flat_first)],
            dst_ref=pair_buf.at[k],
            send_sem=pair_send.at[k],
            recv_sem=pair_recv.at[k],
            device_id=(z * 2 + other, c),
            device_id_type=MESH,
        )

    def flat_copy(k):
        return pltpu.make_async_remote_copy(
            src_ref=flat_sum.at[k, other],
            dst_ref=flat_pair.at[k],
            send_sem=flat_send.at[k],
            recv_sem=flat_recv.at[k],
            device_id=(z * 2 + other, c),
            device_id_type=MESH,
        )

    def up_copy(buf, k, slot, at):
        return pltpu.make_async_remote_copy(
            src_ref=buf.at[k, pl.ds(at, last - at)],
            dst_ref=buf.at[k, pl.ds(at, last - at)],
            send_sem=up_send.at[slot],
            recv_sem=up_recv.at[slot],
            device_id=(r + 2, c),
            device_id_type=MESH,
        )

    def down_copy(buf, k, slot, at):
        return pltpu.make_async_remote_copy(
            src_ref=buf.at[k, pl.ds(0, at)],
            dst_ref=buf.at[k, pl.ds(0, at)],
            send_sem=down_send.at[slot],
            recv_sem=down_recv.at[slot],
            device_id=(r - 2, c),
            device_id_type=MESH,
        )

    def flat(k):
        def own(place):
            return flat_mine[k, place]

        def finish(value):
            flat_sum[k] = value
            flat_copy(k).start()

        return flat_up, flat_down, k, own, finish

    def paired(k):
        k = k - flat_first

        def own(place):
            return pair_buf[k, place]

        def finish(value):
            out_ref[:, lanes(k + flat_first)] = value

        return up_buf, down_buf, k, own, finish

    def total(at, up, down, k, own, finish):
        value = own(at)
        if at > 0:
            value = value + up[k, at - 1]
        if at < last:
            value = value + down[k, at]
        finish(value)

    def pass_up(at, slot, up, down, k, own, finish):
        if at > 0:
            up_copy(up, k, slot, at - 1).wait_recv()
        for place in range(at + 1, line):
            if at > 0:
                up[k, place - 1] = up[k, place - 1] + own(place)
            else:
                up[k, place - 1] = own(place)
        if at < last:
            up_copy(up, k, slot, at).start()
        if 2 * at > last:
            total(at, up, down, k, own, finish)

    def pass_down(at, slot, up, down, k, own, finish):
        if at < last:
            down_copy(down, k, slot, at + 1).wait_recv()
        for place in range(at):
            if at < last:
                down[k, place] = down[k, place] + own(place)
            else:
                down[k, place] = own(place)
        if at > 0:
            down_copy(down, k, slot, at).start()
        if 2 * at <= last:
            total(at, up, down, k, own, finish)

    def either(step, at, slot):
        @pl.when((slot >= 0) & (slot < flat_first))
        def _():
            step(at, slot, *flat(slot))

        @pl.when((slot >= flat_first) & (slot < chunks))
        def _():
            step(at, slot, *paired(slot))

    @pl.loop(0, late)
    def _(k):
        pair_copy(k).start()
        pair_load(k).start()

    @pl.loop(0, chunks + lag * last)
    def _(i):
        @pl.when(i < flat_first)
        def _():
            flat_load(i).wait()

        @pl.when((i >= flat_first) & (i < chunks))
        def _():
            k = i - flat_first
            pair_load(k).wait()
            pair_copy(k).wait_recv()
            for place in range(line):
                pair_buf[k, place] = pair_buf[k, place] + mine[k, place]

        for at in range(line):
            @pl.when(z == at)
            def _():
                either(pass_up, at, i - lag * at)
                either(pass_down, at, i - lag * (last - at))

    @pl.loop(0, flat_first)
    def _(k):
        flat_copy(k).wait_recv()
        out_ref[:, lanes(k)] = flat_sum[k, y] + flat_pair[k]

    @pl.loop(0, late)
    def _(k):
        pair_copy(k).wait_send()

    @pl.loop(0, flat_first)
    def _(k):
        flat_copy(k).wait_send()

    for at in range(line):
        @pl.when(z == at)
        def _():
            for buf, start, stop, shift in ((flat_up, 0, flat_first, 0), (up_buf, 0, late, flat_first)):
                if at < last:
                    @pl.loop(start, stop)
                    def _(k):
                        up_copy(buf, k, k + shift, at).wait_send()
            for buf, start, stop, shift in ((flat_down, 0, flat_first, 0), (down_buf, 0, late, flat_first)):
                if at > 0:
                    @pl.loop(start, stop)
                    def _(k):
                        down_copy(buf, k, k + shift, at).wait_send()


def reduce_rows(value, row_count, chunks, lanes, collective):
    width, columns = value.shape
    line, slice_rows = row_count // 2, width // row_count
    flat_first = (chunks + 3) // 6
    late = chunks - flat_first
    vmem = pl.BlockSpec(memory_space=pltpu.VMEM)
    dma = pltpu.SemaphoreType.DMA
    return pl.pallas_call(
        functools.partial(reduce_kernel, line, flat_first, chunks),
        out_shape=jax.ShapeDtypeStruct((slice_rows, chunks * lanes), jnp.float32),
        in_specs=[pl.BlockSpec(memory_space=pl.ANY)],
        out_specs=vmem,
        scratch_shapes=[
            pltpu.VMEM((late, line, slice_rows, lanes), jnp.float32),
            pltpu.VMEM((flat_first, line, 2, slice_rows, lanes), jnp.float32),
            pltpu.VMEM((late, line, slice_rows, lanes), jnp.float32),
            pltpu.VMEM((late, line - 1, slice_rows, lanes), jnp.float32),
            pltpu.VMEM((late, line - 1, slice_rows, lanes), jnp.float32),
            pltpu.VMEM((flat_first, line - 1, 2, slice_rows, lanes), jnp.float32),
            pltpu.VMEM((flat_first, line - 1, 2, slice_rows, lanes), jnp.float32),
            pltpu.VMEM((flat_first, 2, slice_rows, lanes), jnp.float32),
            pltpu.VMEM((flat_first, slice_rows, lanes), jnp.float32),
            dma((late,)),
            dma((flat_first,)),
            dma((late,)),
            dma((late,)),
            dma((chunks,)),
            dma((chunks,)),
            dma((chunks,)),
            dma((chunks,)),
            dma((flat_first,)),
            dma((flat_first,)),
        ],
        compiler_params=pltpu.CompilerParams(
            collective_id=collective, has_side_effects=True, vmem_limit_bytes=63 * 1024 * 1000
        ),
    )(value.reshape(line, 2, slice_rows, columns))


def finish_kernel(row_count, col_count,
                  owner_ref, slots_ref, own_ref, base_ref, lower_ref, diag_ref,
                  stage, picked, inner, part, reduced, total,
                  stage_send, stage_recv, send_sem, recv_sem, part_send, part_recv, total_send, total_recv):
    r, c = lax.axis_index("row"), lax.axis_index("col")
    ratio = row_count // col_count
    slice_rows, cells = picked.shape[1], picked.shape[2]

    barrier = pltpu.get_barrier_semaphore()
    for peer in range(row_count):
        @pl.when(peer != r)
        def _():
            pl.semaphore_signal(barrier, inc=1, device_id=(peer, c), device_id_type=MESH)
    for peer in range(col_count):
        @pl.when(peer != c)
        def _():
            pl.semaphore_signal(barrier, inc=1, device_id=(r, peer), device_id_type=MESH)
    pl.semaphore_wait(barrier, row_count + col_count - 2)

    def near(offset):
        pair = lax.rem(c // 2 + offset // 2, col_count // 2)
        return pair * 2 + lax.rem(lax.rem(c, 2) + offset % 2, 2)

    def piece(k):
        return pl.ds(k * cells, cells)

    def column_copy(target, k):
        return pltpu.make_async_remote_copy(
            src_ref=slots_ref.at[target, :, piece(k)],
            dst_ref=stage.at[c, :, piece(k)],
            send_sem=stage_send.at[target, k],
            recv_sem=stage_recv.at[c, k],
            device_id=(r, target),
            device_id_type=MESH,
        )

    def column_arrived(source, k):
        return pltpu.make_async_remote_copy(
            src_ref=slots_ref.at[source, :, piece(k)],
            dst_ref=stage.at[source, :, piece(k)],
            send_sem=stage_send.at[source, k],
            recv_sem=stage_recv.at[source, k],
            device_id=(r, source),
            device_id_type=MESH,
        )

    def row_copy(held, source, k):
        target = source * ratio + k
        return pltpu.make_async_remote_copy(
            src_ref=held.at[source, :, piece(k)],
            dst_ref=picked.at[r],
            send_sem=send_sem.at[target],
            recv_sem=recv_sem.at[r],
            device_id=(target, c),
            device_id_type=MESH,
        )

    def row_local(held, source, k):
        return pltpu.make_async_copy(
            held.at[source, :, piece(k)], picked.at[r], recv_sem.at[r]
        )

    def row_arrived(source):
        return pltpu.make_async_remote_copy(
            src_ref=picked.at[source],
            dst_ref=picked.at[source],
            send_sem=send_sem.at[source],
            recv_sem=recv_sem.at[source],
            device_id=(source, c),
            device_id_type=MESH,
        )

    for offset in (*range(2, col_count), 1):
        for k in range(ratio):
            column_copy(near(offset), k).start()
    for offset in range(col_count):
        source = near(offset)
        held = stage if offset else slots_ref
        for k in range(ratio):
            if offset:
                column_arrived(source, k).wait_recv()

            @pl.when(source * ratio + k == r)
            def _():
                row_local(held, source, k).start()

            @pl.when(source * ratio + k != r)
            def _():
                row_copy(held, source, k).start()

    def part_copy(peer):
        return pltpu.make_async_remote_copy(
            src_ref=inner.at[pl.ds(pl.multiple_of(peer * slice_rows, slice_rows), slice_rows), :],
            dst_ref=part.at[r],
            send_sem=part_send.at[peer],
            recv_sem=part_recv.at[r],
            device_id=(peer, c),
            device_id_type=MESH,
        )

    def part_arrived(peer):
        return pltpu.make_async_remote_copy(
            src_ref=inner.at[pl.ds(0, slice_rows), :],
            dst_ref=part.at[peer],
            send_sem=part_send.at[peer],
            recv_sem=part_recv.at[peer],
            device_id=(peer, c),
            device_id_type=MESH,
        )

    def total_copy(peer):
        return pltpu.make_async_remote_copy(
            src_ref=reduced,
            dst_ref=total.at[r],
            send_sem=total_send.at[peer],
            recv_sem=total_recv.at[r],
            device_id=(peer, c),
            device_id_type=MESH,
        )

    def total_arrived(peer):
        return pltpu.make_async_remote_copy(
            src_ref=reduced,
            dst_ref=total.at[peer],
            send_sem=total_send.at[peer],
            recv_sem=total_recv.at[peer],
            device_id=(peer, c),
            device_id_type=MESH,
        )

    def peers(action):
        for peer in range(row_count):
            @pl.when(peer != r)
            def _():
                action(peer)

    step = 256 if cells % 256 == 0 else BLK
    half = row_count // 2
    group_rows = half * slice_rows
    inner[...] = jnp.zeros_like(inner)

    for turn in range(2):
        first = lax.rem(r // half + turn, 2) * half
        for at in range(half):
            @pl.when(first + at != r)
            def _():
                row_arrived(first + at).wait_recv()

            @pl.when(first + at == r)
            def _():
                for offset in range(col_count):
                    source = near(offset)
                    for k in range(ratio):
                        @pl.when(source * ratio + k == r)
                        def _():
                            row_local(stage if offset else slots_ref, source, k).wait()

        group = pl.ds(pl.multiple_of(first * slice_rows, group_rows), group_rows)

        @pl.loop(0, cells // step)
        def _(i):
            at = pl.ds(pl.multiple_of(i * step, step), step)
            block = picked[pl.ds(first, half), :, at].reshape(group_rows, step)
            inner[group, :] += jnp.dot(
                block, own_ref[at, :], precision=lax.Precision.HIGHEST, preferred_element_type=jnp.float32
            )

        for at in range(half):
            @pl.when(first + at != r)
            def _():
                part_copy(first + at).start()

    peers(lambda peer: part_arrived(peer).wait_recv())
    mine = inner[pl.ds(pl.multiple_of(r * slice_rows, slice_rows), slice_rows), :]
    for peer in range(row_count):
        @pl.when(peer == r)
        def _():
            part[peer] = mine
    value = part[0]
    for peer in range(1, row_count):
        value = value + part[peer]
    reduced[...] = value
    peers(lambda peer: total_copy(peer).start())

    @pl.loop(0, cells // step)
    def _(i):
        at = pl.ds(pl.multiple_of(i * step, step), step)
        block = picked[:, :, at].reshape(row_count * slice_rows, step)
        lower_ref[at, :] = block.T

    peers(lambda peer: total_arrived(peer).wait_recv())
    for peer in range(row_count):
        @pl.when(peer == r)
        def _():
            total[peer] = reduced[...]
    base = jnp.where(owner_ref[c] >= 0, base_ref[...], jnp.zeros_like(base_ref))
    diag_ref[...] = base - total[...].reshape(diag_ref.shape)

    for offset in range(col_count):
        source = near(offset)
        held = stage if offset else slots_ref
        if offset:
            for k in range(ratio):
                column_copy(source, k).wait_send()
        for k in range(ratio):
            @pl.when(source * ratio + k != r)
            def _():
                row_copy(held, source, k).wait_send()
    peers(lambda peer: part_copy(peer).wait_send())
    peers(lambda peer: total_copy(peer).wait_send())


def finish(owner, slots, own, base, row_count):
    col_count, slice_rows, _ = slots.shape
    cells, width = own.shape
    vmem = pl.BlockSpec(memory_space=pltpu.VMEM)
    dma = pltpu.SemaphoreType.DMA
    return pl.pallas_call(
        functools.partial(finish_kernel, row_count, col_count),
        out_shape=(
            jax.ShapeDtypeStruct((cells, width), jnp.float32),
            jax.ShapeDtypeStruct((width, width), jnp.float32),
        ),
        in_specs=[pl.BlockSpec(memory_space=pltpu.SMEM)] + [vmem] * 3,
        out_specs=(vmem, vmem),
        scratch_shapes=[
            pltpu.VMEM(slots.shape, jnp.float32),
            pltpu.VMEM((row_count, slice_rows, cells), jnp.float32),
            pltpu.VMEM((width, width), jnp.float32),
            pltpu.VMEM((row_count, slice_rows, width), jnp.float32),
            pltpu.VMEM((slice_rows, width), jnp.float32),
            pltpu.VMEM((row_count, slice_rows, width), jnp.float32),
            dma((col_count, row_count // col_count)),
            dma((col_count, row_count // col_count)),
            dma((row_count,)),
            dma((row_count,)),
            dma((row_count,)),
            dma((row_count,)),
            dma((row_count,)),
            dma((row_count,)),
        ],
        compiler_params=pltpu.CompilerParams(collective_id=0, has_side_effects=True),
    )(owner, slots, own, base)


def per_device(anc_inverse, l_store, diag_inv, block_lists, block_counts, sibling_columns):
    siblings = block_lists.shape[0]
    row_count, col_count = lax.axis_size("row"), lax.axis_size("col")
    r, c = lax.axis_index("row"), lax.axis_index("col")
    row_blocks, col_blocks = anc_inverse.shape[0] // BLK, anc_inverse.shape[1] // BLK
    pairs = col_count // 2
    mate = [(k, k + 1 - 2 * (k % 2)) for k in range(col_count)]
    panel = l_store[0]
    near = [panel, lax.ppermute(panel, "col", mate)]
    moved = [
        lax.ppermute(panel, "col", [(k, (k + 2 * step) % col_count) for k in range(col_count)])
        for step in range(1, pairs)
    ]

    table = listed_table(block_lists, block_counts, row_blocks * row_count)
    row_listed = lax.dynamic_slice_in_dim(table, r * row_blocks, row_blocks, axis=1)
    col_listed = lax.dynamic_slice_in_dim(table, c * col_blocks, col_blocks, axis=1)
    row_ints = row_listed.astype(jnp.int32)
    counts = jnp.sum(row_ints, axis=1)
    place = jnp.cumsum(row_ints, axis=1) - 1
    ids = jnp.arange(row_blocks, dtype=jnp.int32)
    entry = jnp.arange(-(-row_blocks // GROUP) * GROUP, dtype=jnp.int32)
    hits = row_listed[:, :, None] & (place[:, :, None] == entry[None, None, :])
    rows = jnp.sum(jnp.where(hits, ids[None, :, None], 0), axis=1).astype(jnp.int32)

    flat = col_listed.reshape(-1)
    slot = jnp.where(flat, jnp.cumsum(flat.astype(jnp.int32)) - 1, -1).astype(jnp.int32)
    per_column = jnp.sum(table.reshape(siblings, col_count, col_blocks).astype(jnp.int32), axis=(0, 2))
    needed = jnp.max(per_column)
    slots_all = -(-siblings * col_blocks // 40) * 40
    grain = slots_all // 40
    caps = [grain * n for n in (19, 21, 23, 25, 28, 32, 40)]
    level = jnp.sum((needed > jnp.array(caps[:-1], jnp.int32)).astype(jnp.int32))

    match = sibling_columns[:, None] == jnp.arange(col_count, dtype=jnp.int32)[None, :]
    owner = jnp.max(
        jnp.where(match, jnp.arange(siblings, dtype=jnp.int32)[:, None], -1), axis=0
    ).astype(jnp.int32)
    slot_rows = slot.reshape(siblings, col_blocks)

    def pick(column):
        sibling = lax.dynamic_index_in_dim(owner, column, keepdims=False)
        at = jnp.maximum(sibling, 0)
        there = sibling >= 0
        return (
            jnp.where(there, slot_rows[at], -1),
            rows[at],
            jnp.where(there, counts[at], 0),
        )

    def tables(columns):
        found = [pick(column) for column in columns]
        return [jnp.stack(part) for part in zip(*found)]

    mate_of = c + 1 - 2 * (c % 2)
    near_columns = [c, mate_of]
    far_columns = []
    for step in range(1, pairs):
        far_columns += [lax.rem(c - 2 * step + col_count, col_count), lax.rem(mate_of - 2 * step + col_count, col_count)]
    partial_value, high, low = product(*tables(near_columns), anc_inverse, near, slots_all)
    if moved:
        moved, partial_value = lax.optimization_barrier((moved, partial_value))
        far = [panel for one in moved for panel in (one, lax.ppermute(one, "col", mate))]
        partial_value = product(*tables(far_columns), anc_inverse, far, slots_all, (partial_value, high, low))

    def branch(place, cap):
        def run(value):
            compact = reduce_rows(value, row_count, cap // grain, grain * BLK, place + 1)
            return expand(slot, owner, compact, siblings, col_blocks)
        return run

    upper, slots = lax.switch(level, [branch(place, cap) for place, cap in enumerate(caps)], partial_value)
    lower, diag = finish(owner, slots, l_store[0], diag_inv[0], row_count)
    return upper, lower[None], diag[None]


def solution(mesh):
    return jax.shard_map(
        per_device,
        mesh=mesh,
        in_specs=(P("row", "col"), P("col", "row", None), P("col", None, None), P(), P(), P()),
        out_specs=(P(None, "row", "col"), P("col", "row", None), P("col", None, None)),
        check_vma=False,
    )
```

```python
import functools

import jax
import jax.numpy as jnp
from jax import lax
from jax.experimental import pallas as pl
from jax.experimental.pallas import tpu as pltpu
from jax.sharding import PartitionSpec as P

BLK = 128
GROUP = 4
MESH = pl.DeviceIdType.MESH


def listed_table(block_lists, block_counts, block_total):
    block_ids = jnp.arange(block_total, dtype=jnp.int32)
    valid_entry = jnp.arange(block_lists.shape[1], dtype=jnp.int32)[None, :] < block_counts[:, None]
    entry_hits = (block_lists[:, :, None] == block_ids[None, None, :]) & valid_entry[:, :, None]
    return jnp.any(entry_hits, axis=1)


def product_kernel(members, tile_blocks, col_blocks, row_blocks, joins, saved,
                   slot_ref, rows_ref, count_ref, a_ref, *refs):
    panel_refs, refs = refs[:members], refs[members:]
    if joins:
        _, kept_high, kept_low, out_ref, highs, lows, p_high, p_low, stage, sent, kept = refs
    else:
        out_ref, kept_high, kept_low, highs, lows, p_high, p_low, stage, sent, kept = refs
    step, stripes = pl.program_id(0), pl.num_programs(0)
    split = stripes - saved

    def stripe_at(at):
        return jnp.where(at < split, saved + at, at - split) if joins else at

    stripe = stripe_at(step)
    side = lax.rem(step, 2) if joins else 0
    a_high, a_low = highs.at[side], lows.at[side]
    group = p_high.shape[3] // BLK
    listed = p_high.shape[1] * group

    def keep_copies(at):
        return (
            pltpu.make_async_copy(highs.at[0], kept_high.at[at], kept.at[0, 0]),
            pltpu.make_async_copy(lows.at[0], kept_low.at[at], kept.at[0, 1]),
        )

    def load_copies(at):
        to = lax.rem(at, 2)
        return (
            pltpu.make_async_copy(kept_high.at[at - split], highs.at[to], kept.at[to, 0]),
            pltpu.make_async_copy(kept_low.at[at - split], lows.at[to], kept.at[to, 1]),
        )

    @pl.when(step == 0)
    def _():
        for member in range(members):
            @pl.loop(0, count_ref[member])
            def _(i):
                rows = pl.ds(pl.multiple_of(rows_ref[member * listed + i] * BLK, BLK), BLK)
                lanes = pl.ds(pl.multiple_of(lax.rem(i, group) * BLK, BLK), BLK)
                value = -panel_refs[member][rows, :].T
                high = value.astype(jnp.bfloat16)
                p_high[member, i // group, :, lanes] = high
                p_low[member, i // group, :, lanes] = (value - high.astype(jnp.float32)).astype(jnp.bfloat16)

            @pl.loop(count_ref[member], (count_ref[member] + group - 1) // group * group)
            def _(i):
                lanes = pl.ds(pl.multiple_of(lax.rem(i, group) * BLK, BLK), BLK)
                zero = jnp.zeros((p_high.shape[2], BLK), jnp.bfloat16)
                p_high[member, i // group, :, lanes] = zero
                p_low[member, i // group, :, lanes] = zero

    def halve():
        @pl.loop(0, row_blocks)
        def _(block):
            rows = pl.ds(pl.multiple_of(block * BLK, BLK), BLK)
            value = a_ref[rows, :]
            high = value.astype(jnp.bfloat16)
            a_high[block] = high
            a_low[block] = (value - high.astype(jnp.float32)).astype(jnp.bfloat16)

    if joins:
        @pl.when((step + 1 >= split) & (step + 1 < stripes))
        def _():
            for copy in load_copies(step + 1):
                copy.start()

        pl.when(step < split)(halve)

        @pl.when(step >= split)
        def _():
            for copy in load_copies(step):
                copy.wait()
    else:
        @pl.when((step > 0) & (step <= saved))
        def _():
            for copy in keep_copies(step - 1):
                copy.wait()

        halve()

        @pl.when(step < saved)
        def _():
            for copy in keep_copies(step):
                copy.start()

    def slot_of(member, block, at):
        return slot_ref[member * col_blocks + at * tile_blocks + block]

    def slot_copy(member, block, slot):
        return pltpu.make_async_copy(
            stage.at[member, :, pl.ds(block * BLK, BLK)],
            out_ref.at[:, pl.ds(pl.multiple_of(slot * BLK, BLK), BLK)],
            sent.at[member, block],
        )

    def settle(member, at):
        for block in range(tile_blocks):
            slot = slot_of(member, block, at)

            @pl.when(slot >= 0)
            def _():
                slot_copy(member, block, slot).wait()

    for member in range(members):
        @pl.when(step > 0)
        def _():
            settle(member, stripe_at(step - 1))

        stage[member] = jnp.zeros(stage.shape[1:], jnp.float32)

        def add(k, blocks):
            at = [rows_ref[member * listed + k * group + u] for u in range(blocks)]
            part = slice(0, blocks * BLK)
            ph, plo = p_high[member, k, :, part], p_low[member, k, :, part]
            ah, al = [a_high[i] for i in at], [a_low[i] for i in at]
            left = jnp.concatenate([ph, ph, plo], axis=1)
            right = jnp.concatenate(ah + al + ah, axis=0)
            stage[member] += jnp.dot(left, right, preferred_element_type=jnp.float32)

        short = group // 2
        whole = (count_ref[member] + short - 1) // group

        @pl.loop(0, whole)
        def _(k):
            add(k, group)

        @pl.when(count_ref[member] > whole * group)
        def _():
            add(whole, short)

        for block in range(tile_blocks):
            slot = slot_of(member, block, stripe)

            @pl.when(slot >= 0)
            def _():
                slot_copy(member, block, slot).start()

    @pl.when(step == stripes - 1)
    def _():
        for member in range(members):
            settle(member, stripe)


def product(slot, rows, counts, anc, panels, slots_all, before=None):
    members = counts.shape[0]
    depth, cells = anc.shape
    width = panels[0].shape[1]
    row_blocks, col_blocks = depth // BLK, cells // BLK
    tile_blocks = next(n for n in (8, 4, 2, 1) if col_blocks % n == 0)
    tile = tile_blocks * BLK
    groups = rows.shape[1] // GROUP
    joins = () if before is None else tuple(before)
    stripes = col_blocks // tile_blocks
    saved = stripes - 1
    any_space = pl.BlockSpec(memory_space=pl.ANY)
    kept = jax.ShapeDtypeStruct((saved, row_blocks, BLK, tile), jnp.bfloat16)
    value = jax.ShapeDtypeStruct((width, slots_all * BLK), jnp.float32)
    sides = 2 if joins else 1
    first = saved if joins else 0
    held = pl.BlockSpec((depth, width), lambda i, *_: (0, 0), pipeline_mode=pl.Buffered(1))
    return pl.pallas_call(
        functools.partial(product_kernel, members, tile_blocks, col_blocks, row_blocks, len(joins), saved),
        out_shape=value if joins else (value, kept, kept),
        grid_spec=pltpu.PrefetchScalarGridSpec(
            num_scalar_prefetch=3,
            grid=(stripes,),
            in_specs=[pl.BlockSpec((depth, tile), lambda i, *_: (0, jnp.minimum(first + i, stripes - 1)))]
            + [held] * members
            + [any_space] * len(joins),
            out_specs=any_space if joins else (any_space,) * 3,
            scratch_shapes=[
                pltpu.VMEM((sides, row_blocks, BLK, tile), jnp.bfloat16),
                pltpu.VMEM((sides, row_blocks, BLK, tile), jnp.bfloat16),
                pltpu.VMEM((members, groups, width, GROUP * BLK), jnp.bfloat16),
                pltpu.VMEM((members, groups, width, GROUP * BLK), jnp.bfloat16),
                pltpu.VMEM((members, width, tile), jnp.float32),
                pltpu.SemaphoreType.DMA((members, tile_blocks)),
                pltpu.SemaphoreType.DMA((sides, 2)),
            ],
        ),
        input_output_aliases={4 + members: 0} if joins else {},
        cost_estimate=pl.CostEstimate(
            flops=2 * 3 * members * depth * cells * width // 2,
            bytes_accessed=4 * depth * cells + 4 * members * width * cells,
            transcendentals=0,
        ),
        compiler_params=pltpu.CompilerParams(
            dimension_semantics=("arbitrary",), vmem_limit_bytes=63 * 1024 * 1000
        ),
    )(slot.reshape(-1), rows.reshape(-1), counts, anc, *panels, *joins)


def expand_kernel(siblings, col_count, col_blocks, slot_ref, owner_ref, compact_ref, upper_ref, slots_ref):
    @pl.loop(0, col_blocks)
    def _(block):
        lanes = pl.ds(pl.multiple_of(block * BLK, BLK), BLK)
        for sibling in range(siblings):
            slot = slot_ref[sibling * col_blocks + block]
            at = pl.ds(pl.multiple_of(jnp.maximum(slot, 0) * BLK, BLK), BLK)
            value = compact_ref[:, at]
            upper_ref[sibling, :, lanes] = jnp.where(slot >= 0, value, jnp.zeros_like(value))

    for column in range(col_count):
        sibling = owner_ref[column]
        value = upper_ref[jnp.maximum(sibling, 0)]
        slots_ref[column] = jnp.where(sibling >= 0, value, jnp.zeros_like(value))


def expand(slot, owner, compact, siblings, col_blocks):
    col_count = owner.shape[0]
    rows = compact.shape[0]
    return pl.pallas_call(
        functools.partial(expand_kernel, siblings, col_count, col_blocks),
        out_shape=(
            jax.ShapeDtypeStruct((siblings, rows, col_blocks * BLK), jnp.float32),
            jax.ShapeDtypeStruct((col_count, rows, col_blocks * BLK), jnp.float32),
        ),
        in_specs=[pl.BlockSpec(memory_space=pltpu.SMEM)] * 2 + [pl.BlockSpec(memory_space=pltpu.VMEM)],
        out_specs=(pl.BlockSpec(memory_space=pltpu.VMEM),) * 2,
    )(slot, owner, compact)


def reduce_kernel(line, flat_first, chunks,
                  partial_ref, out_ref,
                  mine, flat_mine, pair_buf, up_buf, down_buf, flat_up, flat_down, flat_sum, flat_pair,
                  mine_sem, flat_sem, pair_send, pair_recv, up_send, up_recv, down_send, down_recv, flat_send, flat_recv):
    r, c = lax.axis_index("row"), lax.axis_index("col")
    z, y = r // 2, lax.rem(r, 2)
    other = 1 - y
    width = out_ref.shape[1] // chunks
    last, lag = line - 1, 2
    late = chunks - flat_first

    def lanes(chunk):
        return pl.ds(pl.multiple_of(chunk * width, width), width)

    def flat_load(k):
        return pltpu.make_async_copy(partial_ref.at[:, :, :, lanes(k)], flat_mine.at[k], flat_sem.at[k])

    def pair_load(k):
        return pltpu.make_async_copy(
            partial_ref.at[:, y, :, lanes(k + flat_first)], mine.at[k], mine_sem.at[k]
        )

    @pl.loop(0, flat_first)
    def _(k):
        flat_load(k).start()

    barrier = pltpu.get_barrier_semaphore()
    pl.semaphore_signal(barrier, inc=1, device_id=(z * 2 + other, c), device_id_type=MESH)

    @pl.when(z > 0)
    def _():
        pl.semaphore_signal(barrier, inc=1, device_id=(r - 2, c), device_id_type=MESH)

    @pl.when(z < last)
    def _():
        pl.semaphore_signal(barrier, inc=1, device_id=(r + 2, c), device_id_type=MESH)

    pl.semaphore_wait(barrier, 1 + (z > 0).astype(jnp.int32) + (z < last).astype(jnp.int32))

    def pair_copy(k):
        return pltpu.make_async_remote_copy(
            src_ref=partial_ref.at[:, other, :, lanes(k + flat_first)],
            dst_ref=pair_buf.at[k],
            send_sem=pair_send.at[k],
            recv_sem=pair_recv.at[k],
            device_id=(z * 2 + other, c),
            device_id_type=MESH,
        )

    def flat_copy(k):
        return pltpu.make_async_remote_copy(
            src_ref=flat_sum.at[k, other],
            dst_ref=flat_pair.at[k],
            send_sem=flat_send.at[k],
            recv_sem=flat_recv.at[k],
            device_id=(z * 2 + other, c),
            device_id_type=MESH,
        )

    def up_copy(buf, k, slot, at):
        return pltpu.make_async_remote_copy(
            src_ref=buf.at[k, pl.ds(at, last - at)],
            dst_ref=buf.at[k, pl.ds(at, last - at)],
            send_sem=up_send.at[slot],
            recv_sem=up_recv.at[slot],
            device_id=(r + 2, c),
            device_id_type=MESH,
        )

    def down_copy(buf, k, slot, at):
        return pltpu.make_async_remote_copy(
            src_ref=buf.at[k, pl.ds(0, at)],
            dst_ref=buf.at[k, pl.ds(0, at)],
            send_sem=down_send.at[slot],
            recv_sem=down_recv.at[slot],
            device_id=(r - 2, c),
            device_id_type=MESH,
        )

    def flat(k):
        def own(place):
            return flat_mine[k, place]

        def finish(value):
            flat_sum[k] = value
            flat_copy(k).start()

        return flat_up, flat_down, k, own, finish

    def paired(k):
        k = k - flat_first

        def own(place):
            return pair_buf[k, place]

        def finish(value):
            out_ref[:, lanes(k + flat_first)] = value

        return up_buf, down_buf, k, own, finish

    def total(at, up, down, k, own, finish):
        value = own(at)
        if at > 0:
            value = value + up[k, at - 1]
        if at < last:
            value = value + down[k, at]
        finish(value)

    def pass_up(at, slot, up, down, k, own, finish):
        if at > 0:
            up_copy(up, k, slot, at - 1).wait_recv()
        for place in range(at + 1, line):
            if at > 0:
                up[k, place - 1] = up[k, place - 1] + own(place)
            else:
                up[k, place - 1] = own(place)
        if at < last:
            up_copy(up, k, slot, at).start()
        if 2 * at > last:
            total(at, up, down, k, own, finish)

    def pass_down(at, slot, up, down, k, own, finish):
        if at < last:
            down_copy(down, k, slot, at + 1).wait_recv()
        for place in range(at):
            if at < last:
                down[k, place] = down[k, place] + own(place)
            else:
                down[k, place] = own(place)
        if at > 0:
            down_copy(down, k, slot, at).start()
        if 2 * at <= last:
            total(at, up, down, k, own, finish)

    def either(step, at, slot):
        @pl.when((slot >= 0) & (slot < flat_first))
        def _():
            step(at, slot, *flat(slot))

        @pl.when((slot >= flat_first) & (slot < chunks))
        def _():
            step(at, slot, *paired(slot))

    @pl.loop(0, late)
    def _(k):
        pair_copy(k).start()
        pair_load(k).start()

    @pl.loop(0, chunks + lag * last)
    def _(i):
        @pl.when(i < flat_first)
        def _():
            flat_load(i).wait()

        @pl.when((i >= flat_first) & (i < chunks))
        def _():
            k = i - flat_first
            pair_load(k).wait()
            pair_copy(k).wait_recv()
            for place in range(line):
                pair_buf[k, place] = pair_buf[k, place] + mine[k, place]

        for at in range(line):
            @pl.when(z == at)
            def _():
                either(pass_up, at, i - lag * at)
                either(pass_down, at, i - lag * (last - at))

    @pl.loop(0, flat_first)
    def _(k):
        flat_copy(k).wait_recv()
        out_ref[:, lanes(k)] = flat_sum[k, y] + flat_pair[k]

    @pl.loop(0, late)
    def _(k):
        pair_copy(k).wait_send()

    @pl.loop(0, flat_first)
    def _(k):
        flat_copy(k).wait_send()

    for at in range(line):
        @pl.when(z == at)
        def _():
            for buf, start, stop, shift in ((flat_up, 0, flat_first, 0), (up_buf, 0, late, flat_first)):
                if at < last:
                    @pl.loop(start, stop)
                    def _(k):
                        up_copy(buf, k, k + shift, at).wait_send()
            for buf, start, stop, shift in ((flat_down, 0, flat_first, 0), (down_buf, 0, late, flat_first)):
                if at > 0:
                    @pl.loop(start, stop)
                    def _(k):
                        down_copy(buf, k, k + shift, at).wait_send()


def reduce_rows(value, row_count, chunks, lanes, collective):
    width, columns = value.shape
    line, slice_rows = row_count // 2, width // row_count
    flat_first = (chunks + 3) // 6
    late = chunks - flat_first
    vmem = pl.BlockSpec(memory_space=pltpu.VMEM)
    dma = pltpu.SemaphoreType.DMA
    return pl.pallas_call(
        functools.partial(reduce_kernel, line, flat_first, chunks),
        out_shape=jax.ShapeDtypeStruct((slice_rows, chunks * lanes), jnp.float32),
        in_specs=[pl.BlockSpec(memory_space=pl.ANY)],
        out_specs=vmem,
        scratch_shapes=[
            pltpu.VMEM((late, line, slice_rows, lanes), jnp.float32),
            pltpu.VMEM((flat_first, line, 2, slice_rows, lanes), jnp.float32),
            pltpu.VMEM((late, line, slice_rows, lanes), jnp.float32),
            pltpu.VMEM((late, line - 1, slice_rows, lanes), jnp.float32),
            pltpu.VMEM((late, line - 1, slice_rows, lanes), jnp.float32),
            pltpu.VMEM((flat_first, line - 1, 2, slice_rows, lanes), jnp.float32),
            pltpu.VMEM((flat_first, line - 1, 2, slice_rows, lanes), jnp.float32),
            pltpu.VMEM((flat_first, 2, slice_rows, lanes), jnp.float32),
            pltpu.VMEM((flat_first, slice_rows, lanes), jnp.float32),
            dma((late,)),
            dma((flat_first,)),
            dma((late,)),
            dma((late,)),
            dma((chunks,)),
            dma((chunks,)),
            dma((chunks,)),
            dma((chunks,)),
            dma((flat_first,)),
            dma((flat_first,)),
        ],
        compiler_params=pltpu.CompilerParams(
            collective_id=collective, has_side_effects=True, vmem_limit_bytes=63 * 1024 * 1000
        ),
    )(value.reshape(line, 2, slice_rows, columns))


def finish_kernel(row_count, col_count,
                  owner_ref, slots_ref, own_ref, base_ref, lower_ref, diag_ref,
                  stage, picked, inner, part, reduced, total,
                  stage_send, stage_recv, send_sem, recv_sem, part_send, part_recv, total_send, total_recv):
    r, c = lax.axis_index("row"), lax.axis_index("col")
    ratio = row_count // col_count
    slice_rows, cells = picked.shape[1], picked.shape[2]

    barrier = pltpu.get_barrier_semaphore()
    for peer in range(row_count):
        @pl.when(peer != r)
        def _():
            pl.semaphore_signal(barrier, inc=1, device_id=(peer, c), device_id_type=MESH)
    for peer in range(col_count):
        @pl.when(peer != c)
        def _():
            pl.semaphore_signal(barrier, inc=1, device_id=(r, peer), device_id_type=MESH)
    pl.semaphore_wait(barrier, row_count + col_count - 2)

    def near(offset):
        pair = lax.rem(c // 2 + offset // 2, col_count // 2)
        return pair * 2 + lax.rem(lax.rem(c, 2) + offset % 2, 2)

    def piece(k):
        return pl.ds(k * cells, cells)

    def column_copy(target, k):
        return pltpu.make_async_remote_copy(
            src_ref=slots_ref.at[target, :, piece(k)],
            dst_ref=stage.at[c, :, piece(k)],
            send_sem=stage_send.at[target, k],
            recv_sem=stage_recv.at[c, k],
            device_id=(r, target),
            device_id_type=MESH,
        )

    def column_arrived(source, k):
        return pltpu.make_async_remote_copy(
            src_ref=slots_ref.at[source, :, piece(k)],
            dst_ref=stage.at[source, :, piece(k)],
            send_sem=stage_send.at[source, k],
            recv_sem=stage_recv.at[source, k],
            device_id=(r, source),
            device_id_type=MESH,
        )

    def row_copy(held, source, k):
        target = source * ratio + k
        return pltpu.make_async_remote_copy(
            src_ref=held.at[source, :, piece(k)],
            dst_ref=picked.at[r],
            send_sem=send_sem.at[target],
            recv_sem=recv_sem.at[r],
            device_id=(target, c),
            device_id_type=MESH,
        )

    def row_local(held, source, k):
        return pltpu.make_async_copy(
            held.at[source, :, piece(k)], picked.at[r], recv_sem.at[r]
        )

    def row_arrived(source):
        return pltpu.make_async_remote_copy(
            src_ref=picked.at[source],
            dst_ref=picked.at[source],
            send_sem=send_sem.at[source],
            recv_sem=recv_sem.at[source],
            device_id=(source, c),
            device_id_type=MESH,
        )

    for offset in (*range(2, col_count), 1):
        for k in range(ratio):
            column_copy(near(offset), k).start()
    for offset in range(col_count):
        source = near(offset)
        held = stage if offset else slots_ref
        for k in range(ratio):
            if offset:
                column_arrived(source, k).wait_recv()

            @pl.when(source * ratio + k == r)
            def _():
                row_local(held, source, k).start()

            @pl.when(source * ratio + k != r)
            def _():
                row_copy(held, source, k).start()

    def part_copy(peer):
        return pltpu.make_async_remote_copy(
            src_ref=inner.at[pl.ds(pl.multiple_of(peer * slice_rows, slice_rows), slice_rows), :],
            dst_ref=part.at[r],
            send_sem=part_send.at[peer],
            recv_sem=part_recv.at[r],
            device_id=(peer, c),
            device_id_type=MESH,
        )

    def part_arrived(peer):
        return pltpu.make_async_remote_copy(
            src_ref=inner.at[pl.ds(0, slice_rows), :],
            dst_ref=part.at[peer],
            send_sem=part_send.at[peer],
            recv_sem=part_recv.at[peer],
            device_id=(peer, c),
            device_id_type=MESH,
        )

    def total_copy(peer):
        return pltpu.make_async_remote_copy(
            src_ref=reduced,
            dst_ref=total.at[r],
            send_sem=total_send.at[peer],
            recv_sem=total_recv.at[r],
            device_id=(peer, c),
            device_id_type=MESH,
        )

    def total_arrived(peer):
        return pltpu.make_async_remote_copy(
            src_ref=reduced,
            dst_ref=total.at[peer],
            send_sem=total_send.at[peer],
            recv_sem=total_recv.at[peer],
            device_id=(peer, c),
            device_id_type=MESH,
        )

    def peers(action):
        for peer in range(row_count):
            @pl.when(peer != r)
            def _():
                action(peer)

    step = 256 if cells % 256 == 0 else BLK
    half = row_count // 2
    group_rows = half * slice_rows
    inner[...] = jnp.zeros_like(inner)

    for turn in range(2):
        first = lax.rem(r // half + turn, 2) * half
        for at in range(half):
            @pl.when(first + at != r)
            def _():
                row_arrived(first + at).wait_recv()

            @pl.when(first + at == r)
            def _():
                for offset in range(col_count):
                    source = near(offset)
                    for k in range(ratio):
                        @pl.when(source * ratio + k == r)
                        def _():
                            row_local(stage if offset else slots_ref, source, k).wait()

        group = pl.ds(pl.multiple_of(first * slice_rows, group_rows), group_rows)

        @pl.loop(0, cells // step)
        def _(i):
            at = pl.ds(pl.multiple_of(i * step, step), step)
            block = picked[pl.ds(first, half), :, at].reshape(group_rows, step)
            inner[group, :] += jnp.dot(
                block, own_ref[at, :], precision=lax.Precision.HIGHEST, preferred_element_type=jnp.float32
            )

        for at in range(half):
            @pl.when(first + at != r)
            def _():
                part_copy(first + at).start()

    peers(lambda peer: part_arrived(peer).wait_recv())
    mine = inner[pl.ds(pl.multiple_of(r * slice_rows, slice_rows), slice_rows), :]
    for peer in range(row_count):
        @pl.when(peer == r)
        def _():
            part[peer] = mine
    value = part[0]
    for peer in range(1, row_count):
        value = value + part[peer]
    reduced[...] = value
    peers(lambda peer: total_copy(peer).start())

    @pl.loop(0, cells // step)
    def _(i):
        at = pl.ds(pl.multiple_of(i * step, step), step)
        block = picked[:, :, at].reshape(row_count * slice_rows, step)
        lower_ref[at, :] = block.T

    peers(lambda peer: total_arrived(peer).wait_recv())
    for peer in range(row_count):
        @pl.when(peer == r)
        def _():
            total[peer] = reduced[...]
    base = jnp.where(owner_ref[c] >= 0, base_ref[...], jnp.zeros_like(base_ref))
    diag_ref[...] = base - total[...].reshape(diag_ref.shape)

    for offset in range(col_count):
        source = near(offset)
        held = stage if offset else slots_ref
        if offset:
            for k in range(ratio):
                column_copy(source, k).wait_send()
        for k in range(ratio):
            @pl.when(source * ratio + k != r)
            def _():
                row_copy(held, source, k).wait_send()
    peers(lambda peer: part_copy(peer).wait_send())
    peers(lambda peer: total_copy(peer).wait_send())


def finish(owner, slots, own, base, row_count):
    col_count, slice_rows, _ = slots.shape
    cells, width = own.shape
    vmem = pl.BlockSpec(memory_space=pltpu.VMEM)
    dma = pltpu.SemaphoreType.DMA
    return pl.pallas_call(
        functools.partial(finish_kernel, row_count, col_count),
        out_shape=(
            jax.ShapeDtypeStruct((cells, width), jnp.float32),
            jax.ShapeDtypeStruct((width, width), jnp.float32),
        ),
        in_specs=[pl.BlockSpec(memory_space=pltpu.SMEM)] + [vmem] * 3,
        out_specs=(vmem, vmem),
        scratch_shapes=[
            pltpu.VMEM(slots.shape, jnp.float32),
            pltpu.VMEM((row_count, slice_rows, cells), jnp.float32),
            pltpu.VMEM((width, width), jnp.float32),
            pltpu.VMEM((row_count, slice_rows, width), jnp.float32),
            pltpu.VMEM((slice_rows, width), jnp.float32),
            pltpu.VMEM((row_count, slice_rows, width), jnp.float32),
            dma((col_count, row_count // col_count)),
            dma((col_count, row_count // col_count)),
            dma((row_count,)),
            dma((row_count,)),
            dma((row_count,)),
            dma((row_count,)),
            dma((row_count,)),
            dma((row_count,)),
        ],
        compiler_params=pltpu.CompilerParams(collective_id=0, has_side_effects=True),
    )(owner, slots, own, base)


def per_device(anc_inverse, l_store, diag_inv, block_lists, block_counts, sibling_columns):
    siblings = block_lists.shape[0]
    row_count, col_count = lax.axis_size("row"), lax.axis_size("col")
    r, c = lax.axis_index("row"), lax.axis_index("col")
    row_blocks, col_blocks = anc_inverse.shape[0] // BLK, anc_inverse.shape[1] // BLK
    pairs = col_count // 2
    mate = [(k, k + 1 - 2 * (k % 2)) for k in range(col_count)]
    panel = l_store[0]
    near = [panel, lax.ppermute(panel, "col", mate)]
    moved = [
        lax.ppermute(panel, "col", [(k, (k + 2 * step) % col_count) for k in range(col_count)])
        for step in range(1, pairs)
    ]

    table = listed_table(block_lists, block_counts, row_blocks * row_count)
    row_listed = lax.dynamic_slice_in_dim(table, r * row_blocks, row_blocks, axis=1)
    col_listed = lax.dynamic_slice_in_dim(table, c * col_blocks, col_blocks, axis=1)
    row_ints = row_listed.astype(jnp.int32)
    counts = jnp.sum(row_ints, axis=1)
    place = jnp.cumsum(row_ints, axis=1) - 1
    ids = jnp.arange(row_blocks, dtype=jnp.int32)
    entry = jnp.arange(-(-row_blocks // GROUP) * GROUP, dtype=jnp.int32)
    hits = row_listed[:, :, None] & (place[:, :, None] == entry[None, None, :])
    rows = jnp.sum(jnp.where(hits, ids[None, :, None], 0), axis=1).astype(jnp.int32)

    flat = col_listed.reshape(-1)
    slot = jnp.where(flat, jnp.cumsum(flat.astype(jnp.int32)) - 1, -1).astype(jnp.int32)
    per_column = jnp.sum(table.reshape(siblings, col_count, col_blocks).astype(jnp.int32), axis=(0, 2))
    needed = jnp.max(per_column)
    slots_all = -(-siblings * col_blocks // 40) * 40
    grain = slots_all // 40
    caps = [grain * n for n in (19, 21, 23, 25, 28, 32, 40)]
    level = jnp.sum((needed > jnp.array(caps[:-1], jnp.int32)).astype(jnp.int32))

    match = sibling_columns[:, None] == jnp.arange(col_count, dtype=jnp.int32)[None, :]
    owner = jnp.max(
        jnp.where(match, jnp.arange(siblings, dtype=jnp.int32)[:, None], -1), axis=0
    ).astype(jnp.int32)
    slot_rows = slot.reshape(siblings, col_blocks)

    def tables(columns):
        owned = (sibling_columns[None, :] == jnp.stack(columns)[:, None]).astype(jnp.int32)
        return (
            jnp.sum(owned[:, :, None] * (slot_rows + 1)[None], axis=1) - 1,
            jnp.sum(owned[:, :, None] * rows[None], axis=1),
            jnp.sum(owned * counts[None, :], axis=1),
        )

    mate_of = c + 1 - 2 * (c % 2)
    near_columns = [c, mate_of]
    far_columns = []
    for step in range(1, pairs):
        far_columns += [lax.rem(c - 2 * step + col_count, col_count), lax.rem(mate_of - 2 * step + col_count, col_count)]
    partial_value, high, low = product(*tables(near_columns), anc_inverse, near, slots_all)
    if moved:
        moved, partial_value = lax.optimization_barrier((moved, partial_value))
        far = [panel for one in moved for panel in (one, lax.ppermute(one, "col", mate))]
        partial_value = product(*tables(far_columns), anc_inverse, far, slots_all, (partial_value, high, low))

    def branch(place, cap):
        def run(value):
            compact = reduce_rows(value, row_count, cap // grain, grain * BLK, place + 1)
            return expand(slot, owner, compact, siblings, col_blocks)
        return run

    upper, slots = lax.switch(level, [branch(place, cap) for place, cap in enumerate(caps)], partial_value)
    lower, diag = finish(owner, slots, l_store[0], diag_inv[0], row_count)
    return upper, lower[None], diag[None]


def solution(mesh):
    return jax.shard_map(
        per_device,
        mesh=mesh,
        in_specs=(P("row", "col"), P("col", "row", None), P("col", None, None), P(), P(), P()),
        out_specs=(P(None, "row", "col"), P("col", "row", None), P("col", None, None)),
        check_vma=False,
    )
```

```python
import functools

import jax
import jax.numpy as jnp
from jax import lax
from jax.experimental import pallas as pl
from jax.experimental.pallas import tpu as pltpu
from jax.sharding import PartitionSpec as P

BLK = 128
GROUP = 4
MESH = pl.DeviceIdType.MESH


def listed_table(block_lists, block_counts, block_total):
    block_ids = jnp.arange(block_total, dtype=jnp.int32)
    valid_entry = jnp.arange(block_lists.shape[1], dtype=jnp.int32)[None, :] < block_counts[:, None]
    entry_hits = (block_lists[:, :, None] == block_ids[None, None, :]) & valid_entry[:, :, None]
    return jnp.any(entry_hits, axis=1)


def product_kernel(members, tile_blocks, col_blocks, row_blocks, joins, saved,
                   slot_ref, rows_ref, count_ref, a_ref, *refs):
    panel_refs, refs = refs[:members], refs[members:]
    if joins:
        _, kept_high, kept_low, out_ref, highs, lows, p_high, p_low, stage, sent, kept = refs
    else:
        out_ref, kept_high, kept_low, highs, lows, p_high, p_low, stage, sent, kept = refs
    step, stripes = pl.program_id(0), pl.num_programs(0)
    split = stripes - saved

    def stripe_at(at):
        return jnp.where(at < split, saved + at, at - split) if joins else at

    stripe = stripe_at(step)
    side = lax.rem(step, 2) if joins else 0
    a_high, a_low = highs.at[side], lows.at[side]
    group = p_high.shape[3] // BLK
    listed = p_high.shape[1] * group

    def keep_copies(at):
        return (
            pltpu.make_async_copy(highs.at[0], kept_high.at[at], kept.at[0, 0]),
            pltpu.make_async_copy(lows.at[0], kept_low.at[at], kept.at[0, 1]),
        )

    def load_copies(at):
        to = lax.rem(at, 2)
        return (
            pltpu.make_async_copy(kept_high.at[at - split], highs.at[to], kept.at[to, 0]),
            pltpu.make_async_copy(kept_low.at[at - split], lows.at[to], kept.at[to, 1]),
        )

    @pl.when(step == 0)
    def _():
        for member in range(members):
            @pl.loop(0, count_ref[member])
            def _(i):
                rows = pl.ds(pl.multiple_of(rows_ref[member * listed + i] * BLK, BLK), BLK)
                lanes = pl.ds(pl.multiple_of(lax.rem(i, group) * BLK, BLK), BLK)
                value = -panel_refs[member][rows, :].T
                high = value.astype(jnp.bfloat16)
                p_high[member, i // group, :, lanes] = high
                p_low[member, i // group, :, lanes] = (value - high.astype(jnp.float32)).astype(jnp.bfloat16)

            @pl.loop(count_ref[member], (count_ref[member] + group - 1) // group * group)
            def _(i):
                lanes = pl.ds(pl.multiple_of(lax.rem(i, group) * BLK, BLK), BLK)
                zero = jnp.zeros((p_high.shape[2], BLK), jnp.bfloat16)
                p_high[member, i // group, :, lanes] = zero
                p_low[member, i // group, :, lanes] = zero

    def halve():
        @pl.loop(0, row_blocks)
        def _(block):
            rows = pl.ds(pl.multiple_of(block * BLK, BLK), BLK)
            value = a_ref[rows, :]
            high = value.astype(jnp.bfloat16)
            a_high[block] = high
            a_low[block] = (value - high.astype(jnp.float32)).astype(jnp.bfloat16)

    if joins:
        @pl.when((step + 1 >= split) & (step + 1 < stripes))
        def _():
            for copy in load_copies(step + 1):
                copy.start()

        pl.when(step < split)(halve)

        @pl.when(step >= split)
        def _():
            for copy in load_copies(step):
                copy.wait()
    else:
        @pl.when((step > 0) & (step <= saved))
        def _():
            for copy in keep_copies(step - 1):
                copy.wait()

        halve()

        @pl.when(step < saved)
        def _():
            for copy in keep_copies(step):
                copy.start()

    def slot_of(member, block, at):
        return slot_ref[member * col_blocks + at * tile_blocks + block]

    def slot_copy(member, block, slot):
        return pltpu.make_async_copy(
            stage.at[member, :, pl.ds(block * BLK, BLK)],
            out_ref.at[:, pl.ds(pl.multiple_of(slot * BLK, BLK), BLK)],
            sent.at[member, block],
        )

    def settle(member, at):
        for block in range(tile_blocks):
            slot = slot_of(member, block, at)

            @pl.when(slot >= 0)
            def _():
                slot_copy(member, block, slot).wait()

    for member in range(members):
        @pl.when(step > 0)
        def _():
            settle(member, stripe_at(step - 1))

        stage[member] = jnp.zeros(stage.shape[1:], jnp.float32)

        def add(k, blocks):
            at = [rows_ref[member * listed + k * group + u] for u in range(blocks)]
            part = slice(0, blocks * BLK)
            ph, plo = p_high[member, k, :, part], p_low[member, k, :, part]
            ah, al = [a_high[i] for i in at], [a_low[i] for i in at]
            left = jnp.concatenate([ph, ph, plo], axis=1)
            right = jnp.concatenate(ah + al + ah, axis=0)
            stage[member] += jnp.dot(left, right, preferred_element_type=jnp.float32)

        short = group // 2
        whole = (count_ref[member] + short - 1) // group

        @pl.loop(0, whole)
        def _(k):
            add(k, group)

        @pl.when(count_ref[member] > whole * group)
        def _():
            add(whole, short)

        for block in range(tile_blocks):
            slot = slot_of(member, block, stripe)

            @pl.when(slot >= 0)
            def _():
                slot_copy(member, block, slot).start()

    @pl.when(step == stripes - 1)
    def _():
        for member in range(members):
            settle(member, stripe)


def product(slot, rows, counts, anc, panels, slots_all, before=None):
    members = counts.shape[0]
    depth, cells = anc.shape
    width = panels[0].shape[1]
    row_blocks, col_blocks = depth // BLK, cells // BLK
    tile_blocks = next(n for n in (8, 4, 2, 1) if col_blocks % n == 0)
    tile = tile_blocks * BLK
    groups = rows.shape[1] // GROUP
    joins = () if before is None else tuple(before)
    stripes = col_blocks // tile_blocks
    saved = stripes - 1
    any_space = pl.BlockSpec(memory_space=pl.ANY)
    kept = jax.ShapeDtypeStruct((saved, row_blocks, BLK, tile), jnp.bfloat16)
    value = jax.ShapeDtypeStruct((width, slots_all * BLK), jnp.float32)
    sides = 2 if joins else 1
    first = saved if joins else 0
    held = pl.BlockSpec((depth, width), lambda i, *_: (0, 0), pipeline_mode=pl.Buffered(1))
    return pl.pallas_call(
        functools.partial(product_kernel, members, tile_blocks, col_blocks, row_blocks, len(joins), saved),
        out_shape=value if joins else (value, kept, kept),
        grid_spec=pltpu.PrefetchScalarGridSpec(
            num_scalar_prefetch=3,
            grid=(stripes,),
            in_specs=[pl.BlockSpec((depth, tile), lambda i, *_: (0, jnp.minimum(first + i, stripes - 1)))]
            + [held] * members
            + [any_space] * len(joins),
            out_specs=any_space if joins else (any_space,) * 3,
            scratch_shapes=[
                pltpu.VMEM((sides, row_blocks, BLK, tile), jnp.bfloat16),
                pltpu.VMEM((sides, row_blocks, BLK, tile), jnp.bfloat16),
                pltpu.VMEM((members, groups, width, GROUP * BLK), jnp.bfloat16),
                pltpu.VMEM((members, groups, width, GROUP * BLK), jnp.bfloat16),
                pltpu.VMEM((members, width, tile), jnp.float32),
                pltpu.SemaphoreType.DMA((members, tile_blocks)),
                pltpu.SemaphoreType.DMA((sides, 2)),
            ],
        ),
        input_output_aliases={4 + members: 0} if joins else {},
        cost_estimate=pl.CostEstimate(
            flops=2 * 3 * members * depth * cells * width // 2,
            bytes_accessed=4 * depth * cells + 4 * members * width * cells,
            transcendentals=0,
        ),
        compiler_params=pltpu.CompilerParams(
            dimension_semantics=("arbitrary",), vmem_limit_bytes=63 * 1024 * 1000
        ),
    )(slot.reshape(-1), rows.reshape(-1), counts, anc, *panels, *joins)


def expand_kernel(siblings, col_count, ratio, col_blocks, slot_ref, owner_ref, compact_ref, upper_ref, slots_ref):
    @pl.loop(0, col_blocks)
    def _(block):
        lanes = pl.ds(pl.multiple_of(block * BLK, BLK), BLK)
        for sibling in range(siblings):
            slot = slot_ref[sibling * col_blocks + block]
            at = pl.ds(pl.multiple_of(jnp.maximum(slot, 0) * BLK, BLK), BLK)
            value = compact_ref[:, at]
            upper_ref[sibling, :, lanes] = jnp.where(slot >= 0, value, jnp.zeros_like(value))

    blocks = col_blocks // ratio
    for column in range(col_count):
        sibling = owner_ref[column]
        for k in range(ratio):
            def pack(block, taken):
                slot = jnp.where(sibling >= 0, slot_ref[jnp.maximum(sibling, 0) * col_blocks + k * blocks + block], -1)

                @pl.when(slot >= 0)
                def _():
                    at = pl.ds(pl.multiple_of(slot * BLK, BLK), BLK)
                    slots_ref[column, k, :, pl.ds(pl.multiple_of(taken * BLK, BLK), BLK)] = compact_ref[:, at]

                return taken + (slot >= 0).astype(jnp.int32)

            taken = lax.fori_loop(0, blocks, pack, jnp.int32(0))

            @pl.loop(taken, blocks)
            def _(block):
                lanes = pl.ds(pl.multiple_of(block * BLK, BLK), BLK)
                slots_ref[column, k, :, lanes] = jnp.zeros((slots_ref.shape[2], BLK), jnp.float32)


def expand(slot, owner, compact, siblings, col_blocks, ratio):
    col_count = owner.shape[0]
    rows = compact.shape[0]
    return pl.pallas_call(
        functools.partial(expand_kernel, siblings, col_count, ratio, col_blocks),
        out_shape=(
            jax.ShapeDtypeStruct((siblings, rows, col_blocks * BLK), jnp.float32),
            jax.ShapeDtypeStruct((col_count, ratio, rows, col_blocks // ratio * BLK), jnp.float32),
        ),
        in_specs=[pl.BlockSpec(memory_space=pltpu.SMEM)] * 2 + [pl.BlockSpec(memory_space=pltpu.VMEM)],
        out_specs=(pl.BlockSpec(memory_space=pltpu.VMEM),) * 2,
    )(slot, owner, compact)


def reduce_kernel(line, flat_first, chunks,
                  partial_ref, out_ref,
                  mine, flat_mine, pair_buf, up_buf, down_buf, flat_up, flat_down, flat_sum, flat_pair,
                  mine_sem, flat_sem, pair_send, pair_recv, up_send, up_recv, down_send, down_recv, flat_send, flat_recv):
    r, c = lax.axis_index("row"), lax.axis_index("col")
    z, y = r // 2, lax.rem(r, 2)
    other = 1 - y
    width = out_ref.shape[1] // chunks
    last, lag = line - 1, 2
    late = chunks - flat_first

    def lanes(chunk):
        return pl.ds(pl.multiple_of(chunk * width, width), width)

    def flat_load(k):
        return pltpu.make_async_copy(partial_ref.at[:, :, :, lanes(k)], flat_mine.at[k], flat_sem.at[k])

    def pair_load(k):
        return pltpu.make_async_copy(
            partial_ref.at[:, y, :, lanes(k + flat_first)], mine.at[k], mine_sem.at[k]
        )

    @pl.loop(0, flat_first)
    def _(k):
        flat_load(k).start()

    barrier = pltpu.get_barrier_semaphore()
    pl.semaphore_signal(barrier, inc=1, device_id=(z * 2 + other, c), device_id_type=MESH)

    @pl.when(z > 0)
    def _():
        pl.semaphore_signal(barrier, inc=1, device_id=(r - 2, c), device_id_type=MESH)

    @pl.when(z < last)
    def _():
        pl.semaphore_signal(barrier, inc=1, device_id=(r + 2, c), device_id_type=MESH)

    pl.semaphore_wait(barrier, 1 + (z > 0).astype(jnp.int32) + (z < last).astype(jnp.int32))

    def pair_copy(k):
        return pltpu.make_async_remote_copy(
            src_ref=partial_ref.at[:, other, :, lanes(k + flat_first)],
            dst_ref=pair_buf.at[k],
            send_sem=pair_send.at[k],
            recv_sem=pair_recv.at[k],
            device_id=(z * 2 + other, c),
            device_id_type=MESH,
        )

    def flat_copy(k):
        return pltpu.make_async_remote_copy(
            src_ref=flat_sum.at[k, other],
            dst_ref=flat_pair.at[k],
            send_sem=flat_send.at[k],
            recv_sem=flat_recv.at[k],
            device_id=(z * 2 + other, c),
            device_id_type=MESH,
        )

    def up_copy(buf, k, slot, at):
        return pltpu.make_async_remote_copy(
            src_ref=buf.at[k, pl.ds(at, last - at)],
            dst_ref=buf.at[k, pl.ds(at, last - at)],
            send_sem=up_send.at[slot],
            recv_sem=up_recv.at[slot],
            device_id=(r + 2, c),
            device_id_type=MESH,
        )

    def down_copy(buf, k, slot, at):
        return pltpu.make_async_remote_copy(
            src_ref=buf.at[k, pl.ds(0, at)],
            dst_ref=buf.at[k, pl.ds(0, at)],
            send_sem=down_send.at[slot],
            recv_sem=down_recv.at[slot],
            device_id=(r - 2, c),
            device_id_type=MESH,
        )

    def flat(k):
        def own(place):
            return flat_mine[k, place]

        def finish(value):
            flat_sum[k] = value
            flat_copy(k).start()

        return flat_up, flat_down, k, own, finish

    def paired(k):
        k = k - flat_first

        def own(place):
            return pair_buf[k, place]

        def finish(value):
            out_ref[:, lanes(k + flat_first)] = value

        return up_buf, down_buf, k, own, finish

    def total(at, up, down, k, own, finish):
        value = own(at)
        if at > 0:
            value = value + up[k, at - 1]
        if at < last:
            value = value + down[k, at]
        finish(value)

    def pass_up(at, slot, up, down, k, own, finish):
        if at > 0:
            up_copy(up, k, slot, at - 1).wait_recv()
        for place in range(at + 1, line):
            if at > 0:
                up[k, place - 1] = up[k, place - 1] + own(place)
            else:
                up[k, place - 1] = own(place)
        if at < last:
            up_copy(up, k, slot, at).start()
        if 2 * at > last:
            total(at, up, down, k, own, finish)

    def pass_down(at, slot, up, down, k, own, finish):
        if at < last:
            down_copy(down, k, slot, at + 1).wait_recv()
        for place in range(at):
            if at < last:
                down[k, place] = down[k, place] + own(place)
            else:
                down[k, place] = own(place)
        if at > 0:
            down_copy(down, k, slot, at).start()
        if 2 * at <= last:
            total(at, up, down, k, own, finish)

    def either(step, at, slot):
        @pl.when((slot >= 0) & (slot < flat_first))
        def _():
            step(at, slot, *flat(slot))

        @pl.when((slot >= flat_first) & (slot < chunks))
        def _():
            step(at, slot, *paired(slot))

    @pl.loop(0, late)
    def _(k):
        pair_copy(k).start()
        pair_load(k).start()

    @pl.loop(0, chunks + lag * last)
    def _(i):
        @pl.when(i < flat_first)
        def _():
            flat_load(i).wait()

        @pl.when((i >= flat_first) & (i < chunks))
        def _():
            k = i - flat_first
            pair_load(k).wait()
            pair_copy(k).wait_recv()
            for place in range(line):
                pair_buf[k, place] = pair_buf[k, place] + mine[k, place]

        for at in range(line):
            @pl.when(z == at)
            def _():
                either(pass_up, at, i - lag * at)
                either(pass_down, at, i - lag * (last - at))

    @pl.loop(0, flat_first)
    def _(k):
        flat_copy(k).wait_recv()
        out_ref[:, lanes(k)] = flat_sum[k, y] + flat_pair[k]

    @pl.loop(0, late)
    def _(k):
        pair_copy(k).wait_send()

    @pl.loop(0, flat_first)
    def _(k):
        flat_copy(k).wait_send()

    for at in range(line):
        @pl.when(z == at)
        def _():
            for buf, start, stop, shift in ((flat_up, 0, flat_first, 0), (up_buf, 0, late, flat_first)):
                if at < last:
                    @pl.loop(start, stop)
                    def _(k):
                        up_copy(buf, k, k + shift, at).wait_send()
            for buf, start, stop, shift in ((flat_down, 0, flat_first, 0), (down_buf, 0, late, flat_first)):
                if at > 0:
                    @pl.loop(start, stop)
                    def _(k):
                        down_copy(buf, k, k + shift, at).wait_send()


def reduce_rows(value, row_count, chunks, lanes, collective):
    width, columns = value.shape
    line, slice_rows = row_count // 2, width // row_count
    flat_first = (chunks + 3) // 6
    late = chunks - flat_first
    vmem = pl.BlockSpec(memory_space=pltpu.VMEM)
    dma = pltpu.SemaphoreType.DMA
    return pl.pallas_call(
        functools.partial(reduce_kernel, line, flat_first, chunks),
        out_shape=jax.ShapeDtypeStruct((slice_rows, chunks * lanes), jnp.float32),
        in_specs=[pl.BlockSpec(memory_space=pl.ANY)],
        out_specs=vmem,
        scratch_shapes=[
            pltpu.VMEM((late, line, slice_rows, lanes), jnp.float32),
            pltpu.VMEM((flat_first, line, 2, slice_rows, lanes), jnp.float32),
            pltpu.VMEM((late, line, slice_rows, lanes), jnp.float32),
            pltpu.VMEM((late, line - 1, slice_rows, lanes), jnp.float32),
            pltpu.VMEM((late, line - 1, slice_rows, lanes), jnp.float32),
            pltpu.VMEM((flat_first, line - 1, 2, slice_rows, lanes), jnp.float32),
            pltpu.VMEM((flat_first, line - 1, 2, slice_rows, lanes), jnp.float32),
            pltpu.VMEM((flat_first, 2, slice_rows, lanes), jnp.float32),
            pltpu.VMEM((flat_first, slice_rows, lanes), jnp.float32),
            dma((late,)),
            dma((flat_first,)),
            dma((late,)),
            dma((late,)),
            dma((chunks,)),
            dma((chunks,)),
            dma((chunks,)),
            dma((chunks,)),
            dma((flat_first,)),
            dma((flat_first,)),
        ],
        compiler_params=pltpu.CompilerParams(
            collective_id=collective, has_side_effects=True, vmem_limit_bytes=63 * 1024 * 1000
        ),
    )(value.reshape(line, 2, slice_rows, columns))


def pack_kernel(rows_ref, own_ref, out_ref):
    @pl.loop(0, out_ref.shape[0] // BLK)
    def _(block):
        rows = pl.ds(pl.multiple_of(rows_ref[block] * BLK, BLK), BLK)
        out_ref[pl.ds(pl.multiple_of(block * BLK, BLK), BLK), :] = own_ref[rows, :]


def packed(rows, own):
    vmem = pl.BlockSpec(memory_space=pltpu.VMEM)
    return pl.pallas_call(
        pack_kernel,
        out_shape=jax.ShapeDtypeStruct(own.shape, own.dtype),
        in_specs=[pl.BlockSpec(memory_space=pltpu.SMEM), vmem],
        out_specs=vmem,
    )(rows, own)


def unpack_kernel(place_ref, picked_ref, lower_ref):
    place = place_ref[pl.program_id(0)]
    at = pl.ds(pl.multiple_of(jnp.maximum(place, 0) * BLK, BLK), BLK)
    value = picked_ref[:, :, at].reshape(lower_ref.shape[1], BLK)
    lower_ref[...] = jnp.where(place >= 0, value, jnp.zeros_like(value)).T


def unpacked(place, picked, depth):
    row_count, slice_rows, _ = picked.shape
    width = row_count * slice_rows
    return pl.pallas_call(
        unpack_kernel,
        out_shape=jax.ShapeDtypeStruct((depth, width), picked.dtype),
        grid_spec=pltpu.PrefetchScalarGridSpec(
            num_scalar_prefetch=1,
            grid=(depth // BLK,),
            in_specs=[pl.BlockSpec(picked.shape, lambda i, *_: (0, 0, 0), pipeline_mode=pl.Buffered(1))],
            out_specs=pl.BlockSpec((BLK, width), lambda i, *_: (i, 0)),
        ),
    )(place, picked)


def finish_kernel(row_count, col_count,
                  owner_ref, slots_ref, own_ref, base_ref, picked_ref, diag_ref,
                  stage, picked, inner, part, reduced, total,
                  stage_send, stage_recv, send_sem, recv_sem, part_send, part_recv, total_send, total_recv):
    r, c = lax.axis_index("row"), lax.axis_index("col")
    ratio = row_count // col_count
    slice_rows, cells = picked.shape[1], picked.shape[2]

    barrier = pltpu.get_barrier_semaphore()
    for peer in range(row_count):
        @pl.when(peer != r)
        def _():
            pl.semaphore_signal(barrier, inc=1, device_id=(peer, c), device_id_type=MESH)
    for peer in range(col_count):
        @pl.when(peer != c)
        def _():
            pl.semaphore_signal(barrier, inc=1, device_id=(r, peer), device_id_type=MESH)
    pl.semaphore_wait(barrier, row_count + col_count - 2)

    def near(offset):
        pair = lax.rem(c // 2 + offset // 2, col_count // 2)
        return pair * 2 + lax.rem(lax.rem(c, 2) + offset % 2, 2)

    front = pl.ds(0, cells)

    def column_copy(target, k):
        return pltpu.make_async_remote_copy(
            src_ref=slots_ref.at[target, k, :, front],
            dst_ref=stage.at[c, k],
            send_sem=stage_send.at[target, k],
            recv_sem=stage_recv.at[c, k],
            device_id=(r, target),
            device_id_type=MESH,
        )

    def column_arrived(source, k):
        return pltpu.make_async_remote_copy(
            src_ref=slots_ref.at[source, k, :, front],
            dst_ref=stage.at[source, k],
            send_sem=stage_send.at[source, k],
            recv_sem=stage_recv.at[source, k],
            device_id=(r, source),
            device_id_type=MESH,
        )

    def row_copy(held, source, k):
        target = source * ratio + k
        return pltpu.make_async_remote_copy(
            src_ref=held.at[source, k, :, front],
            dst_ref=picked.at[r],
            send_sem=send_sem.at[target],
            recv_sem=recv_sem.at[r],
            device_id=(target, c),
            device_id_type=MESH,
        )

    def row_local(held, source, k):
        return pltpu.make_async_copy(
            held.at[source, k, :, front], picked.at[r], recv_sem.at[r]
        )

    def row_arrived(source):
        return pltpu.make_async_remote_copy(
            src_ref=picked.at[source],
            dst_ref=picked.at[source],
            send_sem=send_sem.at[source],
            recv_sem=recv_sem.at[source],
            device_id=(source, c),
            device_id_type=MESH,
        )

    for offset in (*range(2, col_count), 1):
        for k in range(ratio):
            column_copy(near(offset), k).start()
    for offset in range(col_count):
        source = near(offset)
        held = stage if offset else slots_ref
        for k in range(ratio):
            if offset:
                column_arrived(source, k).wait_recv()

            @pl.when(source * ratio + k == r)
            def _():
                row_local(held, source, k).start()

            @pl.when(source * ratio + k != r)
            def _():
                row_copy(held, source, k).start()

    def part_copy(peer):
        return pltpu.make_async_remote_copy(
            src_ref=inner.at[pl.ds(pl.multiple_of(peer * slice_rows, slice_rows), slice_rows), :],
            dst_ref=part.at[r],
            send_sem=part_send.at[peer],
            recv_sem=part_recv.at[r],
            device_id=(peer, c),
            device_id_type=MESH,
        )

    def part_arrived(peer):
        return pltpu.make_async_remote_copy(
            src_ref=inner.at[pl.ds(0, slice_rows), :],
            dst_ref=part.at[peer],
            send_sem=part_send.at[peer],
            recv_sem=part_recv.at[peer],
            device_id=(peer, c),
            device_id_type=MESH,
        )

    def total_copy(peer):
        return pltpu.make_async_remote_copy(
            src_ref=reduced,
            dst_ref=total.at[r],
            send_sem=total_send.at[peer],
            recv_sem=total_recv.at[r],
            device_id=(peer, c),
            device_id_type=MESH,
        )

    def total_arrived(peer):
        return pltpu.make_async_remote_copy(
            src_ref=reduced,
            dst_ref=total.at[peer],
            send_sem=total_send.at[peer],
            recv_sem=total_recv.at[peer],
            device_id=(peer, c),
            device_id_type=MESH,
        )

    def peers(action):
        for peer in range(row_count):
            @pl.when(peer != r)
            def _():
                action(peer)

    step = 256 if cells % 256 == 0 else BLK
    half = row_count // 2
    group_rows = half * slice_rows
    inner[...] = jnp.zeros_like(inner)

    for turn in range(2):
        first = lax.rem(r // half + turn, 2) * half
        for at in range(half):
            @pl.when(first + at != r)
            def _():
                row_arrived(first + at).wait_recv()

            @pl.when(first + at == r)
            def _():
                for offset in range(col_count):
                    source = near(offset)
                    for k in range(ratio):
                        @pl.when(source * ratio + k == r)
                        def _():
                            row_local(stage if offset else slots_ref, source, k).wait()

        group = pl.ds(pl.multiple_of(first * slice_rows, group_rows), group_rows)

        @pl.loop(0, cells // step)
        def _(i):
            at = pl.ds(pl.multiple_of(i * step, step), step)
            block = picked[pl.ds(first, half), :, at].reshape(group_rows, step)
            inner[group, :] += jnp.dot(
                block, own_ref[at, :], precision=lax.Precision.HIGHEST, preferred_element_type=jnp.float32
            )

        for at in range(half):
            @pl.when(first + at != r)
            def _():
                part_copy(first + at).start()

    peers(lambda peer: part_arrived(peer).wait_recv())
    mine = inner[pl.ds(pl.multiple_of(r * slice_rows, slice_rows), slice_rows), :]
    for peer in range(row_count):
        @pl.when(peer == r)
        def _():
            part[peer] = mine
    value = part[0]
    for peer in range(1, row_count):
        value = value + part[peer]
    reduced[...] = value
    peers(lambda peer: total_copy(peer).start())

    @pl.loop(0, row_count)
    def _(source):
        picked_ref[source] = picked[source]

    peers(lambda peer: total_arrived(peer).wait_recv())
    for peer in range(row_count):
        @pl.when(peer == r)
        def _():
            total[peer] = reduced[...]
    base = jnp.where(owner_ref[c] >= 0, base_ref[...], jnp.zeros_like(base_ref))
    diag_ref[...] = base - total[...].reshape(diag_ref.shape)

    for offset in range(col_count):
        source = near(offset)
        held = stage if offset else slots_ref
        if offset:
            for k in range(ratio):
                column_copy(source, k).wait_send()
        for k in range(ratio):
            @pl.when(source * ratio + k != r)
            def _():
                row_copy(held, source, k).wait_send()
    peers(lambda peer: part_copy(peer).wait_send())
    peers(lambda peer: total_copy(peer).wait_send())


def finish(owner, slots, own, base, row_count, most, collective):
    col_count, ratio, slice_rows, _ = slots.shape
    width = own.shape[1]
    cells = most * BLK
    vmem = pl.BlockSpec(memory_space=pltpu.VMEM)
    dma = pltpu.SemaphoreType.DMA
    return pl.pallas_call(
        functools.partial(finish_kernel, row_count, col_count),
        out_shape=(
            jax.ShapeDtypeStruct((row_count, slice_rows, cells), jnp.float32),
            jax.ShapeDtypeStruct((width, width), jnp.float32),
        ),
        in_specs=[pl.BlockSpec(memory_space=pltpu.SMEM)] + [vmem] * 3,
        out_specs=(vmem, vmem),
        scratch_shapes=[
            pltpu.VMEM((col_count, ratio, slice_rows, cells), jnp.float32),
            pltpu.VMEM((row_count, slice_rows, cells), jnp.float32),
            pltpu.VMEM((width, width), jnp.float32),
            pltpu.VMEM((row_count, slice_rows, width), jnp.float32),
            pltpu.VMEM((slice_rows, width), jnp.float32),
            pltpu.VMEM((row_count, slice_rows, width), jnp.float32),
            dma((col_count, row_count // col_count)),
            dma((col_count, row_count // col_count)),
            dma((row_count,)),
            dma((row_count,)),
            dma((row_count,)),
            dma((row_count,)),
            dma((row_count,)),
            dma((row_count,)),
        ],
        compiler_params=pltpu.CompilerParams(collective_id=collective, has_side_effects=True),
    )(owner, slots, own, base)


def per_device(anc_inverse, l_store, diag_inv, block_lists, block_counts, sibling_columns):
    siblings = block_lists.shape[0]
    row_count, col_count = lax.axis_size("row"), lax.axis_size("col")
    r, c = lax.axis_index("row"), lax.axis_index("col")
    row_blocks, col_blocks = anc_inverse.shape[0] // BLK, anc_inverse.shape[1] // BLK
    pairs = col_count // 2
    mate = [(k, k + 1 - 2 * (k % 2)) for k in range(col_count)]
    panel = l_store[0]
    near = [panel, lax.ppermute(panel, "col", mate)]
    moved = [
        lax.ppermute(panel, "col", [(k, (k + 2 * step) % col_count) for k in range(col_count)])
        for step in range(1, pairs)
    ]

    table = listed_table(block_lists, block_counts, row_blocks * row_count)
    row_listed = lax.dynamic_slice_in_dim(table, r * row_blocks, row_blocks, axis=1)
    col_listed = lax.dynamic_slice_in_dim(table, c * col_blocks, col_blocks, axis=1)
    row_ints = row_listed.astype(jnp.int32)
    counts = jnp.sum(row_ints, axis=1)
    place = jnp.cumsum(row_ints, axis=1) - 1
    ids = jnp.arange(row_blocks, dtype=jnp.int32)
    entry = jnp.arange(-(-row_blocks // GROUP) * GROUP, dtype=jnp.int32)
    hits = row_listed[:, :, None] & (place[:, :, None] == entry[None, None, :])
    rows = jnp.sum(jnp.where(hits, ids[None, :, None], 0), axis=1).astype(jnp.int32)

    flat = col_listed.reshape(-1)
    slot = jnp.where(flat, jnp.cumsum(flat.astype(jnp.int32)) - 1, -1).astype(jnp.int32)
    per_column = jnp.sum(table.reshape(siblings, col_count, col_blocks).astype(jnp.int32), axis=(0, 2))
    needed = jnp.max(per_column)
    slots_all = -(-siblings * col_blocks // 40) * 40
    grain = slots_all // 40
    caps = [grain * n for n in (19, 20, 21, 22, 23, 25, 28, 32, 40)]
    level = jnp.sum((needed > jnp.array(caps[:-1], jnp.int32)).astype(jnp.int32))

    match = sibling_columns[:, None] == jnp.arange(col_count, dtype=jnp.int32)[None, :]
    owner = jnp.max(
        jnp.where(match, jnp.arange(siblings, dtype=jnp.int32)[:, None], -1), axis=0
    ).astype(jnp.int32)
    slot_rows = slot.reshape(siblings, col_blocks)

    def tables(columns):
        owned = (sibling_columns[None, :] == jnp.stack(columns)[:, None]).astype(jnp.int32)
        return (
            jnp.sum(owned[:, :, None] * (slot_rows + 1)[None], axis=1) - 1,
            jnp.sum(owned[:, :, None] * rows[None], axis=1),
            jnp.sum(owned * counts[None, :], axis=1),
        )

    mate_of = c + 1 - 2 * (c % 2)
    near_columns = [c, mate_of]
    far_columns = []
    for step in range(1, pairs):
        far_columns += [lax.rem(c - 2 * step + col_count, col_count), lax.rem(mate_of - 2 * step + col_count, col_count)]
    near_tables = tables(near_columns)
    partial_value, high, low = product(*near_tables, anc_inverse, near, slots_all)
    if moved:
        moved, partial_value = lax.optimization_barrier((moved, partial_value))
        far = [panel for one in moved for panel in (one, lax.ppermute(one, "col", mate))]
        partial_value = product(*tables(far_columns), anc_inverse, far, slots_all, (partial_value, high, low))

    def branch(place, cap):
        def run(value):
            compact = reduce_rows(value, row_count, cap // grain, grain * BLK, place + 1)
            return expand(slot, owner, compact, siblings, col_blocks, row_count // col_count)
        return run

    upper, slots = lax.switch(level, [branch(place, cap) for place, cap in enumerate(caps)], partial_value)

    own_rows = near_tables[1][0]
    own_place = jnp.sum(
        jnp.where(sibling_columns == c, 1, 0)[:, None] * jnp.where(row_listed, place + 1, 0), axis=0
    ) - 1
    most = jnp.max(jnp.sum(table.reshape(siblings, row_count, row_blocks).astype(jnp.int32), axis=2))
    sizes = sorted({-(-row_blocks * n // 20) for n in (16, 18, 20)})
    depth_level = jnp.sum((most > jnp.array(sizes[:-1], jnp.int32)).astype(jnp.int32))

    def end(number, size):
        def run(value, own, base):
            picked, diag = finish(owner, value, own, base, row_count, size, len(caps) + 1 + number)
            return unpacked(own_place, picked, own.shape[0]), diag
        return run

    lower, diag = lax.switch(
        depth_level, [end(number, size) for number, size in enumerate(sizes)], slots, packed(own_rows, panel), diag_inv[0]
    )
    return upper, lower[None], diag[None]


def solution(mesh):
    return jax.shard_map(
        per_device,
        mesh=mesh,
        in_specs=(P("row", "col"), P("col", "row", None), P("col", None, None), P(), P(), P()),
        out_specs=(P(None, "row", "col"), P("col", "row", None), P("col", None, None)),
        check_vma=False,
    )
```

```python
import functools

import jax
import jax.numpy as jnp
from jax import lax
from jax.experimental import pallas as pl
from jax.experimental.pallas import tpu as pltpu
from jax.sharding import PartitionSpec as P

BLK = 128
GROUP = 4
MESH = pl.DeviceIdType.MESH


def listed_table(block_lists, block_counts, block_total):
    block_ids = jnp.arange(block_total, dtype=jnp.int32)
    valid_entry = jnp.arange(block_lists.shape[1], dtype=jnp.int32)[None, :] < block_counts[:, None]
    entry_hits = (block_lists[:, :, None] == block_ids[None, None, :]) & valid_entry[:, :, None]
    return jnp.any(entry_hits, axis=1)


def product_kernel(members, tile_blocks, col_blocks, row_blocks, joins, saved,
                   slot_ref, rows_ref, count_ref, a_ref, *refs):
    panel_refs, refs = refs[:members], refs[members:]
    if joins:
        _, kept_high, kept_low, out_ref, highs, lows, p_high, p_low, stage, sent, kept = refs
    else:
        out_ref, kept_high, kept_low, highs, lows, p_high, p_low, stage, sent, kept = refs
    step, stripes = pl.program_id(0), pl.num_programs(0)
    split = stripes - saved

    def stripe_at(at):
        return jnp.where(at < split, saved + at, at - split) if joins else at

    stripe = stripe_at(step)
    side = lax.rem(step, 2) if joins else 0
    a_high, a_low = highs.at[side], lows.at[side]
    group = p_high.shape[3] // BLK
    listed = p_high.shape[1] * group

    def keep_copies(at):
        return (
            pltpu.make_async_copy(highs.at[0], kept_high.at[at], kept.at[0, 0]),
            pltpu.make_async_copy(lows.at[0], kept_low.at[at], kept.at[0, 1]),
        )

    def load_copies(at):
        to = lax.rem(at, 2)
        return (
            pltpu.make_async_copy(kept_high.at[at - split], highs.at[to], kept.at[to, 0]),
            pltpu.make_async_copy(kept_low.at[at - split], lows.at[to], kept.at[to, 1]),
        )

    @pl.when(step == 0)
    def _():
        for member in range(members):
            @pl.loop(0, count_ref[member])
            def _(i):
                rows = pl.ds(pl.multiple_of(rows_ref[member * listed + i] * BLK, BLK), BLK)
                lanes = pl.ds(pl.multiple_of(lax.rem(i, group) * BLK, BLK), BLK)
                value = -panel_refs[member][rows, :].T
                high = value.astype(jnp.bfloat16)
                p_high[member, i // group, :, lanes] = high
                p_low[member, i // group, :, lanes] = (value - high.astype(jnp.float32)).astype(jnp.bfloat16)

            @pl.loop(count_ref[member], (count_ref[member] + group - 1) // group * group)
            def _(i):
                lanes = pl.ds(pl.multiple_of(lax.rem(i, group) * BLK, BLK), BLK)
                zero = jnp.zeros((p_high.shape[2], BLK), jnp.bfloat16)
                p_high[member, i // group, :, lanes] = zero
                p_low[member, i // group, :, lanes] = zero

    def halve():
        @pl.loop(0, row_blocks)
        def _(block):
            rows = pl.ds(pl.multiple_of(block * BLK, BLK), BLK)
            value = a_ref[rows, :]
            high = value.astype(jnp.bfloat16)
            a_high[block] = high
            a_low[block] = (value - high.astype(jnp.float32)).astype(jnp.bfloat16)

    if joins:
        @pl.when((step + 1 >= split) & (step + 1 < stripes))
        def _():
            for copy in load_copies(step + 1):
                copy.start()

        pl.when(step < split)(halve)

        @pl.when(step >= split)
        def _():
            for copy in load_copies(step):
                copy.wait()
    else:
        @pl.when((step > 0) & (step <= saved))
        def _():
            for copy in keep_copies(step - 1):
                copy.wait()

        halve()

        @pl.when(step < saved)
        def _():
            for copy in keep_copies(step):
                copy.start()

    def slot_of(member, block, at):
        return slot_ref[member * col_blocks + at * tile_blocks + block]

    def slot_copy(member, block, slot):
        return pltpu.make_async_copy(
            stage.at[member, :, pl.ds(block * BLK, BLK)],
            out_ref.at[:, pl.ds(pl.multiple_of(slot * BLK, BLK), BLK)],
            sent.at[member, block],
        )

    def settle(member, at):
        for block in range(tile_blocks):
            slot = slot_of(member, block, at)

            @pl.when(slot >= 0)
            def _():
                slot_copy(member, block, slot).wait()

    for member in range(members):
        @pl.when(step > 0)
        def _():
            settle(member, stripe_at(step - 1))

        stage[member] = jnp.zeros(stage.shape[1:], jnp.float32)

        def add(k, blocks):
            at = [rows_ref[member * listed + k * group + u] for u in range(blocks)]
            part = slice(0, blocks * BLK)
            ph, plo = p_high[member, k, :, part], p_low[member, k, :, part]
            ah, al = [a_high[i] for i in at], [a_low[i] for i in at]
            left = jnp.concatenate([ph, ph, plo], axis=1)
            right = jnp.concatenate(ah + al + ah, axis=0)
            stage[member] += jnp.dot(left, right, preferred_element_type=jnp.float32)

        short = group // 2
        whole = (count_ref[member] + short - 1) // group

        @pl.loop(0, whole)
        def _(k):
            add(k, group)

        @pl.when(count_ref[member] > whole * group)
        def _():
            add(whole, short)

        for block in range(tile_blocks):
            slot = slot_of(member, block, stripe)

            @pl.when(slot >= 0)
            def _():
                slot_copy(member, block, slot).start()

    @pl.when(step == stripes - 1)
    def _():
        for member in range(members):
            settle(member, stripe)


def product(slot, rows, counts, anc, panels, slots_all, before=None):
    members = counts.shape[0]
    depth, cells = anc.shape
    width = panels[0].shape[1]
    row_blocks, col_blocks = depth // BLK, cells // BLK
    tile_blocks = next(n for n in (8, 4, 2, 1) if col_blocks % n == 0)
    tile = tile_blocks * BLK
    groups = rows.shape[1] // GROUP
    joins = () if before is None else tuple(before)
    stripes = col_blocks // tile_blocks
    saved = stripes - 1
    any_space = pl.BlockSpec(memory_space=pl.ANY)
    kept = jax.ShapeDtypeStruct((saved, row_blocks, BLK, tile), jnp.bfloat16)
    value = jax.ShapeDtypeStruct((width, slots_all * BLK), jnp.float32)
    sides = 2 if joins else 1
    first = saved if joins else 0
    held = pl.BlockSpec((depth, width), lambda i, *_: (0, 0), pipeline_mode=pl.Buffered(1))
    return pl.pallas_call(
        functools.partial(product_kernel, members, tile_blocks, col_blocks, row_blocks, len(joins), saved),
        out_shape=value if joins else (value, kept, kept),
        grid_spec=pltpu.PrefetchScalarGridSpec(
            num_scalar_prefetch=3,
            grid=(stripes,),
            in_specs=[pl.BlockSpec((depth, tile), lambda i, *_: (0, jnp.minimum(first + i, stripes - 1)))]
            + [held] * members
            + [any_space] * len(joins),
            out_specs=any_space if joins else (any_space,) * 3,
            scratch_shapes=[
                pltpu.VMEM((sides, row_blocks, BLK, tile), jnp.bfloat16),
                pltpu.VMEM((sides, row_blocks, BLK, tile), jnp.bfloat16),
                pltpu.VMEM((members, groups, width, GROUP * BLK), jnp.bfloat16),
                pltpu.VMEM((members, groups, width, GROUP * BLK), jnp.bfloat16),
                pltpu.VMEM((members, width, tile), jnp.float32),
                pltpu.SemaphoreType.DMA((members, tile_blocks)),
                pltpu.SemaphoreType.DMA((sides, 2)),
            ],
        ),
        input_output_aliases={4 + members: 0} if joins else {},
        cost_estimate=pl.CostEstimate(
            flops=2 * 3 * members * depth * cells * width // 2,
            bytes_accessed=4 * depth * cells + 4 * members * width * cells,
            transcendentals=0,
        ),
        compiler_params=pltpu.CompilerParams(
            dimension_semantics=("arbitrary",), vmem_limit_bytes=63 * 1024 * 1000
        ),
    )(slot.reshape(-1), rows.reshape(-1), counts, anc, *panels, *joins)


def expand_kernel(siblings, col_count, ratio, col_blocks, slot_ref, owner_ref, compact_ref, upper_ref, slots_ref):
    @pl.loop(0, col_blocks)
    def _(block):
        lanes = pl.ds(pl.multiple_of(block * BLK, BLK), BLK)
        for sibling in range(siblings):
            slot = slot_ref[sibling * col_blocks + block]
            at = pl.ds(pl.multiple_of(jnp.maximum(slot, 0) * BLK, BLK), BLK)
            value = compact_ref[:, at]
            upper_ref[sibling, :, lanes] = jnp.where(slot >= 0, value, jnp.zeros_like(value))

    blocks = col_blocks // ratio
    for column in range(col_count):
        sibling = owner_ref[column]
        for k in range(ratio):
            def pack(block, taken):
                slot = jnp.where(sibling >= 0, slot_ref[jnp.maximum(sibling, 0) * col_blocks + k * blocks + block], -1)

                @pl.when(slot >= 0)
                def _():
                    at = pl.ds(pl.multiple_of(slot * BLK, BLK), BLK)
                    slots_ref[column, k, :, pl.ds(pl.multiple_of(taken * BLK, BLK), BLK)] = compact_ref[:, at]

                return taken + (slot >= 0).astype(jnp.int32)

            taken = lax.fori_loop(0, blocks, pack, jnp.int32(0))

            @pl.loop(taken, blocks)
            def _(block):
                lanes = pl.ds(pl.multiple_of(block * BLK, BLK), BLK)
                slots_ref[column, k, :, lanes] = jnp.zeros((slots_ref.shape[2], BLK), jnp.float32)


def expand(slot, owner, compact, siblings, col_blocks, ratio):
    col_count = owner.shape[0]
    rows = compact.shape[0]
    return pl.pallas_call(
        functools.partial(expand_kernel, siblings, col_count, ratio, col_blocks),
        out_shape=(
            jax.ShapeDtypeStruct((siblings, rows, col_blocks * BLK), jnp.float32),
            jax.ShapeDtypeStruct((col_count, ratio, rows, col_blocks // ratio * BLK), jnp.float32),
        ),
        in_specs=[pl.BlockSpec(memory_space=pltpu.SMEM)] * 2 + [pl.BlockSpec(memory_space=pltpu.VMEM)],
        out_specs=(pl.BlockSpec(memory_space=pltpu.VMEM),) * 2,
    )(slot, owner, compact)


def reduce_kernel(line, flat_first, chunks,
                  partial_ref, out_ref,
                  mine, flat_mine, pair_buf, up_buf, down_buf, flat_up, flat_down, flat_sum, flat_pair,
                  mine_sem, flat_sem, pair_send, pair_recv, up_send, up_recv, down_send, down_recv, flat_send, flat_recv):
    r, c = lax.axis_index("row"), lax.axis_index("col")
    z, y = r // 2, lax.rem(r, 2)
    other = 1 - y
    width = out_ref.shape[1] // chunks
    last, lag = line - 1, 2
    late = chunks - flat_first

    def lanes(chunk):
        return pl.ds(pl.multiple_of(chunk * width, width), width)

    def flat_load(k):
        return pltpu.make_async_copy(partial_ref.at[:, :, :, lanes(k)], flat_mine.at[k], flat_sem.at[k])

    def pair_load(k):
        return pltpu.make_async_copy(
            partial_ref.at[:, y, :, lanes(k + flat_first)], mine.at[k], mine_sem.at[k]
        )

    @pl.loop(0, flat_first)
    def _(k):
        flat_load(k).start()

    barrier = pltpu.get_barrier_semaphore()
    pl.semaphore_signal(barrier, inc=1, device_id=(z * 2 + other, c), device_id_type=MESH)

    @pl.when(z > 0)
    def _():
        pl.semaphore_signal(barrier, inc=1, device_id=(r - 2, c), device_id_type=MESH)

    @pl.when(z < last)
    def _():
        pl.semaphore_signal(barrier, inc=1, device_id=(r + 2, c), device_id_type=MESH)

    pl.semaphore_wait(barrier, 1 + (z > 0).astype(jnp.int32) + (z < last).astype(jnp.int32))

    def pair_copy(k):
        return pltpu.make_async_remote_copy(
            src_ref=partial_ref.at[:, other, :, lanes(k + flat_first)],
            dst_ref=pair_buf.at[k],
            send_sem=pair_send.at[k],
            recv_sem=pair_recv.at[k],
            device_id=(z * 2 + other, c),
            device_id_type=MESH,
        )

    def flat_copy(k):
        return pltpu.make_async_remote_copy(
            src_ref=flat_sum.at[k, other],
            dst_ref=flat_pair.at[k],
            send_sem=flat_send.at[k],
            recv_sem=flat_recv.at[k],
            device_id=(z * 2 + other, c),
            device_id_type=MESH,
        )

    def up_copy(buf, k, slot, at):
        return pltpu.make_async_remote_copy(
            src_ref=buf.at[k, pl.ds(at, last - at)],
            dst_ref=buf.at[k, pl.ds(at, last - at)],
            send_sem=up_send.at[slot],
            recv_sem=up_recv.at[slot],
            device_id=(r + 2, c),
            device_id_type=MESH,
        )

    def down_copy(buf, k, slot, at):
        return pltpu.make_async_remote_copy(
            src_ref=buf.at[k, pl.ds(0, at)],
            dst_ref=buf.at[k, pl.ds(0, at)],
            send_sem=down_send.at[slot],
            recv_sem=down_recv.at[slot],
            device_id=(r - 2, c),
            device_id_type=MESH,
        )

    def flat(k):
        def own(place):
            return flat_mine[k, place]

        def finish(value):
            flat_sum[k] = value
            flat_copy(k).start()

        return flat_up, flat_down, k, own, finish

    def paired(k):
        k = k - flat_first

        def own(place):
            return pair_buf[k, place]

        def finish(value):
            out_ref[:, lanes(k + flat_first)] = value

        return up_buf, down_buf, k, own, finish

    def total(at, up, down, k, own, finish):
        value = own(at)
        if at > 0:
            value = value + up[k, at - 1]
        if at < last:
            value = value + down[k, at]
        finish(value)

    def pass_up(at, slot, up, down, k, own, finish):
        if at > 0:
            up_copy(up, k, slot, at - 1).wait_recv()
        for place in range(at + 1, line):
            if at > 0:
                up[k, place - 1] = up[k, place - 1] + own(place)
            else:
                up[k, place - 1] = own(place)
        if at < last:
            up_copy(up, k, slot, at).start()
        if 2 * at > last:
            total(at, up, down, k, own, finish)

    def pass_down(at, slot, up, down, k, own, finish):
        if at < last:
            down_copy(down, k, slot, at + 1).wait_recv()
        for place in range(at):
            if at < last:
                down[k, place] = down[k, place] + own(place)
            else:
                down[k, place] = own(place)
        if at > 0:
            down_copy(down, k, slot, at).start()
        if 2 * at <= last:
            total(at, up, down, k, own, finish)

    def either(step, at, slot):
        @pl.when((slot >= 0) & (slot < flat_first))
        def _():
            step(at, slot, *flat(slot))

        @pl.when((slot >= flat_first) & (slot < chunks))
        def _():
            step(at, slot, *paired(slot))

    @pl.loop(0, late)
    def _(k):
        pair_copy(k).start()
        pair_load(k).start()

    @pl.loop(0, chunks + lag * last)
    def _(i):
        @pl.when(i < flat_first)
        def _():
            flat_load(i).wait()

        @pl.when((i >= flat_first) & (i < chunks))
        def _():
            k = i - flat_first
            pair_load(k).wait()
            pair_copy(k).wait_recv()
            for place in range(line):
                pair_buf[k, place] = pair_buf[k, place] + mine[k, place]

        for at in range(line):
            @pl.when(z == at)
            def _():
                either(pass_up, at, i - lag * at)
                either(pass_down, at, i - lag * (last - at))

    @pl.loop(0, flat_first)
    def _(k):
        flat_copy(k).wait_recv()
        out_ref[:, lanes(k)] = flat_sum[k, y] + flat_pair[k]

    @pl.loop(0, late)
    def _(k):
        pair_copy(k).wait_send()

    @pl.loop(0, flat_first)
    def _(k):
        flat_copy(k).wait_send()

    for at in range(line):
        @pl.when(z == at)
        def _():
            for buf, start, stop, shift in ((flat_up, 0, flat_first, 0), (up_buf, 0, late, flat_first)):
                if at < last:
                    @pl.loop(start, stop)
                    def _(k):
                        up_copy(buf, k, k + shift, at).wait_send()
            for buf, start, stop, shift in ((flat_down, 0, flat_first, 0), (down_buf, 0, late, flat_first)):
                if at > 0:
                    @pl.loop(start, stop)
                    def _(k):
                        down_copy(buf, k, k + shift, at).wait_send()


def reduce_rows(value, row_count, chunks, lanes, collective):
    width, columns = value.shape
    line, slice_rows = row_count // 2, width // row_count
    flat_first = (chunks + 3) // 6
    late = chunks - flat_first
    vmem = pl.BlockSpec(memory_space=pltpu.VMEM)
    dma = pltpu.SemaphoreType.DMA
    return pl.pallas_call(
        functools.partial(reduce_kernel, line, flat_first, chunks),
        out_shape=jax.ShapeDtypeStruct((slice_rows, chunks * lanes), jnp.float32),
        in_specs=[pl.BlockSpec(memory_space=pl.ANY)],
        out_specs=vmem,
        scratch_shapes=[
            pltpu.VMEM((late, line, slice_rows, lanes), jnp.float32),
            pltpu.VMEM((flat_first, line, 2, slice_rows, lanes), jnp.float32),
            pltpu.VMEM((late, line, slice_rows, lanes), jnp.float32),
            pltpu.VMEM((late, line - 1, slice_rows, lanes), jnp.float32),
            pltpu.VMEM((late, line - 1, slice_rows, lanes), jnp.float32),
            pltpu.VMEM((flat_first, line - 1, 2, slice_rows, lanes), jnp.float32),
            pltpu.VMEM((flat_first, line - 1, 2, slice_rows, lanes), jnp.float32),
            pltpu.VMEM((flat_first, 2, slice_rows, lanes), jnp.float32),
            pltpu.VMEM((flat_first, slice_rows, lanes), jnp.float32),
            dma((late,)),
            dma((flat_first,)),
            dma((late,)),
            dma((late,)),
            dma((chunks,)),
            dma((chunks,)),
            dma((chunks,)),
            dma((chunks,)),
            dma((flat_first,)),
            dma((flat_first,)),
        ],
        compiler_params=pltpu.CompilerParams(
            collective_id=collective, has_side_effects=True, vmem_limit_bytes=63 * 1024 * 1000
        ),
    )(value.reshape(line, 2, slice_rows, columns))


def pack_kernel(rows_ref, own_ref, out_ref):
    @pl.loop(0, out_ref.shape[0] // BLK)
    def _(block):
        rows = pl.ds(pl.multiple_of(rows_ref[block] * BLK, BLK), BLK)
        out_ref[pl.ds(pl.multiple_of(block * BLK, BLK), BLK), :] = own_ref[rows, :]


def packed(rows, own):
    vmem = pl.BlockSpec(memory_space=pltpu.VMEM)
    return pl.pallas_call(
        pack_kernel,
        out_shape=jax.ShapeDtypeStruct(own.shape, own.dtype),
        in_specs=[pl.BlockSpec(memory_space=pltpu.SMEM), vmem],
        out_specs=vmem,
    )(rows, own)


def unpack_kernel(place_ref, picked_ref, lower_ref):
    place = place_ref[pl.program_id(0)]
    at = pl.ds(pl.multiple_of(jnp.maximum(place, 0) * BLK, BLK), BLK)
    value = picked_ref[:, :, at].reshape(lower_ref.shape[1], BLK)
    lower_ref[...] = jnp.where(place >= 0, value, jnp.zeros_like(value)).T


def unpacked(place, picked, depth):
    row_count, slice_rows, _ = picked.shape
    width = row_count * slice_rows
    return pl.pallas_call(
        unpack_kernel,
        out_shape=jax.ShapeDtypeStruct((depth, width), picked.dtype),
        grid_spec=pltpu.PrefetchScalarGridSpec(
            num_scalar_prefetch=1,
            grid=(depth // BLK,),
            in_specs=[pl.BlockSpec(picked.shape, lambda i, *_: (0, 0, 0), pipeline_mode=pl.Buffered(1))],
            out_specs=pl.BlockSpec((BLK, width), lambda i, *_: (i, 0)),
        ),
    )(place, picked)


def finish_kernel(row_count, col_count,
                  owner_ref, slots_ref, own_ref, base_ref, picked_ref, diag_ref,
                  stage, picked, inner, part, reduced, total,
                  stage_send, stage_recv, send_sem, recv_sem, part_send, part_recv, total_send, total_recv):
    r, c = lax.axis_index("row"), lax.axis_index("col")
    ratio = row_count // col_count
    slice_rows, cells = picked.shape[1], picked.shape[2]

    barrier = pltpu.get_barrier_semaphore()
    for peer in range(row_count):
        @pl.when(peer != r)
        def _():
            pl.semaphore_signal(barrier, inc=1, device_id=(peer, c), device_id_type=MESH)
    for peer in range(col_count):
        @pl.when(peer != c)
        def _():
            pl.semaphore_signal(barrier, inc=1, device_id=(r, peer), device_id_type=MESH)
    pl.semaphore_wait(barrier, row_count + col_count - 2)

    def near(offset):
        pair = lax.rem(c // 2 + offset // 2, col_count // 2)
        return pair * 2 + lax.rem(lax.rem(c, 2) + offset % 2, 2)

    front = pl.ds(0, cells)

    def column_copy(target, k):
        return pltpu.make_async_remote_copy(
            src_ref=slots_ref.at[target, k, :, front],
            dst_ref=stage.at[c, k],
            send_sem=stage_send.at[target, k],
            recv_sem=stage_recv.at[c, k],
            device_id=(r, target),
            device_id_type=MESH,
        )

    def column_arrived(source, k):
        return pltpu.make_async_remote_copy(
            src_ref=slots_ref.at[source, k, :, front],
            dst_ref=stage.at[source, k],
            send_sem=stage_send.at[source, k],
            recv_sem=stage_recv.at[source, k],
            device_id=(r, source),
            device_id_type=MESH,
        )

    def row_copy(held, source, k):
        target = source * ratio + k
        return pltpu.make_async_remote_copy(
            src_ref=held.at[source, k, :, front],
            dst_ref=picked.at[r],
            send_sem=send_sem.at[target],
            recv_sem=recv_sem.at[r],
            device_id=(target, c),
            device_id_type=MESH,
        )

    def row_local(held, source, k):
        return pltpu.make_async_copy(
            held.at[source, k, :, front], picked.at[r], recv_sem.at[r]
        )

    def row_arrived(source):
        return pltpu.make_async_remote_copy(
            src_ref=picked.at[source],
            dst_ref=picked.at[source],
            send_sem=send_sem.at[source],
            recv_sem=recv_sem.at[source],
            device_id=(source, c),
            device_id_type=MESH,
        )

    for offset in (*range(2, col_count), 1):
        for k in range(ratio):
            column_copy(near(offset), k).start()
    for offset in range(col_count):
        source = near(offset)
        held = stage if offset else slots_ref
        for k in range(ratio):
            if offset:
                column_arrived(source, k).wait_recv()

            @pl.when(source * ratio + k == r)
            def _():
                row_local(held, source, k).start()

            @pl.when(source * ratio + k != r)
            def _():
                row_copy(held, source, k).start()

    def part_copy(peer):
        return pltpu.make_async_remote_copy(
            src_ref=inner.at[pl.ds(pl.multiple_of(peer * slice_rows, slice_rows), slice_rows), :],
            dst_ref=part.at[r],
            send_sem=part_send.at[peer],
            recv_sem=part_recv.at[r],
            device_id=(peer, c),
            device_id_type=MESH,
        )

    def part_arrived(peer):
        return pltpu.make_async_remote_copy(
            src_ref=inner.at[pl.ds(0, slice_rows), :],
            dst_ref=part.at[peer],
            send_sem=part_send.at[peer],
            recv_sem=part_recv.at[peer],
            device_id=(peer, c),
            device_id_type=MESH,
        )

    def total_copy(peer):
        return pltpu.make_async_remote_copy(
            src_ref=reduced,
            dst_ref=total.at[r],
            send_sem=total_send.at[peer],
            recv_sem=total_recv.at[r],
            device_id=(peer, c),
            device_id_type=MESH,
        )

    def total_arrived(peer):
        return pltpu.make_async_remote_copy(
            src_ref=reduced,
            dst_ref=total.at[peer],
            send_sem=total_send.at[peer],
            recv_sem=total_recv.at[peer],
            device_id=(peer, c),
            device_id_type=MESH,
        )

    def peers(action):
        for peer in range(row_count):
            @pl.when(peer != r)
            def _():
                action(peer)

    step = 256 if cells % 256 == 0 else BLK
    half = row_count // 2
    group_rows = half * slice_rows
    inner[...] = jnp.zeros_like(inner)

    for turn in range(2):
        first = lax.rem(r // half + turn, 2) * half
        for at in range(half):
            @pl.when(first + at != r)
            def _():
                row_arrived(first + at).wait_recv()

            @pl.when(first + at == r)
            def _():
                for offset in range(col_count):
                    source = near(offset)
                    for k in range(ratio):
                        @pl.when(source * ratio + k == r)
                        def _():
                            row_local(stage if offset else slots_ref, source, k).wait()

        group = pl.ds(pl.multiple_of(first * slice_rows, group_rows), group_rows)

        @pl.loop(0, cells // step)
        def _(i):
            at = pl.ds(pl.multiple_of(i * step, step), step)
            block = picked[pl.ds(first, half), :, at].reshape(group_rows, step)
            inner[group, :] += jnp.dot(
                block, own_ref[at, :], precision=lax.Precision.HIGHEST, preferred_element_type=jnp.float32
            )

        for at in range(half):
            @pl.when(first + at != r)
            def _():
                part_copy(first + at).start()

    peers(lambda peer: part_arrived(peer).wait_recv())
    mine = inner[pl.ds(pl.multiple_of(r * slice_rows, slice_rows), slice_rows), :]
    for peer in range(row_count):
        @pl.when(peer == r)
        def _():
            part[peer] = mine
    value = part[0]
    for peer in range(1, row_count):
        value = value + part[peer]
    reduced[...] = value
    peers(lambda peer: total_copy(peer).start())

    @pl.loop(0, row_count)
    def _(source):
        picked_ref[source] = picked[source]

    peers(lambda peer: total_arrived(peer).wait_recv())
    for peer in range(row_count):
        @pl.when(peer == r)
        def _():
            total[peer] = reduced[...]
    base = jnp.where(owner_ref[c] >= 0, base_ref[...], jnp.zeros_like(base_ref))
    diag_ref[...] = base - total[...].reshape(diag_ref.shape)

    for offset in range(col_count):
        source = near(offset)
        held = stage if offset else slots_ref
        if offset:
            for k in range(ratio):
                column_copy(source, k).wait_send()
        for k in range(ratio):
            @pl.when(source * ratio + k != r)
            def _():
                row_copy(held, source, k).wait_send()
    peers(lambda peer: part_copy(peer).wait_send())
    peers(lambda peer: total_copy(peer).wait_send())


def finish(owner, slots, own, base, row_count, most, collective):
    col_count, ratio, slice_rows, _ = slots.shape
    width = own.shape[1]
    cells = most * BLK
    vmem = pl.BlockSpec(memory_space=pltpu.VMEM)
    dma = pltpu.SemaphoreType.DMA
    return pl.pallas_call(
        functools.partial(finish_kernel, row_count, col_count),
        out_shape=(
            jax.ShapeDtypeStruct((row_count, slice_rows, cells), jnp.float32),
            jax.ShapeDtypeStruct((width, width), jnp.float32),
        ),
        in_specs=[pl.BlockSpec(memory_space=pltpu.SMEM)] + [vmem] * 3,
        out_specs=(vmem, vmem),
        scratch_shapes=[
            pltpu.VMEM((col_count, ratio, slice_rows, cells), jnp.float32),
            pltpu.VMEM((row_count, slice_rows, cells), jnp.float32),
            pltpu.VMEM((width, width), jnp.float32),
            pltpu.VMEM((row_count, slice_rows, width), jnp.float32),
            pltpu.VMEM((slice_rows, width), jnp.float32),
            pltpu.VMEM((row_count, slice_rows, width), jnp.float32),
            dma((col_count, row_count // col_count)),
            dma((col_count, row_count // col_count)),
            dma((row_count,)),
            dma((row_count,)),
            dma((row_count,)),
            dma((row_count,)),
            dma((row_count,)),
            dma((row_count,)),
        ],
        compiler_params=pltpu.CompilerParams(collective_id=collective, has_side_effects=True),
    )(owner, slots, own, base)


def per_device(anc_inverse, l_store, diag_inv, block_lists, block_counts, sibling_columns):
    siblings = block_lists.shape[0]
    row_count, col_count = lax.axis_size("row"), lax.axis_size("col")
    r, c = lax.axis_index("row"), lax.axis_index("col")
    row_blocks, col_blocks = anc_inverse.shape[0] // BLK, anc_inverse.shape[1] // BLK
    pairs = col_count // 2
    mate = [(k, k + 1 - 2 * (k % 2)) for k in range(col_count)]
    panel = l_store[0]
    near = [panel, lax.ppermute(panel, "col", mate)]
    moved = [
        lax.ppermute(panel, "col", [(k, (k + 2 * step) % col_count) for k in range(col_count)])
        for step in range(1, pairs)
    ]

    table = listed_table(block_lists, block_counts, row_blocks * row_count)
    row_listed = lax.dynamic_slice_in_dim(table, r * row_blocks, row_blocks, axis=1)
    col_listed = lax.dynamic_slice_in_dim(table, c * col_blocks, col_blocks, axis=1)
    row_ints = row_listed.astype(jnp.int32)
    counts = jnp.sum(row_ints, axis=1)
    place = jnp.cumsum(row_ints, axis=1) - 1
    ids = jnp.arange(row_blocks, dtype=jnp.int32)
    entry = jnp.arange(-(-row_blocks // GROUP) * GROUP, dtype=jnp.int32)
    hits = row_listed[:, :, None] & (place[:, :, None] == entry[None, None, :])
    rows = jnp.sum(jnp.where(hits, ids[None, :, None], 0), axis=1).astype(jnp.int32)

    flat = col_listed.reshape(-1)
    slot = jnp.where(flat, jnp.cumsum(flat.astype(jnp.int32)) - 1, -1).astype(jnp.int32)
    per_column = jnp.sum(table.reshape(siblings, col_count, col_blocks).astype(jnp.int32), axis=(0, 2))
    needed = jnp.max(per_column)
    slots_all = -(-siblings * col_blocks // 40) * 40
    grain = slots_all // 40
    caps = [grain * n for n in (19, 20, 21, 22, 23, 25, 28, 32, 40)]
    level = jnp.sum((needed > jnp.array(caps[:-1], jnp.int32)).astype(jnp.int32))

    match = sibling_columns[:, None] == jnp.arange(col_count, dtype=jnp.int32)[None, :]
    owner = jnp.max(
        jnp.where(match, jnp.arange(siblings, dtype=jnp.int32)[:, None], -1), axis=0
    ).astype(jnp.int32)
    slot_rows = slot.reshape(siblings, col_blocks)

    def tables(columns):
        owned = (sibling_columns[None, :] == jnp.stack(columns)[:, None]).astype(jnp.int32)
        return (
            jnp.sum(owned[:, :, None] * (slot_rows + 1)[None], axis=1) - 1,
            jnp.sum(owned[:, :, None] * rows[None], axis=1),
            jnp.sum(owned * counts[None, :], axis=1),
        )

    mate_of = c + 1 - 2 * (c % 2)
    near_columns = [c, mate_of]
    far_columns = []
    for step in range(1, pairs):
        far_columns += [lax.rem(c - 2 * step + col_count, col_count), lax.rem(mate_of - 2 * step + col_count, col_count)]
    near_tables = tables(near_columns)
    near_tables, own_packed = lax.optimization_barrier((near_tables, packed(near_tables[1][0], panel)))
    partial_value, high, low = product(*near_tables, anc_inverse, near, slots_all)
    if moved:
        moved, partial_value = lax.optimization_barrier((moved, partial_value))
        far = [panel for one in moved for panel in (one, lax.ppermute(one, "col", mate))]
        partial_value = product(*tables(far_columns), anc_inverse, far, slots_all, (partial_value, high, low))

    def branch(place, cap):
        def run(value):
            compact = reduce_rows(value, row_count, cap // grain, grain * BLK, place + 1)
            return expand(slot, owner, compact, siblings, col_blocks, row_count // col_count)
        return run

    upper, slots = lax.switch(level, [branch(place, cap) for place, cap in enumerate(caps)], partial_value)

    own_place = jnp.sum(
        jnp.where(sibling_columns == c, 1, 0)[:, None] * jnp.where(row_listed, place + 1, 0), axis=0
    ) - 1
    most = jnp.max(jnp.sum(table.reshape(siblings, row_count, row_blocks).astype(jnp.int32), axis=2))
    sizes = sorted({-(-row_blocks * n // 20) for n in (16, 18, 20)})
    depth_level = jnp.sum((most > jnp.array(sizes[:-1], jnp.int32)).astype(jnp.int32))

    def end(number, size):
        def run(value, own, base):
            picked, diag = finish(owner, value, own, base, row_count, size, len(caps) + 1 + number)
            return unpacked(own_place, picked, own.shape[0]), diag
        return run

    lower, diag = lax.switch(
        depth_level, [end(number, size) for number, size in enumerate(sizes)], slots, own_packed, diag_inv[0]
    )
    return upper, lower[None], diag[None]


def solution(mesh):
    return jax.shard_map(
        per_device,
        mesh=mesh,
        in_specs=(P("row", "col"), P("col", "row", None), P("col", None, None), P(), P(), P()),
        out_specs=(P(None, "row", "col"), P("col", "row", None), P("col", None, None)),
        check_vma=False,
    )
```
